32 devices in a mesh: seq: 4 (over z), exp: 2 (over x), tp: 4 (over y, core).
Axes of the slice: x: 2, y: 2, z: 4, core: 2. Of those that a mesh axis runs over, the one named last changes fastest.
Arguments:
- query_heads: bfloat16 [1024, 32, 128], P(('seq', 'exp'), 'tp'), may hold values from -10 to 10
- key_heads: bfloat16 [1024, 8, 128], P(('seq', 'exp'), 'tp'), may hold values from -10 to 10
- value_head_rows: bfloat16 [1024, 8, 128], P(('seq', 'exp'), 'tp'), may hold values from -6 to 6
- state_input: bfloat16 [1024, 4096], P(('seq', 'exp'), 'tp'), may hold values from -6 to 6
- state_gate: bfloat16 [1024, 4096], P(('seq', 'exp'), 'tp'), may hold values from -6 to 6
- state_inflow: bfloat16 [1024, 8, 128], P(('seq', 'exp'), 'tp'), may hold values from -6 to 6
- state_readout: bfloat16 [1024, 8, 128], P(('seq', 'exp'), 'tp'), may hold values from -6 to 6
- step_size: float32 [1024, 64], P(('seq', 'exp'), 'tp'), may hold values from 0.01 to 0.1
- log_decay: float32 [1024, 64], P(('seq', 'exp'), 'tp'), may hold values from -1 to 0
- skip_scale: float32 [64], P('tp'), may hold values from 0.5 to 2
- state_gain: float32 [4096], P('tp'), may hold values from 0.25 to 1.75
- hidden_in: bfloat16 [1024, 2048], P(('seq', 'exp')), may hold values from -400 to 400
- mlp_gain: float32 [2048], replicated, may hold values from 0.25 to 1.75
- router_weight: bfloat16 [2048, 8], replicated, may hold values from -0.125 to 0.125
- expert_ids: int32 [1024, 2], P(('seq', 'exp')), may hold values from 0 to 7, as said below
- slot_index: int32 [1024, 2], P(('seq', 'exp')), may hold values from -1 to 39, as said below
- gate_up: bfloat16 [8, 7168, 2, 2048], P('exp', ('seq', 'tp')), may hold values from -0.125 to 0.125
- down_proj: bfloat16 [8, 7168, 2048], P('exp', ('seq', 'tp')), may hold values from -0.0625 to 0.0625
Outputs:
- window_out: bfloat16 [1024, 32, 128], P(('seq', 'exp'), 'tp')
- state_out: bfloat16 [1024, 4096], P(('seq', 'exp'), 'tp')
- routed_out: bfloat16 [1024, 2048], P(('seq', 'exp'), 'tp')
The draws below stay inside these ranges and needn't reach their ends.
Inputs may be any that keep to these rules, and one draw needn't show every extreme that they name: `expert_ids`: the 2 ids of a row differ. slot_index[t, k] is the place of the choice expert_ids[t, k] in that expert's buffer of 40 places for the 128 rows of the device block that holds row t (rows b * 128 to b * 128 + 127); the live places of one expert within one block are distinct; -1 marks a dropped choice.
All inputs are finite; a program needn't handle non-finite values.
Results may differ from the reference program's by a relative error of at most 0.02.
Values may be sent and summed in bfloat16 or wider, within the bound.
No kernel may reach another device: no remote copies, remote signals or barrier semaphores. Data moves between devices by JAX's collectives and lax.ppermute only.
A program may use at most 192 MiB of HBM per device.

```python
import math
import jax
import jax.numpy as jnp
import numpy as np
from jax import lax

D = 2048
FF = 7168
EXPERTS = 8
TOP = 2
QUERY_HEAD_COUNT = 32
KEY_VALUE_HEADS = 8
HEAD_SIZE = 128
WINDOW = 4096
STATE_HEAD_COUNT = 64
HP = 64
NS = 128
NG = 8
STRETCH = 128
TOK = 128
PROMPT_TOKENS = 1024
CAP = 40


def attention_law(key):
    folded = jax.random.fold_in(key, 101)
    random_subkeys = jax.random.split(folded, 2)
    query_rows = jnp.clip(jax.random.normal(random_subkeys[0], (PROMPT_TOKENS, QUERY_HEAD_COUNT, HEAD_SIZE), jnp.float32), -4.0, 4.0)
    key_row_list = jnp.clip(jax.random.normal(random_subkeys[1], (PROMPT_TOKENS, KEY_VALUE_HEADS, HEAD_SIZE), jnp.float32), -4.0, 4.0)
    return (query_rows, key_row_list)


def draw_query_heads(key, part):
    return attention_law(key)[0].astype(jnp.bfloat16)


def draw_key_heads(key, part):
    return attention_law(key)[1].astype(jnp.bfloat16)


def draw_log_decay(key, part):
    folded = jax.random.fold_in(key, 202)
    random_subkeys = jax.random.split(folded, 7)
    slow_share = 0.5
    gradual_heads = jax.random.uniform(random_subkeys[0], (STATE_HEAD_COUNT,)) < slow_share
    fast_rate = jnp.exp(jax.random.uniform(random_subkeys[1], (STATE_HEAD_COUNT,), minval=math.log(1.0 / 50.0), maxval=math.log(1.0 / 30.0)))
    slow_rate = 0.5 / PROMPT_TOKENS * jnp.exp(jax.random.uniform(random_subkeys[2], (STATE_HEAD_COUNT,), minval=math.log(0.7), maxval=math.log(1.4)))
    head_rate = jnp.where(gradual_heads, slow_rate, fast_rate)
    block_factor = jnp.exp(jax.random.uniform(random_subkeys[3], (PROMPT_TOKENS // TOK, STATE_HEAD_COUNT), minval=math.log(0.6), maxval=math.log(1.5)))
    position_factor = jnp.exp(jax.random.uniform(random_subkeys[4], (PROMPT_TOKENS, STATE_HEAD_COUNT), minval=math.log(0.6), maxval=math.log(1.4)))
    decay_rates = head_rate[None, :] * jnp.repeat(block_factor, TOK, axis=0) * position_factor
    span_rows = jax.random.randint(random_subkeys[5], (3,), 0, PROMPT_TOKENS)
    span_depth = jax.random.uniform(random_subkeys[6], (3, STATE_HEAD_COUNT), minval=0.22, maxval=0.45)
    decay_rates = decay_rates.at[span_rows].add(jnp.where(gradual_heads[None, :], span_depth, 0.0))
    return -decay_rates


def draw_hidden_in(key, part):
    folded = jax.random.fold_in(key, 303)
    random_subkeys = jax.random.split(folded, 3)
    row_scale = jnp.exp(jax.random.uniform(random_subkeys[0], (PROMPT_TOKENS, 1), minval=0.0, maxval=math.log(10.0)))
    column_scale = jnp.exp(jax.random.uniform(random_subkeys[1], (1, D), minval=0.0, maxval=math.log(10.0)))
    values = jnp.clip(jax.random.normal(random_subkeys[2], (PROMPT_TOKENS, D), jnp.float32), -4.0, 4.0)
    return (values * row_scale * column_scale).astype(jnp.bfloat16)


def route_law(key):
    folded = jax.random.fold_in(key, 404)
    random_subkeys = jax.random.split(folded, 5)
    blocks = PROMPT_TOKENS // TOK
    weight_table = np.array([max(1, 4 * EXPERTS // (counter + 1) ** 2) for counter in range(EXPERTS)], np.int32)
    bounds = np.cumsum(weight_table)
    expert_order = jax.random.permutation(random_subkeys[0], EXPERTS)
    ticket = jax.random.randint(random_subkeys[1], (PROMPT_TOKENS,), 0, int(bounds[-1]))
    ranked = jnp.sum(ticket[:, None] >= jnp.asarray(bounds, jnp.int32)[None, :], axis=1)
    block_keys = jax.random.split(random_subkeys[2], blocks)
    forced = jax.vmap(lambda sub: jax.random.permutation(sub, TOK))(block_keys).reshape(PROMPT_TOKENS) < CAP
    ranked = jnp.where(forced, 0, ranked)
    first_pick = expert_order[ranked]
    offset = jax.random.randint(random_subkeys[3], (PROMPT_TOKENS,), 1, EXPERTS)
    second = (first_pick + offset) % EXPERTS
    chosen = jnp.stack([first_pick, second], axis=1).astype(jnp.int32)
    order_keys = jax.random.split(random_subkeys[4], blocks)
    priority = jax.vmap(lambda sub: jax.random.permutation(sub, TOK * TOP))(order_keys)
    flat_ids = chosen.reshape(blocks, TOK * TOP)
    matching = flat_ids[:, :, None] == flat_ids[:, None, :]
    earlier = priority[:, None, :] < priority[:, :, None]
    places = jnp.sum(matching & earlier, axis=-1)
    slot_values = jnp.where(places < CAP, places, -1).reshape(PROMPT_TOKENS, TOP)
    return (chosen, slot_values.astype(jnp.int32))


def draw_expert_ids(key, part):
    return route_law(key)[0]


def draw_slot_index(key, part):
    return route_law(key)[1]


def levels(key, dims, shards, smallest, top_value):
    level, own = 1.0, jax.random.fold_in(key, 6)
    for axis_at, parts in shards:
        draws = jnp.exp(jax.random.uniform(jax.random.fold_in(own, axis_at), (parts,), jnp.float32, smallest / len(shards), top_value / len(shards)))
        level = level * jnp.repeat(draws, dims[axis_at] // parts).reshape([-1 if axis == axis_at else 1 for axis in range(len(dims))])
    return level


def gaussian(own_key, extent, width, most, cuts=(), held_as=jnp.bfloat16):
    gain = levels(own_key, extent, cuts, -0.22, 0.18) if cuts else 1.0
    entries = jax.random.normal(own_key, extent, jnp.float32) * width * gain
    return jnp.minimum(jnp.maximum(entries, -most), most).astype(held_as)


def setup_inputs(seed: int = 0) -> dict:
    keys = jax.random.split(jax.random.key(seed), 19)
    query_heads = draw_query_heads(jax.random.fold_in(keys[18], 71), 0)
    key_heads = draw_key_heads(jax.random.fold_in(keys[18], 71), 0)
    value_head_rows = gaussian(keys[2], (PROMPT_TOKENS, KEY_VALUE_HEADS, HEAD_SIZE), 1.0, 6.0, ((0, 8), (1, 4)))
    state_input = gaussian(keys[3], (PROMPT_TOKENS, STATE_HEAD_COUNT * HP), 1.0, 6.0, ((0, 8), (1, 4)))
    state_gate = gaussian(keys[4], (PROMPT_TOKENS, STATE_HEAD_COUNT * HP), 1.0, 6.0, ((0, 8), (1, 4)))
    state_inflow = gaussian(keys[5], (PROMPT_TOKENS, NG, NS), 1.0, 6.0, ((0, 8), (1, 4)))
    state_readout = gaussian(keys[6], (PROMPT_TOKENS, NG, NS), 1.0, 6.0, ((0, 8), (1, 4)))
    step_size = jnp.clip(jnp.exp(math.log(0.1) - 2.3025851 * jax.random.uniform(keys[7], (PROMPT_TOKENS, STATE_HEAD_COUNT), jnp.float32) ** levels(keys[7], (PROMPT_TOKENS, STATE_HEAD_COUNT), ((0, 8), (1, 4)), -0.2, 0.2)), 0.01, 0.1)
    log_decay = draw_log_decay(jax.random.fold_in(keys[18], 71), 0)
    skip_scale = jnp.clip(jnp.exp(math.log(2.0) - 1.3862944 * jax.random.uniform(keys[9], (STATE_HEAD_COUNT,), jnp.float32) ** levels(keys[9], (STATE_HEAD_COUNT,), ((0, 4),), -0.2, 0.2)), 0.5, 2.0)
    state_gain = jnp.clip(1.0 + 0.15 * jax.random.normal(keys[10], (STATE_HEAD_COUNT * HP,), jnp.float32), 0.25, 1.75)
    hidden_in = draw_hidden_in(jax.random.fold_in(keys[18], 71), 0)
    mlp_gain = jnp.clip(1.0 + 0.15 * jax.random.normal(keys[12], (D,), jnp.float32), 0.25, 1.75)
    router_weight = gaussian(keys[13], (D, EXPERTS), D ** -0.5, 0.125)
    expert_ids = draw_expert_ids(jax.random.fold_in(keys[18], 71), 0)
    slot_index = draw_slot_index(jax.random.fold_in(keys[18], 71), 0)
    gate_up = gaussian(keys[16], (EXPERTS, FF, 2, D), D ** -0.5, 0.125, ((0, 2), (1, 16)))
    down_proj = gaussian(keys[17], (EXPERTS, FF, D), FF ** -0.5, 0.0625, ((0, 2), (1, 16)))
    return dict(query_heads=query_heads, key_heads=key_heads, value_head_rows=value_head_rows, state_input=state_input, state_gate=state_gate, state_inflow=state_inflow, state_readout=state_readout, step_size=step_size, log_decay=log_decay, skip_scale=skip_scale, state_gain=state_gain, hidden_in=hidden_in, mlp_gain=mlp_gain, router_weight=router_weight, expert_ids=expert_ids, slot_index=slot_index, gate_up=gate_up, down_proj=down_proj)


EPSILON = 1e-05

def window_attention(query_heads, key_heads, value_head_rows):
    group_width = QUERY_HEAD_COUNT // KEY_VALUE_HEADS
    query_tile_block = min(PROMPT_TOKENS, 256)
    key_span = WINDOW + query_tile_block
    score_scale = 1.0 / math.sqrt(HEAD_SIZE)
    padded_keys = jnp.pad(key_heads, ((WINDOW, 0), (0, 0), (0, 0)))
    padded_values = jnp.pad(value_head_rows, ((WINDOW, 0), (0, 0), (0, 0)))

    def one_block(counter):
        first_row = counter * query_tile_block
        query_rows = lax.dynamic_slice_in_dim(query_heads, first_row, query_tile_block, 0).astype(jnp.float32)
        query_rows = query_rows.reshape(query_tile_block, KEY_VALUE_HEADS, group_width, HEAD_SIZE)
        key_row_list = lax.dynamic_slice_in_dim(padded_keys, first_row, key_span, 0).astype(jnp.float32)
        value_rows = lax.dynamic_slice_in_dim(padded_values, first_row, key_span, 0).astype(jnp.float32)
        scores = jnp.einsum('qkgd,jkd->kgqj', query_rows, key_row_list, precision=lax.Precision.HIGHEST) * score_scale
        query_pos = first_row + jnp.arange(query_tile_block, dtype=jnp.int32)
        key_pos = first_row - WINDOW + jnp.arange(key_span, dtype=jnp.int32)
        visible = (key_pos[None, :] <= query_pos[:, None]) & (key_pos[None, :] > query_pos[:, None] - WINDOW) & (key_pos[None, :] >= 0)
        scores = jnp.where(visible, scores, -jnp.inf)
        top_score = lax.optimization_barrier(jnp.max(scores, axis=-1, keepdims=True))
        weights = jnp.exp(scores - top_score)
        totals = lax.optimization_barrier(jnp.sum(weights, axis=-1))
        rounded = lax.optimization_barrier(weights.astype(jnp.bfloat16)).astype(jnp.float32)
        outputs = jnp.einsum('kgqj,jkd->qkgd', rounded, value_rows, precision=lax.Precision.HIGHEST)
        outputs = outputs / jnp.transpose(totals, (2, 0, 1))[..., None]
        return outputs.reshape(query_tile_block, QUERY_HEAD_COUNT, HEAD_SIZE).astype(jnp.bfloat16)
    outputs = lax.map(one_block, jnp.arange(PROMPT_TOKENS // query_tile_block, dtype=jnp.int32))
    return outputs.reshape(PROMPT_TOKENS, QUERY_HEAD_COUNT, HEAD_SIZE)

def state_space(state_input, state_gate, state_inflow, state_readout, step_size, log_decay, skip_scale, state_gain):
    stretch_count = PROMPT_TOKENS // STRETCH
    per_group = STATE_HEAD_COUNT // NG
    inputs = state_input.reshape(stretch_count, STRETCH, NG, per_group, HP)
    inflow = state_inflow.reshape(stretch_count, STRETCH, NG, NS)
    readout = state_readout.reshape(stretch_count, STRETCH, NG, NS)
    step_rows = step_size.reshape(stretch_count, STRETCH, NG, per_group)
    decay_rows = log_decay.reshape(stretch_count, STRETCH, NG, per_group)
    causal = (jnp.arange(STRETCH)[:, None] >= jnp.arange(STRETCH)[None, :])[:, :, None, None]

    def advance(carried, packed):
        stretch_in, stretch_inflow, stretch_readout, stretch_steps, stretch_decay = packed
        cumulative = jnp.cumsum(stretch_decay, axis=0)
        read_write = jnp.einsum('ign,jgn->ijg', stretch_readout.astype(jnp.float32), stretch_inflow.astype(jnp.float32), precision=lax.Precision.HIGHEST)
        decay_gap = cumulative[:, None] - cumulative[None, :]
        decay_mat = jnp.where(causal, jnp.exp(jnp.where(causal, decay_gap, 0.0)), 0.0)
        mixing = decay_mat * read_write[..., None] * stretch_steps[None]
        mixing = lax.optimization_barrier(mixing.astype(jnp.bfloat16)).astype(jnp.float32)
        inputs_wide = stretch_in.astype(jnp.float32)
        intra = jnp.einsum('ijgk,jgkp->igkp', mixing, inputs_wide, precision=lax.Precision.HIGHEST)
        stretch_total = cumulative[-1]
        weight_in = jnp.exp(stretch_total[None] - cumulative) * stretch_steps
        weighted = weight_in[..., None] * stretch_inflow.astype(jnp.float32)[:, :, None, :]
        weighted = lax.optimization_barrier(weighted.astype(jnp.bfloat16)).astype(jnp.float32)
        stretch_state = jnp.einsum('jgkn,jgkp->gknp', weighted, inputs_wide, precision=lax.Precision.HIGHEST)
        inter = jnp.exp(cumulative)[..., None] * jnp.einsum('ign,gknp->igkp', stretch_readout.astype(jnp.float32), carried, precision=lax.Precision.HIGHEST)
        carried = jnp.exp(stretch_total)[..., None, None] * carried + stretch_state
        return (carried, intra + inter)
    initial = jnp.zeros((NG, per_group, NS, HP), jnp.float32)
    _, mixed = lax.scan(advance, initial, (inputs, inflow, readout, step_rows, decay_rows))
    skip_rows = skip_scale.reshape(NG, per_group)
    output = mixed + skip_rows[:, :, None] * inputs.astype(jnp.float32)
    gate_rows = state_gate.reshape(stretch_count, STRETCH, NG, per_group, HP).astype(jnp.float32)
    gated = output * jax.nn.silu(gate_rows)
    mean_square = lax.optimization_barrier(jnp.mean(gated * gated, axis=(3, 4), keepdims=True))
    normed = gated * lax.rsqrt(mean_square + EPSILON)
    return (normed.reshape(PROMPT_TOKENS, STATE_HEAD_COUNT * HP) * state_gain).astype(jnp.bfloat16)

def routed_mlp(hidden_in, mlp_gain, router_weight, expert_ids, slot_index, gate_up, down_proj):
    hidden = hidden_in.astype(jnp.float32)
    mean_square = lax.optimization_barrier(jnp.mean(hidden * hidden, axis=-1, keepdims=True))
    normed = (hidden * lax.rsqrt(mean_square + EPSILON) * mlp_gain).astype(jnp.bfloat16)
    logits = jnp.dot(normed, router_weight, preferred_element_type=jnp.float32)
    gate_values = jax.nn.sigmoid(logits)
    chosen = jnp.take_along_axis(gate_values, expert_ids, axis=1)
    mixing = chosen / lax.optimization_barrier(jnp.sum(chosen, axis=1, keepdims=True))
    block_count = PROMPT_TOKENS // TOK
    row_block = jnp.arange(PROMPT_TOKENS, dtype=jnp.int32) // TOK
    is_live = slot_index >= 0
    places = EXPERTS * block_count * CAP
    target = jnp.where(is_live, (expert_ids * block_count + row_block[:, None]) * CAP + slot_index, places)
    buffer = jnp.zeros((places + 1, D), jnp.bfloat16)
    buffer = buffer.at[target.reshape(-1)].set(jnp.repeat(normed, TOP, axis=0))
    expert_inputs = buffer[:-1].reshape(EXPERTS, block_count * CAP, D)

    def one_expert(packed):
        expert_rows, expert_gate_up, expert_down = packed
        rows_wide = expert_rows.astype(jnp.float32)
        gate_part = jnp.dot(rows_wide, expert_gate_up[:, 0, :].astype(jnp.float32).T, precision=lax.Precision.HIGHEST)
        up_part = jnp.dot(rows_wide, expert_gate_up[:, 1, :].astype(jnp.float32).T, precision=lax.Precision.HIGHEST)
        hidden_units = lax.optimization_barrier((jax.nn.silu(gate_part) * up_part).astype(jnp.bfloat16)).astype(jnp.float32)
        return jnp.dot(hidden_units, expert_down.astype(jnp.float32), precision=lax.Precision.HIGHEST)
    outputs = lax.map(one_expert, (expert_inputs, gate_up, down_proj))
    flat_rows = outputs.reshape(places, D)
    picked = flat_rows[jnp.where(is_live, target, 0)]
    weights = jnp.where(is_live, mixing, 0.0)
    return lax.optimization_barrier(jnp.sum(weights[..., None] * picked, axis=1)).astype(jnp.bfloat16)

def reference(query_heads, key_heads, value_head_rows, state_input, state_gate, state_inflow, state_readout, step_size, log_decay, skip_scale, state_gain, hidden_in, mlp_gain, router_weight, expert_ids, slot_index, gate_up, down_proj):
    window_out = window_attention(query_heads, key_heads, value_head_rows)
    state_out = state_space(state_input, state_gate, state_inflow, state_readout, step_size, log_decay, skip_scale, state_gain)
    routed_out = routed_mlp(hidden_in, mlp_gain, router_weight, expert_ids, slot_index, gate_up, down_proj)
    return (window_out, state_out, routed_out)
```

```python
import functools
import math

import jax
import jax.numpy as jnp
from jax import lax
from jax.experimental import pallas as pl
from jax.experimental.pallas import tpu as pltpu
from jax.sharding import PartitionSpec as P

EXPERTS = 8
WINDOW = 4096
HP = 64
NS = 128
STRETCH = 128
CAP = 40
EPSILON = 1e-05
F32 = jnp.float32
BF16 = jnp.bfloat16


def bits_of(count):
    assert count & (count - 1) == 0
    return [1 << b for b in reversed(range(count.bit_length() - 1))]


def swap(block, axis, bit):
    return lax.ppermute(block, axis, [(i, i ^ bit) for i in range(lax.axis_size(axis))])


def spread(block, stages):
    for axis, bit in stages:
        block = jnp.stack([block, swap(block, axis, bit)])
    return block


def stages_of(axis, bits):
    return [(axis, bit) for bit in bits]


def offsets_of(bits):
    offsets = [0]
    for bit in bits:
        offsets = offsets + [o ^ bit for o in offsets]
    return offsets


def attention_kernel(place_ref, query_ref, kv_ref, out_ref, top_ref, sum_ref, acc_ref):
    step = pl.program_id(0)
    steps = pl.num_programs(0)
    rows, width = query_ref.shape
    keys = kv_ref.shape[0]
    shared = kv_ref.shape[1] // (2 * 128)
    group = width // 128 // shared
    mine = place_ref[0]
    other = place_ref[1 + step]

    @pl.when(step == 0)
    def _():
        top_ref[...] = jnp.full_like(top_ref, -jnp.inf)
        sum_ref[...] = jnp.zeros_like(sum_ref)
        acc_ref[...] = jnp.zeros_like(acc_ref)

    gap = (mine - other) * rows

    @pl.when((gap >= 0) & (gap - (keys - 1) < WINDOW))
    def _():
        scale = 1.0 / math.sqrt(128)
        for k in range(shared):
            key = kv_ref[:, k * 128 : (k + 1) * 128]
            value = kv_ref[:, (shared + k) * 128 : (shared + k + 1) * 128]
            query = jnp.concatenate(
                [query_ref[:, (k * group + g) * 128 : (k * group + g + 1) * 128] for g in range(group)],
                axis=0,
            )
            score = (
                lax.dot_general(query, key, (((1,), (1,)), ((), ())), preferred_element_type=F32)
                * scale
            )
            row = lax.rem(lax.broadcasted_iota(jnp.int32, score.shape, 0), rows)
            column = lax.broadcasted_iota(jnp.int32, score.shape, 1)
            behind = gap + row - column
            score = jnp.where((behind >= 0) & (behind < WINDOW), score, -jnp.inf)
            old = top_ref[k]
            new = jnp.maximum(old, jnp.max(score, axis=1, keepdims=True))
            safe = jnp.where(new == -jnp.inf, 0.0, new)
            weight = jnp.exp(score - safe[:, :1])
            shrink = jnp.exp(old - safe)
            top_ref[k] = new
            sum_ref[k] = sum_ref[k] * shrink + jnp.sum(weight, axis=1, keepdims=True)
            acc_ref[k] = acc_ref[k] * shrink[:, :1] + jnp.dot(
                weight.astype(BF16), value, preferred_element_type=F32
            )

    @pl.when(step == steps - 1)
    def _():
        for k in range(shared):
            done = acc_ref[k] / sum_ref[k][:, :1]
            for g in range(group):
                h = k * group + g
                out_ref[:, h * 128 : (h + 1) * 128] = done[g * rows : (g + 1) * rows].astype(BF16)


def attention(query, kv_all, place):
    rows, width = query.shape
    blocks, keys, kv_width = kv_all.shape
    shared = kv_width // 256
    tall = width // 128 // shared * rows
    return pl.pallas_call(
        attention_kernel,
        out_shape=jax.ShapeDtypeStruct((rows, width), BF16),
        grid_spec=pltpu.PrefetchScalarGridSpec(
            num_scalar_prefetch=1,
            grid=(blocks,),
            in_specs=[
                pl.BlockSpec((rows, width), lambda j, place: (0, 0)),
                pl.BlockSpec((None, keys, kv_width), lambda j, place: (j, 0, 0)),
            ],
            out_specs=pl.BlockSpec((rows, width), lambda j, place: (0, 0)),
            scratch_shapes=[
                pltpu.VMEM((shared, tall, 128), F32),
                pltpu.VMEM((shared, tall, 128), F32),
                pltpu.VMEM((shared, tall, 128), F32),
            ],
        ),
        name="attention",
    )(place, query, kv_all)


def expert_kernel(
    offsets,
    where_ref,
    info_ref,
    left_ref,
    right_ref,
    gate_up_ref,
    down_ref,
    keep0_ref,
    keep1_ref,
    send0_ref,
    send1_ref,
    rows_ref,
    hot_ref,
    weight_ref,
):
    expert = pl.program_id(1)
    experts = pl.num_programs(1)
    me = where_ref[0]
    first = where_ref[1]
    far, gx, nz, tokens, half = keep0_ref.shape
    parts = 2 * far
    local = rows_ref.shape[1]
    pairs = rows_ref.shape[0]

    def column(part, h):
        return pl.multiple_of((me ^ offsets[part]) * (2 * half) + h * half, 128)

    def pair_at(p):
        return (2 * p) // nz, (2 * p) % nz

    @pl.when(expert == 0)
    def _():
        for p in range(pairs):
            mx, mz = pair_at(p)
            info = jnp.concatenate([info_ref[mx, mz], info_ref[mx, mz + 1]], axis=1)
            info_id = info[0:2].astype(jnp.int32)
            info_slot = info[2:4].astype(jnp.int32)
            block = lax.broadcasted_iota(jnp.int32, (1, 2 * tokens), 1) // tokens
            row = lax.broadcasted_iota(jnp.int32, (2 * CAP, 2 * tokens), 0)
            for e in range(local):
                match = []
                for k in range(2):
                    live = (info_slot[k : k + 1] >= 0) & (info_id[k : k + 1] == first + e)
                    code = jnp.where(live, block * CAP + info_slot[k : k + 1], -1)
                    match.append(row == code)
                hot_ref[p, e] = (match[0] | match[1]).astype(F32).astype(BF16)
                share = jnp.where(match[0], info[4:5], 0.0) + jnp.where(match[1], info[5:6], 0.0)
                weight_ref[p, e] = jnp.broadcast_to(
                    jnp.sum(share, axis=1, keepdims=True), (2 * CAP, 128)
                )
            hot = hot_ref[p].reshape(local * 2 * CAP, 2 * tokens)
            for part in range(parts):
                core, high = part // far, part % far
                for h in range(2):
                    if h == 0:
                        piece = left_ref[core, high, mx, mz : mz + 2]
                    else:
                        piece = right_ref[core, mx, high, mz : mz + 2]
                    piece = piece.reshape(2 * tokens, half)
                    picked = jnp.dot(hot, piece, preferred_element_type=F32).astype(BF16)
                    rows_ref[p, :, :, pl.ds(column(part, h), half)] = picked.reshape(
                        local, 2 * CAP, half
                    )

    rows = rows_ref[:, expert].reshape(pairs * 2 * CAP, rows_ref.shape[3])
    nt = (((1,), (1,)), ((), ()))
    gate = lax.dot_general(rows, gate_up_ref[0], nt, preferred_element_type=F32)
    up = lax.dot_general(rows, gate_up_ref[1], nt, preferred_element_type=F32)
    hidden = (gate / (1.0 + jnp.exp(-gate)) * up).astype(BF16)
    value = jnp.dot(hidden, down_ref[...], preferred_element_type=F32)
    for p in range(pairs):
        scaled = value[p * 2 * CAP : (p + 1) * 2 * CAP] * weight_ref[p, expert][:, :1]
        rows_ref[p, expert] = scaled.astype(BF16)

    @pl.when(expert == experts - 1)
    def _():
        for p in range(pairs):
            mx, mz = pair_at(p)
            hot = hot_ref[p].reshape(local * 2 * CAP, 2 * tokens)
            for part in range(parts):
                core, high = part // far, part % far
                for h in range(2):
                    value = rows_ref[p, :, :, pl.ds(column(part, h), half)]
                    value = value.reshape(local * 2 * CAP, half)
                    total = lax.dot_general(
                        hot, value, (((0,), (0,)), ((), ())), preferred_element_type=F32
                    )
                    total = total.astype(BF16).reshape(2, tokens, half)
                    if h == 0:
                        target = send0_ref if core else keep0_ref
                        target[high, mx, mz : mz + 2] = total
                    else:
                        target = send1_ref if core else keep1_ref
                        target[mx, high, mz : mz + 2] = total


def experts_apply(offsets, where, info, left, right, gate_up, down):
    nx, nz = info.shape[:2]
    _, far, _, _, tokens, half = left.shape
    local, _, units, width = gate_up.shape
    gx = max(1, 8 // nz)
    pairs = gx * nz // 2
    once = pl.Buffered(1)
    shape0 = jax.ShapeDtypeStruct((far, nx, nz, tokens, half), BF16)
    shape1 = jax.ShapeDtypeStruct((nx, far, nz, tokens, half), BF16)
    spec0 = pl.BlockSpec((far, gx, nz, tokens, half), lambda g, e, w: (0, g, 0, 0, 0))
    spec1 = pl.BlockSpec((gx, far, nz, tokens, half), lambda g, e, w: (g, 0, 0, 0, 0))
    return pl.pallas_call(
        functools.partial(expert_kernel, offsets),
        out_shape=[shape0, shape1, shape0, shape1],
        grid_spec=pltpu.PrefetchScalarGridSpec(
            num_scalar_prefetch=1,
            grid=(nx // gx, local),
            in_specs=[
                pl.BlockSpec((gx, nz, 8, 128), lambda g, e, w: (g, 0, 0, 0)),
                pl.BlockSpec(
                    (2, far, gx, nz, tokens, half),
                    lambda g, e, w: (0, 0, g, 0, 0, 0),
                    pipeline_mode=once,
                ),
                pl.BlockSpec(
                    (2, gx, far, nz, tokens, half),
                    lambda g, e, w: (0, g, 0, 0, 0, 0),
                    pipeline_mode=once,
                ),
                pl.BlockSpec((None, 2, units, width), lambda g, e, w: (e, 0, 0, 0)),
                pl.BlockSpec((None, units, width), lambda g, e, w: (e, 0, 0)),
            ],
            out_specs=[spec0, spec1, spec0, spec1],
            scratch_shapes=[
                pltpu.VMEM((pairs, local, 2 * CAP, width), BF16),
                pltpu.VMEM((pairs, local, 2 * CAP, 2 * tokens), BF16),
                pltpu.VMEM((pairs, local, 2 * CAP, 128), F32),
            ],
        ),
        compiler_params=pltpu.CompilerParams(vmem_limit_bytes=60 * 1024 * 1024),
        name="experts",
    )(where, info, left, right, gate_up, down)


def state_local(state_input, state_inflow, state_readout, step_size, log_decay):
    rows = state_input.shape[0]
    heads = step_size.shape[1]
    groups = state_inflow.shape[1]
    per_group = heads // groups
    inputs = state_input.reshape(rows, groups, per_group, HP)
    step_rows = step_size.reshape(rows, groups, per_group)
    cumulative = jnp.cumsum(log_decay.reshape(rows, groups, per_group), axis=0)
    read_write = jnp.einsum(
        "ign,jgn->ijg", state_readout, state_inflow, preferred_element_type=F32
    )
    causal = (jnp.arange(rows)[:, None] >= jnp.arange(rows)[None, :])[:, :, None, None]
    gap = cumulative[:, None] - cumulative[None]
    decay = jnp.where(causal, jnp.exp(jnp.where(causal, gap, 0.0)), 0.0)
    mixing = (decay * read_write[..., None] * step_rows[None]).astype(BF16)
    intra = jnp.einsum("ijgk,jgkp->igkp", mixing, inputs, preferred_element_type=F32)
    total = cumulative[-1]
    weight = jnp.exp(total[None] - cumulative) * step_rows
    weighted = (weight[..., None] * state_inflow[:, :, None, :]).astype(BF16)
    state = jnp.einsum("jgkn,jgkp->gknp", weighted, inputs, preferred_element_type=F32)
    return cumulative, intra, total, state


def state_entering(state, totals):
    nx = lax.axis_size("exp")
    nz = lax.axis_size("seq")
    place = lax.axis_index("seq") * nx + lax.axis_index("exp")
    count = nx * nz
    offsets = jnp.arange(count, dtype=jnp.int32)
    entering = jnp.zeros_like(state)
    span = 1
    while span < count:
        axis, bit = ("exp", span) if span < nx else ("seq", span // nx)
        if span * 2 < count:
            pairs = [(i, i ^ bit) for i in range(lax.axis_size(axis))]
        else:
            pairs = [(i, i ^ bit) for i in range(lax.axis_size(axis)) if not i & bit]
        other = lax.ppermute(state.astype(BF16), axis, pairs).astype(F32)
        upper = (place & span) != 0
        near = totals[:span]
        before = ((place ^ offsets[:span]) < place)[:, None, None]
        lead = jnp.exp(jnp.sum(jnp.where(before, near, 0.0), axis=0))
        entering = jnp.where(upper, lead[..., None, None] * other + entering, entering)
        own = jnp.exp(jnp.sum(near, axis=0))[..., None, None]
        theirs = jnp.exp(jnp.sum(totals[span : 2 * span], axis=0))[..., None, None]
        state = jnp.where(upper, own * other + state, theirs * state + other)
        span *= 2
    return entering


def state_finish(
    cumulative, intra, entering, state_input, state_gate, state_readout, skip_scale, state_gain
):
    rows, channels = state_input.shape
    groups = state_readout.shape[1]
    per_group = cumulative.shape[2]
    inter = jnp.exp(cumulative)[..., None] * jnp.einsum(
        "ign,gknp->igkp", state_readout.astype(F32), entering, precision=lax.Precision.HIGHEST
    )
    inputs = state_input.reshape(rows, groups, per_group, HP).astype(F32)
    output = intra + inter + skip_scale.reshape(groups, per_group)[:, :, None] * inputs
    gate_rows = state_gate.reshape(rows, groups, per_group, HP).astype(F32)
    gated = output * jax.nn.silu(gate_rows)
    mean_square = jnp.mean(gated * gated, axis=(2, 3), keepdims=True)
    normed = gated * lax.rsqrt(mean_square + EPSILON)
    return (normed.reshape(rows, channels) * state_gain).astype(BF16)


def local(
    query_heads,
    key_heads,
    value_head_rows,
    state_input,
    state_gate,
    state_inflow,
    state_readout,
    step_size,
    log_decay,
    skip_scale,
    state_gain,
    hidden_in,
    mlp_gain,
    router_weight,
    expert_ids,
    slot_index,
    gate_up,
    down_proj,
):
    nz, nx, nt = lax.axis_size("seq"), lax.axis_size("exp"), lax.axis_size("tp")
    z, x, t = lax.axis_index("seq"), lax.axis_index("exp"), lax.axis_index("tp")
    rows, width = hidden_in.shape
    chunk = width // nt
    half = chunk // 2
    tp_bits = bits_of(nt)
    seq_stages = stages_of("seq", bits_of(nz))
    exp_stages = stages_of("exp", bits_of(nx))
    far_stages, core_stages = stages_of("tp", tp_bits[:-1]), stages_of("tp", tp_bits[-1:])

    hidden = hidden_in.astype(F32)
    mean_square = jnp.mean(hidden * hidden, axis=-1, keepdims=True)
    normed = (hidden * lax.rsqrt(mean_square + EPSILON) * mlp_gain).astype(BF16)
    own = lax.dynamic_slice_in_dim(normed, t * chunk, chunk, 1)

    logits = jnp.dot(normed, router_weight, preferred_element_type=F32)
    gate_values = jax.nn.sigmoid(logits)
    one_hot = expert_ids[..., None] == jnp.arange(EXPERTS, dtype=jnp.int32)
    chosen = jnp.sum(jnp.where(one_hot, gate_values[:, None, :], 0.0), axis=-1)
    mixing = chosen / jnp.sum(chosen, axis=1, keepdims=True)

    cumulative, intra, total, state = state_local(
        state_input, state_inflow, state_readout, step_size, log_decay
    )
    heads = step_size.shape[1]
    decay_row = jnp.pad(total.reshape(1, heads), ((0, 1), (0, rows - heads)))
    info = jnp.concatenate(
        [expert_ids.T.astype(F32), slot_index.T.astype(F32), mixing.T, decay_row], axis=0
    )

    piece = spread(own, seq_stages)
    info_all = spread(info, seq_stages + exp_stages)
    left = spread(piece[..., :half], exp_stages + far_stages + core_stages)
    right = spread(piece[..., half:], far_stages + exp_stages + core_stages)
    left = left.reshape(2, nt // 2, nx, nz, rows, half)
    right = right.reshape(2, nx, nt // 2, nz, rows, half)
    info_all = info_all.reshape(nx, nz, 8, rows)

    where = jnp.stack([t, x * gate_up.shape[0]]).astype(jnp.int32)
    keep0, keep1, send0, send1 = experts_apply(
        offsets_of(tp_bits), where, info_all, left, right, jnp.swapaxes(gate_up, 1, 2), down_proj
    )

    flat = lambda a: a.reshape(rows, a.shape[1] * a.shape[2])
    kv = jnp.concatenate([flat(key_heads), flat(value_head_rows)], axis=1)
    kv_all = spread(kv, seq_stages + exp_stages).reshape(nx * nz, rows, kv.shape[1])
    off_x, off_z = offsets_of(bits_of(nx)), offsets_of(bits_of(nz))
    offset_x = jnp.array(off_x, jnp.int32)[:, None]
    offset_z = jnp.array(off_z, jnp.int32)[None, :]
    places = ((z ^ offset_z) * nx + (x ^ offset_x)).reshape(-1)
    place = jnp.concatenate([(z * nx + x)[None], places]).astype(jnp.int32)
    window_out = attention(flat(query_heads), kv_all, place).reshape(query_heads.shape)

    groups = state_inflow.shape[1]
    totals = jnp.stack(
        [info_all[off_x.index(i), off_z.index(k), 6, :heads] for k in range(nz) for i in range(nx)]
    ).reshape(nz * nx, groups, heads // groups)
    entering = state_entering(state, totals)
    state_out = state_finish(
        cumulative, intra, entering, state_input, state_gate, state_readout, skip_scale, state_gain
    )

    def settle(kept, stages):
        for axis, bit in stages:
            count = kept.shape[0] // 2
            kept = kept[:count] + swap(kept[count:].astype(BF16), axis, bit).astype(F32)
        return kept

    def join(kept, sent):
        kept = kept.astype(F32) + swap(sent, *core_stages[0]).astype(F32)
        return kept.reshape(-1, rows, half)

    kept0 = settle(join(keep0, send0), far_stages[::-1] + exp_stages[::-1])
    kept1 = settle(join(keep1, send1), exp_stages[::-1] + far_stages[::-1])
    kept = settle(jnp.concatenate([kept0, kept1], axis=-1), seq_stages[::-1])
    routed_out = kept.reshape(rows, chunk).astype(BF16)
    return window_out, state_out, routed_out


def solution(mesh):
    block = ("seq", "exp")
    return jax.shard_map(
        local,
        mesh=mesh,
        in_specs=(
            P(block, "tp", None),
            P(block, "tp", None),
            P(block, "tp", None),
            P(block, "tp"),
            P(block, "tp"),
            P(block, "tp", None),
            P(block, "tp", None),
            P(block, "tp"),
            P(block, "tp"),
            P("tp"),
            P("tp"),
            P(block, None),
            P(),
            P(),
            P(block, None),
            P(block, None),
            P("exp", ("seq", "tp"), None, None),
            P("exp", ("seq", "tp"), None),
        ),
        out_specs=(P(block, "tp", None), P(block, "tp"), P(block, "tp")),
        check_vma=False,
    )
```

```python
import functools
import math

import jax
import jax.numpy as jnp
from jax import lax
from jax.experimental import pallas as pl
from jax.experimental.pallas import tpu as pltpu
from jax.sharding import PartitionSpec as P

SEQ, EXP, TP = "seq", "exp", "tp"
WINDOW = 4096
HP = 64
NS = 128
STRETCH = 128
CAP = 40
EPSILON = 1e-05
F32 = jnp.float32
BF16 = jnp.bfloat16


def bits_of(count):
    assert count & (count - 1) == 0
    return [1 << b for b in reversed(range(count.bit_length() - 1))]


def swap(block, axis, bit):
    return lax.ppermute(block, axis, [(i, i ^ bit) for i in range(lax.axis_size(axis))])


def spread(block, stages):
    for axis, bit in stages:
        block = jnp.stack([block, swap(block, axis, bit)])
    return block


def stages_of(axis, bits):
    return [(axis, bit) for bit in bits]


def offsets_of(bits):
    offsets = [0]
    for bit in bits:
        offsets = offsets + [o ^ bit for o in offsets]
    return offsets


def staged_call(body, scalars, near, arrays, out_shape, scratch=(), vmem=20):
    count, outs = len(arrays), len(out_shape)

    def kernel(*refs):
        inside = list(refs)
        first, inside = inside[: len(scalars) + len(near)], inside[len(scalars) + len(near) :]
        sources, inside = inside[:count], inside[count:]
        results, inside = inside[:outs], inside[outs:]
        targets, inside = inside[:count], inside[count:]
        sem, extra = inside[0], inside[1:]
        copies = [
            pltpu.make_async_copy(source, target, sem.at[i])
            for i, (source, target) in enumerate(zip(sources, targets))
        ]
        for copy in copies:
            copy.start()
        for copy in copies:
            copy.wait()
        body(*first, *targets, *results, *extra)

    smem = pl.BlockSpec(memory_space=pltpu.SMEM)
    local = pl.BlockSpec(memory_space=pltpu.VMEM)
    return pl.pallas_call(
        kernel,
        out_shape=out_shape,
        in_specs=[smem] * len(scalars)
        + [local] * len(near)
        + [pl.BlockSpec(memory_space=pltpu.HBM)] * count,
        out_specs=[local] * outs,
        scratch_shapes=[pltpu.VMEM(a.shape, a.dtype) for a in arrays]
        + [pltpu.SemaphoreType.DMA((count,))]
        + list(scratch),
        compiler_params=pltpu.CompilerParams(vmem_limit_bytes=vmem * 1024 * 1024),
    )(*scalars, *near, *[pltpu.with_memory_space_constraint(a, pltpu.HBM) for a in arrays])


def attention_kernel(offsets, where_ref, query_ref, *refs):
    kv_refs, (out_ref, score_ref, top_ref, sum_ref, acc_ref) = refs[:-5], refs[-5:]
    total, size = query_ref.shape
    shared = 2
    wide = kv_refs[0].shape[1] // 2
    keys = wide // shared
    heads = total // keys
    mine = where_ref[2]
    scale = 1.0 / math.sqrt(size)
    row = lax.broadcasted_iota(jnp.int32, (total, keys), 0)
    column = lax.broadcasted_iota(jnp.int32, (total, keys), 1)
    lower = lax.rem(row, heads) < heads // shared
    behind = row // heads - column
    source = lax.broadcasted_iota(jnp.int32, (wide, wide), 0)
    target = lax.broadcasted_iota(jnp.int32, (wide, wide), 1)
    apart = target == lax.rem(source, keys) * shared + source // keys
    apart = apart.astype(F32).astype(BF16)
    part = lambda rows: jnp.dot(apart, rows, preferred_element_type=F32).astype(BF16)
    blocks = [(kv_ref, b) for kv_ref in kv_refs for b in range(kv_ref.shape[0])]
    gaps = [(mine - (mine ^ offset)) * keys for offset in offsets]
    seen = [(gap >= 0) & (gap - (keys - 1) < WINDOW) for gap in gaps]
    top_ref[...] = jnp.full_like(top_ref, -jnp.inf)
    sum_ref[...] = jnp.zeros_like(sum_ref)
    acc_ref[...] = jnp.zeros_like(acc_ref)

    def scores(at):
        kv_ref, b = blocks[at]
        score = lax.dot_general(
            query_ref[...],
            part(kv_ref[b, :wide]),
            (((1,), (1,)), ((), ())),
            preferred_element_type=F32,
        )
        return jnp.where(lower, score[:, :keys], score[:, keys:]) * scale

    for at, gap in enumerate(gaps):
        inside = (gap >= keys - 1) & (gap + keys - 1 < WINDOW)

        @pl.when(inside)
        def _(at=at):
            score = scores(at)
            score_ref[at] = score
            top_ref[...] = jnp.maximum(top_ref[...], score)

        @pl.when(seen[at] & jnp.logical_not(inside))
        def _(at=at, gap=gap):
            distance = behind + gap
            score = jnp.where((distance >= 0) & (distance < WINDOW), scores(at), -jnp.inf)
            score_ref[at] = score
            top_ref[...] = jnp.maximum(top_ref[...], score)

    top = jnp.max(top_ref[...], axis=1, keepdims=True)
    top_ref[...] = jnp.broadcast_to(top, (total, keys))

    for at, (kv_ref, b) in enumerate(blocks):

        @pl.when(seen[at])
        def _(at=at, kv_ref=kv_ref, b=b):
            weight = jnp.exp(score_ref[at] - top_ref[...])
            sum_ref[...] += weight
            weight = jnp.concatenate(
                [jnp.where(lower, weight, 0.0), jnp.where(lower, 0.0, weight)], axis=1
            )
            acc_ref[...] += jnp.dot(
                weight.astype(BF16), part(kv_ref[b, wide:]), preferred_element_type=F32
            )

    out_ref[...] = (acc_ref[...] / jnp.sum(sum_ref[...], axis=1, keepdims=True)).astype(BF16)


def attention(query, kv_parts, offsets, where):
    rows, heads, size = query.shape
    assert kv_parts[0].shape[1] == 4 * rows and size == rows
    total = rows * heads
    vmem = pl.BlockSpec(memory_space=pltpu.VMEM)
    out = pl.pallas_call(
        functools.partial(attention_kernel, offsets),
        out_shape=jax.ShapeDtypeStruct((total, size), BF16),
        in_specs=[pl.BlockSpec(memory_space=pltpu.SMEM), vmem] + [vmem] * len(kv_parts),
        out_specs=vmem,
        scratch_shapes=[pltpu.VMEM((len(offsets), total, rows), F32)]
        + [pltpu.VMEM((total, rows), F32)] * 2
        + [pltpu.VMEM((total, size), F32)],
        compiler_params=pltpu.CompilerParams(
            vmem_limit_bytes=(len(offsets) + 40) * total * rows * 4
        ),
        name="attention",
    )(where, query.reshape(total, size), *kv_parts)
    return out.reshape(rows, heads, size)


def norm_kernel(
    where_ref, hidden_ref, gain_ref, router_ref, id_ref, slot_ref, log_ref, own_ref, normed_ref
):
    rows, _ = hidden_ref.shape
    chunk = own_ref.shape[1]
    hidden = hidden_ref[...].astype(F32)
    mean_square = jnp.mean(hidden * hidden, axis=1, keepdims=True)
    normed = (hidden * lax.rsqrt(mean_square + EPSILON) * gain_ref[...]).astype(BF16)
    normed_ref[...] = normed
    start = pl.multiple_of(where_ref[0] * chunk, 128)
    own_ref[0:rows, :] = normed_ref[:, pl.ds(start, chunk)]
    logits = lax.dot_general(
        router_ref[...], normed, (((1,), (1,)), ((), ())), preferred_element_type=F32
    )
    gates = 1.0 / (1.0 + jnp.exp(-logits))
    expert = lax.broadcasted_iota(jnp.int32, gates.shape, 0)
    chosen = [
        jnp.sum(jnp.where(id_ref[k : k + 1] == expert, gates, 0.0), axis=0, keepdims=True)
        for k in range(2)
    ]
    both = chosen[0] + chosen[1]
    decay = jnp.sum(log_ref[...], axis=1, keepdims=True)
    head = lax.broadcasted_iota(jnp.int32, log_ref.shape, 0)
    lane = lax.broadcasted_iota(jnp.int32, log_ref.shape, 1)
    decay = jnp.sum(jnp.where(head == lane, decay, 0.0), axis=0, keepdims=True)
    info = jnp.concatenate(
        [
            id_ref[...].astype(F32),
            slot_ref[...].astype(F32),
            chosen[0] / both,
            chosen[1] / both,
            decay,
            jnp.zeros_like(decay),
        ],
        axis=0,
    )
    parts = []
    for _ in range(3):
        part = info.astype(BF16).astype(F32)
        parts.append(part)
        info = info - part
    tail = jnp.concatenate(
        [
            jnp.concatenate([parts[0], parts[1]], axis=1),
            jnp.concatenate([parts[2], jnp.zeros_like(info)], axis=1),
        ],
        axis=0,
    )
    tail = jnp.concatenate([tail, jnp.zeros((16, chunk - 256), F32)], axis=1)
    own_ref[rows:, :] = tail.astype(BF16)


def info_of(block):
    block = block.astype(F32)
    return block[0:8, 0:128] + block[0:8, 128:256] + block[8:16, 0:128]


def norm_share(where, chunk, hidden, gain, router, ids, slots, log_decay):
    rows, width = hidden.shape
    assert rows == 128 and chunk >= 512
    return staged_call(
        norm_kernel,
        (where,),
        (),
        (hidden, gain, router, ids, slots, log_decay),
        [jax.ShapeDtypeStruct((rows + 16, chunk), BF16)],
        [pltpu.VMEM((rows, width), BF16)],
    )[0]


def expert_kernel(
    offsets,
    where_ref,
    info_ref,
    left_ref,
    right_ref,
    gate_up_ref,
    down_ref,
    keep0_ref,
    keep1_ref,
    send0_ref,
    send1_ref,
    rows_ref,
    hot_ref,
    weight_ref,
):
    expert = pl.program_id(1)
    experts = pl.num_programs(1)
    me = where_ref[0]
    first = where_ref[1]
    far, _, nz, tokens, half = keep0_ref.shape
    parts = 2 * far
    local = rows_ref.shape[1]
    pairs = rows_ref.shape[0]

    def column(part, h):
        return pl.multiple_of((me ^ offsets[part]) * (2 * half) + h * half, 128)

    def pair_at(p):
        return (2 * p) // nz, (2 * p) % nz

    @pl.when(expert == 0)
    def _():
        for p in range(pairs):
            mx, mz = pair_at(p)
            info = jnp.concatenate([info_of(info_ref[mx, mz]), info_of(info_ref[mx, mz + 1])], axis=1)
            info_id = info[0:2].astype(jnp.int32)
            info_slot = info[2:4].astype(jnp.int32)
            block = lax.broadcasted_iota(jnp.int32, (1, 2 * tokens), 1) // tokens
            row = lax.broadcasted_iota(jnp.int32, (2 * CAP, 2 * tokens), 0)
            for e in range(local):
                match = []
                for k in range(2):
                    live = (info_slot[k : k + 1] >= 0) & (info_id[k : k + 1] == first + e)
                    code = jnp.where(live, block * CAP + info_slot[k : k + 1], -1)
                    match.append(row == code)
                hot_ref[p, e] = (match[0] | match[1]).astype(F32).astype(BF16)
                share = jnp.where(match[0], info[4:5], 0.0) + jnp.where(match[1], info[5:6], 0.0)
                weight_ref[p, e] = jnp.broadcast_to(
                    jnp.sum(share, axis=1, keepdims=True), (2 * CAP, 128)
                )
            hot = hot_ref[p].reshape(local * 2 * CAP, 2 * tokens)
            for part in range(parts):
                core, high = part // far, part % far
                for h in range(2):
                    if h == 0:
                        piece = left_ref[core, high, mx, mz : mz + 2]
                    else:
                        piece = right_ref[core, mx, high, mz : mz + 2]
                    piece = piece.reshape(2 * tokens, half)
                    picked = jnp.dot(hot, piece, preferred_element_type=F32).astype(BF16)
                    rows_ref[p, :, :, pl.ds(column(part, h), half)] = picked.reshape(
                        local, 2 * CAP, half
                    )

    rows = rows_ref[:, expert].reshape(pairs * 2 * CAP, rows_ref.shape[3])
    nt = (((1,), (1,)), ((), ()))
    gate = lax.dot_general(rows, gate_up_ref[0], nt, preferred_element_type=F32)
    up = lax.dot_general(rows, gate_up_ref[1], nt, preferred_element_type=F32)
    hidden = (gate / (1.0 + jnp.exp(-gate)) * up).astype(BF16)
    value = jnp.dot(hidden, down_ref[...], preferred_element_type=F32)
    for p in range(pairs):
        scaled = value[p * 2 * CAP : (p + 1) * 2 * CAP] * weight_ref[p, expert][:, :1]
        rows_ref[p, expert] = scaled.astype(BF16)

    @pl.when(expert == experts - 1)
    def _():
        for p in range(pairs):
            mx, mz = pair_at(p)
            hot = hot_ref[p].reshape(local * 2 * CAP, 2 * tokens)
            for part in range(parts):
                core, high = part // far, part % far
                for h in range(2):
                    value = rows_ref[p, :, :, pl.ds(column(part, h), half)]
                    value = value.reshape(local * 2 * CAP, half)
                    total = lax.dot_general(
                        hot, value, (((0,), (0,)), ((), ())), preferred_element_type=F32
                    )
                    total = total.astype(BF16).reshape(2, tokens, half)
                    if h == 0:
                        target = send0_ref if core else keep0_ref
                        target[high, mx, mz : mz + 2] = total
                    else:
                        target = send1_ref if core else keep1_ref
                        target[mx, high, mz : mz + 2] = total


def experts_apply(offsets, where, info, left, right, gate_up, down):
    nx, nz = info.shape[:2]
    _, far, _, _, tokens, half = left.shape
    local, _, units, width = gate_up.shape
    gx = max(1, 8 // nz)
    pairs = gx * nz // 2
    once = pl.Buffered(1)
    shape0 = jax.ShapeDtypeStruct((far, nx, nz, tokens, half), BF16)
    shape1 = jax.ShapeDtypeStruct((nx, far, nz, tokens, half), BF16)
    spec0 = pl.BlockSpec((far, gx, nz, tokens, half), lambda g, e, w: (0, g, 0, 0, 0))
    spec1 = pl.BlockSpec((gx, far, nz, tokens, half), lambda g, e, w: (g, 0, 0, 0, 0))
    return pl.pallas_call(
        functools.partial(expert_kernel, offsets),
        out_shape=[shape0, shape1, shape0, shape1],
        grid_spec=pltpu.PrefetchScalarGridSpec(
            num_scalar_prefetch=1,
            grid=(nx // gx, local),
            in_specs=[
                pl.BlockSpec((gx, nz, 16, 256), lambda g, e, w: (g, 0, 0, 0)),
                pl.BlockSpec(
                    (2, far, gx, nz, tokens, half),
                    lambda g, e, w: (0, 0, g, 0, 0, 0),
                    pipeline_mode=once,
                ),
                pl.BlockSpec(
                    (2, gx, far, nz, tokens, half),
                    lambda g, e, w: (0, g, 0, 0, 0, 0),
                    pipeline_mode=once,
                ),
                pl.BlockSpec((None, 2, units, width), lambda g, e, w: (e, 0, 0, 0)),
                pl.BlockSpec((None, units, width), lambda g, e, w: (e, 0, 0)),
            ],
            out_specs=[spec0, spec1, spec0, spec1],
            scratch_shapes=[
                pltpu.VMEM((pairs, local, 2 * CAP, width), BF16),
                pltpu.VMEM((pairs, local, 2 * CAP, 2 * tokens), BF16),
                pltpu.VMEM((pairs, local, 2 * CAP, 128), F32),
            ],
        ),
        compiler_params=pltpu.CompilerParams(vmem_limit_bytes=60 * 1024 * 1024),
        name="experts",
    )(where, info, left, right, gate_up, down)


def matches(info_ref, blocks, first, local):
    info = jnp.concatenate([info_of(info_ref[b]) for b in blocks], axis=1)
    tokens = info_ref.shape[2] // 2
    ids, slots = info[0:2].astype(jnp.int32), info[2:4].astype(jnp.int32)
    block = lax.broadcasted_iota(jnp.int32, (1, 2 * tokens), 1) // tokens
    row = lax.broadcasted_iota(jnp.int32, (2 * CAP, 2 * tokens), 0)
    for e in range(local):
        found = []
        for k in range(2):
            live = (slots[k : k + 1] >= 0) & (ids[k : k + 1] == first + e)
            found.append(row == jnp.where(live, block * CAP + slots[k : k + 1], -1))
        share = jnp.where(found[0], info[4:5], 0.0) + jnp.where(found[1], info[5:6], 0.0)
        yield (found[0] | found[1]).astype(F32).astype(BF16), jnp.sum(share, axis=1, keepdims=True)


def column_of(me, offset, h, half):
    return pl.multiple_of((me ^ offset) * (2 * half) + h * half, 128)


def combine(me, offsets, hot, value_of, keep_ref, send_ref, xo):
    tokens, half = keep_ref.shape[-2:]
    for core in range(2):
        for yi in range(2):
            for h in range(2):
                value = value_of(column_of(me, offsets[core][yi], h, half), half)
                total = lax.dot_general(
                    hot, value, (((0,), (0,)), ((), ())), preferred_element_type=F32
                )
                target = send_ref if core else keep_ref
                place = (h, yi, xo) if h == 0 else (h, xo, yi)
                target[place] = total.astype(BF16).reshape(2, tokens, half)


def paired(both):
    count, width = both.shape
    lane = lax.broadcasted_iota(jnp.int32, (count, 128), 1)
    low = lane < 64
    even = jnp.where(low, 2 * lane, 2 * lane - 128)
    take = lambda a, i: jnp.take_along_axis(a, i, axis=1, mode="promise_in_bounds")
    hidden = []
    for c in range(0, width, 256):
        one = both[:, c : c + 128]
        two = both[:, c + 128 : c + 256] if c + 128 < width else one
        gate = jnp.where(low, take(one, even), take(two, even))
        up = jnp.where(low, take(one, even + 1), take(two, even + 1))
        unit = (gate / (1.0 + jnp.exp(-gate)) * up).astype(BF16)
        hidden.append(unit[:, : (width - c) // 2] if width - c < 256 else unit)
    return jnp.concatenate(hidden, axis=1)


def gather_kernel(offsets, *refs):
    where_ref, gate_up_ref, down_ref = refs[:3]
    pieces = refs[3:19]
    results = refs[19:23]
    all_ref, rows_ref, hot_ref, weight_ref, wide_ref, tall_ref, info_ref = refs[23:30]
    piece_sem, wide_sem, tall_sem, info_sem = refs[30:]
    me, first = where_ref[0], where_ref[1]
    pairs, local, places, width = rows_ref.shape
    tokens, half = all_ref.shape[2], pieces[0].shape[-1]
    units = down_ref.shape[1]
    count = pairs * places

    def fetch(e, slot):
        return (
            pltpu.make_async_copy(gate_up_ref.at[e], wide_ref.at[slot], wide_sem.at[slot]),
            pltpu.make_async_copy(down_ref.at[e], tall_ref.at[slot], tall_sem.at[slot]),
        )

    copies = []
    for p in range(pairs):
        g, xo = p // 2, p % 2
        for core in range(2):
            for yi in range(2):
                for h in range(2):
                    if h == 0:
                        source = pieces[8 * g + 2 * core + yi].at[xo, :, 0:tokens]
                    else:
                        source = pieces[8 * g + 4 + 2 * core + xo].at[yi]
                    column = column_of(me, offsets[core][yi], h, half)
                    copies.append(
                        pltpu.make_async_copy(
                            source,
                            all_ref.at[p, :, :, pl.ds(column, half)],
                            piece_sem.at[len(copies)],
                        )
                    )
    notes = [
        pltpu.make_async_copy(
            pieces[b // 4 * 8].at[b // 2 % 2, b % 2, tokens : tokens + 16],
            info_ref.at[b],
            info_sem.at[b],
        )
        for b in range(2 * pairs)
    ]
    for copy in notes + copies:
        copy.start()
    for slot in range(2):
        if slot < local:
            for copy in fetch(slot, slot):
                copy.start()
    for copy in notes:
        copy.wait()
    for p in range(pairs):
        for e, (hot, weight) in enumerate(matches(info_ref, (2 * p, 2 * p + 1), first, local)):
            hot_ref[p, e] = hot
            weight_ref[p, e] = jnp.broadcast_to(weight, (places, 128))
    for p in range(pairs):
        for copy in copies[8 * p : 8 * p + 8]:
            copy.wait()
        hot = hot_ref[p].reshape(local * places, 2 * tokens)
        picked = jnp.dot(
            hot, all_ref[p].reshape(2 * tokens, width), preferred_element_type=F32
        ).astype(BF16)
        rows_ref[p] = picked.reshape(local, places, width)

    def one_expert(e, _):
        slot = lax.rem(e, 2)
        for copy in fetch(e, slot):
            copy.wait()
        rows = rows_ref[:, e].reshape(count, width)
        wide = wide_ref[slot].reshape(2 * units, width)
        both = lax.dot_general(
            rows, wide, (((1,), (1,)), ((), ())), preferred_element_type=F32
        )
        value = jnp.dot(paired(both), tall_ref[slot], preferred_element_type=F32)
        for p in range(pairs):
            scaled = value[p * places : (p + 1) * places] * weight_ref[p, e][:, :1]
            rows_ref[p, e] = scaled.astype(BF16)

        @pl.when(e + 2 < local)
        def _():
            for copy in fetch(e + 2, slot):
                copy.start()

        return 0

    lax.fori_loop(0, local, one_expert, 0)
    for p in range(pairs):
        combine(
            me,
            offsets,
            hot_ref[p].reshape(local * places, 2 * tokens),
            lambda column, half: rows_ref[p, :, :, pl.ds(column, half)].reshape(
                local * places, half
            ),
            *results[p // 2 * 2 : p // 2 * 2 + 2],
            p % 2,
        )


def experts_gather(offsets, where, pieces, gate_up, down):
    half = pieces[0].shape[-1]
    tokens = pieces[4].shape[-2]
    local, units, _, width = gate_up.shape
    pairs, places = 4, 2 * CAP
    result = jax.ShapeDtypeStruct((2, 2, 2, 2, tokens, half), BF16)
    smem = pl.BlockSpec(memory_space=pltpu.SMEM)
    vmem = pl.BlockSpec(memory_space=pltpu.VMEM)
    hbm = pl.BlockSpec(memory_space=pl.ANY)
    return pl.pallas_call(
        functools.partial(gather_kernel, offsets),
        out_shape=[result] * 4,
        in_specs=[smem, hbm, hbm] + [hbm] * len(pieces),
        out_specs=[vmem] * 4,
        scratch_shapes=[
            pltpu.VMEM((pairs, 2, tokens, width), BF16),
            pltpu.VMEM((pairs, local, places, width), BF16),
            pltpu.VMEM((pairs, local, places, 2 * tokens), BF16),
            pltpu.VMEM((pairs, local, places, 128), F32),
            pltpu.VMEM((2, units, 2, width), BF16),
            pltpu.VMEM((2, units, width), BF16),
            pltpu.VMEM((2 * pairs, 16, 2 * 128), BF16),
            pltpu.SemaphoreType.DMA((8 * pairs,)),
            pltpu.SemaphoreType.DMA((2,)),
            pltpu.SemaphoreType.DMA((2,)),
            pltpu.SemaphoreType.DMA((2 * pairs,)),
        ],
        compiler_params=pltpu.CompilerParams(vmem_limit_bytes=44 * 1024 * 1024),
        name="experts",
    )(where, gate_up, down, *pieces)


def group_bits():
    far, near = bits_of(lax.axis_size(SEQ))
    (side,) = bits_of(lax.axis_size(EXP))
    high, core = bits_of(lax.axis_size(TP))
    return far, near, side, high, core


def spread_near(block):
    _, _, side, high, core = group_bits()
    half = block.shape[-1] // 2
    left, right = block[..., :half], block[..., :-16, half:]
    left = jnp.stack([left, swap(left, EXP, side)])
    right = jnp.stack([right, swap(right, TP, high)])
    left2 = swap(left, TP, high)
    right2 = swap(right, EXP, side)
    first = [swap(left, TP, core), swap(right, TP, core)]
    second = [swap(left2, TP, core), swap(right2, TP, core)]
    return [left, left2, first[0], second[0], right, right2, first[1], second[1]]


def fold(kept, sent, axis, bit):
    return kept + swap(sent.astype(BF16), axis, bit).astype(F32)


HIGHEST = lax.Precision.HIGHEST


def running_sum(log_ref, rows, columns):
    i = lax.broadcasted_iota(jnp.int32, (rows, rows), 0)
    j = lax.broadcasted_iota(jnp.int32, (rows, rows), 1)
    decay = log_ref[...]
    if columns:
        ones = (j <= i).astype(F32)
        return lax.dot_general(
            ones, decay, (((1,), (1,)), ((), ())), precision=HIGHEST, preferred_element_type=F32
        )
    ones = (i <= j).astype(F32)
    return jnp.dot(decay, ones, precision=HIGHEST, preferred_element_type=F32)


def group_rows(ref, g, groups):
    count = ref.shape[0]
    row = lax.broadcasted_iota(jnp.int32, (count // groups, count), 0)
    column = lax.broadcasted_iota(jnp.int32, (count // groups, count), 1)
    pick = (column == row * groups + g).astype(F32).astype(BF16)
    return jnp.dot(pick, ref[...], preferred_element_type=F32)


def state_kernel(input_ref, inflow_ref, readout_ref, step_ref, log_ref, intra_ref, state_ref, sent_ref):
    rows = input_ref.shape[0]
    heads = step_ref.shape[0]
    groups = inflow_ref.shape[0] // rows
    per_group = heads // groups
    across = running_sum(log_ref, rows, False)
    down = running_sum(log_ref, rows, True)
    step = step_ref[...]
    i = lax.broadcasted_iota(jnp.int32, (rows, rows), 0)
    j = lax.broadcasted_iota(jnp.int32, (rows, rows), 1)
    causal = j <= i
    weight = jnp.transpose(jnp.exp(across[:, rows - 1 :] - across) * step)
    for g in range(groups):
        wide = group_rows(inflow_ref, g, groups)
        both = lax.dot_general(
            group_rows(readout_ref, g, groups).astype(BF16),
            wide.astype(BF16),
            (((1,), (1,)), ((), ())),
            preferred_element_type=F32,
        )
        for pair in range(0, per_group, 2):
            first = g * per_group + pair
            columns = slice(first * HP, (first + 2) * HP)
            inputs = input_ref[:, columns]
            intra, state = [], []
            for h in (first, first + 1):
                gap = jnp.where(causal, down[:, h : h + 1] - across[h : h + 1], 0.0)
                decay = jnp.where(causal, jnp.exp(gap), 0.0)
                mixing = (decay * both * step[h : h + 1]).astype(BF16)
                intra.append(jnp.dot(mixing, inputs, preferred_element_type=F32))
                weighted = (weight[:, h : h + 1] * wide).astype(BF16)
                state.append(
                    lax.dot_general(
                        weighted, inputs, (((0,), (0,)), ((), ())), preferred_element_type=F32
                    )
                )
            left = lax.broadcasted_iota(jnp.int32, (rows, 2 * HP), 1) < HP
            intra_ref[:, columns] = jnp.where(left, intra[0], intra[1])
            left = lax.broadcasted_iota(jnp.int32, (NS, 2 * HP), 1) < HP
            block = jnp.where(left, state[0], state[1])
            state_ref[:, columns] = block
            sent_ref[:, columns] = block.astype(BF16)


def state_local(inputs, inflow, readout, step, log_decay):
    rows, channels = inputs.shape
    assert rows == STRETCH
    return staged_call(
        state_kernel,
        (),
        (),
        (inputs, inflow, readout, step, log_decay),
        [
            jax.ShapeDtypeStruct((rows, channels), F32),
            jax.ShapeDtypeStruct((NS, channels), F32),
            jax.ShapeDtypeStruct((NS, channels), BF16),
        ],
    )


def lanes_of(factors, heads):
    left = lax.broadcasted_iota(jnp.int32, (1, 2 * HP), 1) < HP
    return jnp.concatenate(
        [
            jnp.where(left, factors[:, h : h + 1], factors[:, h + 1 : h + 2])
            for h in range(0, heads, 2)
        ],
        axis=1,
    )


def decay_between(place, total_ref, order, span, heads):
    row = lambda m: info_of(total_ref[order[m]])[6:7]
    upper = (place & span) != 0
    lead = own = jnp.zeros_like(row(0))
    theirs = jnp.zeros_like(own)
    for m in range(span):
        lead = lead + jnp.where((place ^ m) < place, row(m), 0.0)
        own = own + row(m)
        theirs = theirs + row(span + m)
    lead, own, theirs = jnp.exp(lead), jnp.exp(own), jnp.exp(theirs)
    return (
        lanes_of(jnp.where(upper, lead, 0.0), heads),
        lanes_of(jnp.where(upper, own, 1.0), heads),
        lanes_of(jnp.where(upper, 1.0, theirs), heads),
    )


def scan_kernel(order, span, heads, where_ref, total_ref, other_ref, state_ref, *refs):
    entering_ref = refs[0] if len(refs) == 4 else None
    new_entering_ref, new_state_ref, sent_ref = refs[-3:]
    lead, own, theirs = decay_between(where_ref[2], total_ref, order, span, heads)
    other = other_ref[...].astype(F32)
    entering = lead * other
    if entering_ref is not None:
        entering = entering + entering_ref[...]
    new_entering_ref[...] = entering
    state = own * other + theirs * state_ref[...]
    new_state_ref[...] = state
    sent_ref[...] = state.astype(BF16)


def scan_step(order, span, heads, where, totals, other, state, *entering):
    vmem = pl.BlockSpec(memory_space=pltpu.VMEM)
    smem = pl.BlockSpec(memory_space=pltpu.SMEM)
    like = jax.ShapeDtypeStruct(state.shape, F32)
    return pl.pallas_call(
        functools.partial(scan_kernel, order, span, heads),
        out_shape=[like, like, jax.ShapeDtypeStruct(state.shape, BF16)],
        in_specs=[smem] + [vmem] * (3 + len(entering)),
        out_specs=[vmem] * 3,
        compiler_params=pltpu.CompilerParams(vmem_limit_bytes=20 * 1024 * 1024),
    )(where, totals, other, state, *entering)


def span_route(span):
    nx, nz = lax.axis_size(EXP), lax.axis_size(SEQ)
    axis, bit = (EXP, span) if span < nx else (SEQ, span // nx)
    both = span * 2 < nx * nz
    pairs = [(i, i ^ bit) for i in range(lax.axis_size(axis)) if both or not i & bit]
    return axis, pairs


def finish_kernel(
    order, span, where_ref, total_ref, other_ref, entering_ref, intra_ref, readout_ref, log_ref, input_ref, gate_ref, skip_ref, gain_ref, out_ref
):
    rows, channels = input_ref.shape
    heads = log_ref.shape[0]
    groups = readout_ref.shape[0] // rows
    width = channels // groups
    grown = jnp.exp(running_sum(log_ref, rows, True))
    lead, _, _ = decay_between(where_ref[2], total_ref, order, span, heads)
    left = lax.broadcasted_iota(jnp.int32, (rows, 2 * HP), 1) < HP
    for g in range(groups):
        columns = slice(g * width, (g + 1) * width)
        inter = jnp.dot(
            group_rows(readout_ref, g, groups),
            lead[:, columns] * other_ref[:, columns].astype(F32) + entering_ref[:, columns],
            precision=HIGHEST,
            preferred_element_type=F32,
        )
        first = g * (heads // groups)
        factor = jnp.concatenate(
            [
                jnp.where(left, grown[:, h : h + 1], grown[:, h + 1 : h + 2])
                for h in range(first, first + heads // groups, 2)
            ],
            axis=1,
        )
        mixed = (
            intra_ref[:, columns]
            + factor * inter
            + skip_ref[:, columns] * input_ref[:, columns].astype(F32)
        )
        gate = gate_ref[:, columns].astype(F32)
        gated = mixed * (gate / (1.0 + jnp.exp(-gate)))
        mean_square = jnp.mean(gated * gated, axis=1, keepdims=True)
        normed = gated * lax.rsqrt(mean_square + EPSILON)
        out_ref[:, columns] = (normed * gain_ref[:, columns]).astype(BF16)


def state_finish(order, span, where, totals, other, entering, intra, *arrays):
    return staged_call(
        functools.partial(finish_kernel, order, span),
        (where,),
        (totals, other, entering, intra),
        arrays,
        [jax.ShapeDtypeStruct(arrays[2].shape, BF16)],
    )[0]


def routed_in_general(own, gate_up, down_proj):
    nz, nx, nt = lax.axis_size(SEQ), lax.axis_size(EXP), lax.axis_size(TP)
    x, t = lax.axis_index(EXP), lax.axis_index(TP)
    info, own = own[-16:, :256], own[:-16]
    rows, chunk = own.shape
    half = chunk // 2
    tp_bits = bits_of(nt)
    seq_stages = stages_of(SEQ, bits_of(nz))
    exp_stages = stages_of(EXP, bits_of(nx))
    far_stages, core_stages = stages_of(TP, tp_bits[:-1]), stages_of(TP, tp_bits[-1:])

    piece = spread(own, seq_stages)
    info_all = spread(info, seq_stages + exp_stages)
    left = spread(piece[..., :half], exp_stages + far_stages + core_stages)
    right = spread(piece[..., half:], far_stages + exp_stages + core_stages)
    left = left.reshape(2, nt // 2, nx, nz, rows, half)
    right = right.reshape(2, nx, nt // 2, nz, rows, half)
    info_all = info_all.reshape(nx, nz, 16, 256)

    where = jnp.stack([t, x * gate_up.shape[0]]).astype(jnp.int32)
    keep0, keep1, send0, send1 = experts_apply(
        offsets_of(tp_bits), where, info_all, left, right, jnp.swapaxes(gate_up, 1, 2), down_proj
    )

    def settle(kept, stages):
        for axis, bit in stages:
            count = kept.shape[0] // 2
            kept = kept[:count] + swap(kept[count:].astype(BF16), axis, bit).astype(F32)
        return kept

    def join(kept, sent):
        kept = kept.astype(F32) + swap(sent, *core_stages[0]).astype(F32)
        return kept.reshape(-1, rows, half)

    kept0 = settle(join(keep0, send0), far_stages[::-1] + exp_stages[::-1])
    kept1 = settle(join(keep1, send1), exp_stages[::-1] + far_stages[::-1])
    kept = settle(jnp.concatenate([kept0, kept1], axis=-1), seq_stages[::-1])
    routed_out = kept.reshape(rows, chunk).astype(BF16)
    order = [
        offsets_of(bits_of(nx)).index(i) * nz + offsets_of(bits_of(nz)).index(k)
        for k in range(nz)
        for i in range(nx)
    ]
    return routed_out, info_all.reshape(-1, 16, 256), order


def local(
    query_heads,
    key_heads,
    value_head_rows,
    state_input,
    state_gate,
    state_inflow,
    state_readout,
    step_size,
    log_decay,
    skip_scale,
    state_gain,
    hidden_in,
    mlp_gain,
    router_weight,
    expert_ids,
    slot_index,
    gate_up,
    down_proj,
):
    nz, nx, nt = lax.axis_size(SEQ), lax.axis_size(EXP), lax.axis_size(TP)
    z, x, t = lax.axis_index(SEQ), lax.axis_index(EXP), lax.axis_index(TP)
    _, width = hidden_in.shape
    chunk = width // nt
    seq_stages = stages_of(SEQ, bits_of(nz))
    exp_stages = stages_of(EXP, bits_of(nx))

    where = jnp.stack([t, x * gate_up.shape[0], z * nx + x]).astype(jnp.int32)
    own = norm_share(
        where,
        chunk,
        hidden_in,
        mlp_gain[None],
        router_weight.T,
        expert_ids.T,
        slot_index.T,
        log_decay.T,
    )
    flat = lambda a: a.reshape(-1, a.shape[2])
    heads = step_size.shape[1]
    inflow, readout = flat(state_inflow), flat(state_readout)
    intra, state, sent = state_local(state_input, inflow, readout, step_size.T, log_decay.T)
    kv = jnp.concatenate([flat(key_heads), flat(value_head_rows)], axis=0)
    finish_args = (
        intra,
        readout,
        log_decay.T,
        state_input,
        state_gate,
        jnp.repeat(skip_scale, HP)[None],
        state_gain[None],
    )

    if (nz, nx, nt) != (4, 2, 4):
        routed_out, info_all, order = routed_in_general(own, gate_up, down_proj)
        stages = seq_stages + exp_stages
        kv_own = spread(kv, stages[:-1])
        kv_parts = [a.reshape(-1, *kv.shape) for a in (kv_own, swap(kv_own, *stages[-1]))]
        far = [o * nx for o in offsets_of(bits_of(nz))]
        window_out = attention(
            query_heads, kv_parts, [i ^ o for i in offsets_of(bits_of(nx)) for o in far], where
        )
        entering, span = (), 1
        while span * 2 < nx * nz:
            other = lax.ppermute(sent, *span_route(span))
            *entering, state, sent = scan_step(
                order, span, heads, where, info_all, other, state, *entering
            )
            span *= 2
        other = lax.ppermute(sent, *span_route(span))
        state_out = state_finish(order, span, where, info_all, other, *entering, *finish_args)
        return window_out, state_out, routed_out

    return in_groups(
        where, own, kv, sent, state, query_heads, finish_args, gate_up, down_proj
    )


def in_groups(where, own, kv, sent, state, query_heads, finish_args, gate_up, down_proj):
    nz, nx = lax.axis_size(SEQ), lax.axis_size(EXP)
    heads = finish_args[2].shape[0]
    far, near, side, high, core = group_bits()
    order = [(k >> 1 << 2) | (i << 1) | (k & 1) for k in range(nz) for i in range(nx)]
    beyond = swap(own, SEQ, far)
    beside = swap(own, SEQ, near)
    here = jnp.stack([own, beside])
    kv_own = jnp.stack([kv, swap(kv, EXP, side)])
    kv_own = jnp.stack([kv_own, swap(kv_own, SEQ, far)])
    there = jnp.stack([beyond, swap(beyond, SEQ, near)])
    pieces_a = spread_near(here)
    pieces_b = spread_near(there)
    info_all = jnp.concatenate(
        [p[0][..., -16:, :256].reshape(-1, 16, 256) for p in (pieces_a, pieces_b)], axis=0
    )
    other = lax.ppermute(sent, *span_route(1))
    *entering, state, sent = scan_step(order, 1, heads, where, info_all, other, state)
    other2 = lax.ppermute(sent, *span_route(2))
    kv_other = swap(kv_own, SEQ, near)

    offsets = ((0, high), (core, core ^ high))
    keep_a, send_a, keep_b, send_b = experts_gather(
        offsets, where, pieces_a + pieces_b, gate_up, down_proj
    )

    kept_b = fold(keep_b.astype(F32), send_b, TP, core)
    kept_a = fold(keep_a.astype(F32), send_a, TP, core)
    *entering, state, sent = scan_step(order, 2, heads, where, info_all, other2, state, *entering)
    other4 = lax.ppermute(sent, *span_route(4))
    firsts, routed = [], []
    for name, kept in (("b", kept_b), ("a", kept_a)):
        left = fold(kept[0, 0], kept[0, 1], TP, high)
        right = fold(kept[1, 0], kept[1, 1], EXP, side)
        firsts.append((name, left, right))
    kv_parts = [a.reshape(-1, *kv.shape) for a in (kv_own, kv_other)]
    kv_offsets = [n * nx ^ f * nx ^ i for n in (0, near) for f in (0, far) for i in (0, side)]
    window_out = attention(query_heads, kv_parts, kv_offsets, where)
    state_out = state_finish(order, 4, where, info_all, other4, *entering, *finish_args)
    for name, left, right in firsts:
        left = fold(left[0], left[1], EXP, side)
        right = fold(right[0], right[1], TP, high)
        both = jnp.concatenate([left, right], axis=-1)
        routed.append(fold(both[0], both[1], SEQ, near))
    routed_out = fold(routed[1], routed[0], SEQ, far).astype(BF16)
    return window_out, state_out, routed_out


def solution(mesh):
    block = (SEQ, EXP)
    program = jax.shard_map(
        local,
        mesh=mesh,
        in_specs=(
            P(block, TP, None),
            P(block, TP, None),
            P(block, TP, None),
            P(block, TP),
            P(block, TP),
            P(block, TP, None),
            P(block, TP, None),
            P(block, TP),
            P(block, TP),
            P(TP),
            P(TP),
            P(block, None),
            P(),
            P(),
            P(block, None),
            P(block, None),
            P(EXP, (SEQ, TP), None, None),
            P(EXP, (SEQ, TP), None),
        ),
        out_specs=(P(block, TP, None), P(block, TP), P(block, TP)),
        check_vma=False,
    )
    if tuple(mesh.shape[a] for a in (SEQ, EXP, TP)) != (4, 2, 4):
        return program
    return program
```

```python
import functools
import math

import jax
import jax.numpy as jnp
from jax import lax
from jax.experimental import pallas as pl
from jax.experimental.pallas import tpu as pltpu
from jax.sharding import PartitionSpec as P

SEQ, EXP, TP = "seq", "exp", "tp"
WINDOW = 4096
HP = 64
NS = 128
STRETCH = 128
CAP = 40
EPSILON = 1e-05
F32 = jnp.float32
BF16 = jnp.bfloat16


def bits_of(count):
    assert count & (count - 1) == 0
    return [1 << b for b in reversed(range(count.bit_length() - 1))]


def swap(block, axis, bit):
    return lax.ppermute(block, axis, [(i, i ^ bit) for i in range(lax.axis_size(axis))])


def spread(block, stages):
    for axis, bit in stages:
        block = jnp.stack([block, swap(block, axis, bit)])
    return block


def stages_of(axis, bits):
    return [(axis, bit) for bit in bits]


def offsets_of(bits):
    offsets = [0]
    for bit in bits:
        offsets = offsets + [o ^ bit for o in offsets]
    return offsets


def staged_call(body, scalars, near, arrays, out_shape, scratch=(), vmem=20):
    count, outs = len(arrays), len(out_shape)

    def kernel(*refs):
        inside = list(refs)
        first, inside = inside[: len(scalars) + len(near)], inside[len(scalars) + len(near) :]
        sources, inside = inside[:count], inside[count:]
        results, inside = inside[:outs], inside[outs:]
        targets, inside = inside[:count], inside[count:]
        sem, extra = inside[0], inside[1:]
        copies = [
            pltpu.make_async_copy(source, target, sem.at[i])
            for i, (source, target) in enumerate(zip(sources, targets))
        ]
        for copy in copies:
            copy.start()
        for copy in copies:
            copy.wait()
        body(*first, *targets, *results, *extra)

    smem = pl.BlockSpec(memory_space=pltpu.SMEM)
    local = pl.BlockSpec(memory_space=pltpu.VMEM)
    return pl.pallas_call(
        kernel,
        out_shape=out_shape,
        in_specs=[smem] * len(scalars)
        + [local] * len(near)
        + [pl.BlockSpec(memory_space=pltpu.HBM)] * count,
        out_specs=[local] * outs,
        scratch_shapes=[pltpu.VMEM(a.shape, a.dtype) for a in arrays]
        + [pltpu.SemaphoreType.DMA((count,))]
        + list(scratch),
        compiler_params=pltpu.CompilerParams(vmem_limit_bytes=vmem * 1024 * 1024),
    )(*scalars, *near, *[pltpu.with_memory_space_constraint(a, pltpu.HBM) for a in arrays])


def attention_kernel(offsets, begins, ends, where_ref, query_ref, *refs):
    count = len(refs) - (5 if ends else 4) - (0 if begins else 3)
    kv_refs, refs = refs[:count], refs[count:]
    if not begins:
        old_top_ref, old_sum_ref, old_acc_ref, *refs = refs
    if ends:
        out_ref, *refs = refs
        score_ref, top_ref, sum_ref, acc_ref = refs
    else:
        top_ref, sum_ref, acc_ref, score_ref = refs
    total, size = query_ref.shape
    wide = kv_refs[0].shape[1] // 2
    keys = wide // 2
    heads = total // keys
    mine = where_ref[2]
    scale = math.log2(math.e) / math.sqrt(size)
    row = lax.broadcasted_iota(jnp.int32, (total, keys), 0)
    column = lax.broadcasted_iota(jnp.int32, (total, keys), 1)
    lower = lax.rem(row, heads) < heads // 2
    behind = row // heads - column
    blocks = [(kv_ref, b) for kv_ref in kv_refs for b in range(kv_ref.shape[0])]
    gaps = [(mine - (mine ^ offset)) * keys for offset in offsets]
    seen = [(gap >= 0) & (gap - (keys - 1) < WINDOW) for gap in gaps]
    top_ref[...] = jnp.full_like(top_ref, -jnp.inf) if begins else old_top_ref[...]

    def scores(at):
        kv_ref, b = blocks[at]
        score = lax.dot_general(
            query_ref[...], kv_ref[b, :wide], (((1,), (1,)), ((), ())), preferred_element_type=F32
        )
        return jnp.where(lower, score[:, :keys], score[:, keys:])

    for at, gap in enumerate(gaps):
        inside = (gap >= keys - 1) & (gap + keys - 1 < WINDOW)

        @pl.when(inside)
        def _(at=at):
            score = scores(at)
            score_ref[at] = score
            top_ref[...] = jnp.maximum(top_ref[...], score)

        @pl.when(seen[at] & jnp.logical_not(inside))
        def _(at=at, gap=gap):
            distance = behind + gap
            score = jnp.where((distance >= 0) & (distance < WINDOW), scores(at), -jnp.inf)
            score_ref[at] = score
            top_ref[...] = jnp.maximum(top_ref[...], score)

    top = jnp.max(top_ref[...], axis=1, keepdims=True)
    top_ref[...] = jnp.broadcast_to(top, (total, keys))
    if begins:
        sum_ref[...] = jnp.zeros_like(sum_ref)
        acc_ref[...] = jnp.zeros_like(acc_ref)
    else:
        shrink = jnp.exp2((old_top_ref[...] - top_ref[...]) * scale)
        sum_ref[...] = old_sum_ref[...] * shrink
        acc_ref[...] = old_acc_ref[...] * shrink

    for at, (kv_ref, b) in enumerate(blocks):

        @pl.when(seen[at])
        def _(at=at, kv_ref=kv_ref, b=b):
            weight = jnp.exp2((score_ref[at] - top_ref[...]) * scale)
            sum_ref[...] += weight
            weight = jnp.concatenate(
                [jnp.where(lower, weight, 0.0), jnp.where(lower, 0.0, weight)], axis=1
            )
            acc_ref[...] += jnp.dot(
                weight.astype(BF16), kv_ref[b, wide:], preferred_element_type=F32
            )

    if ends:
        out_ref[...] = (acc_ref[...] / jnp.sum(sum_ref[...], axis=1, keepdims=True)).astype(BF16)


def attention(query, kv_parts, offsets, where, carried=None, ends=True):
    rows, heads, size = query.shape
    assert kv_parts[0].shape[1] == 4 * rows and size == rows
    total = rows * heads
    begins = carried is None
    vmem = pl.BlockSpec(memory_space=pltpu.VMEM)
    state = [jax.ShapeDtypeStruct((total, rows), F32)] * 3
    scores = [pltpu.VMEM((len(offsets), total, rows), F32)]
    out = pl.pallas_call(
        functools.partial(attention_kernel, offsets, begins, ends),
        out_shape=jax.ShapeDtypeStruct((total, size), BF16) if ends else state,
        in_specs=[pl.BlockSpec(memory_space=pltpu.SMEM), vmem]
        + [vmem] * (len(kv_parts) + (0 if begins else 3)),
        out_specs=vmem if ends else [vmem] * 3,
        scratch_shapes=scores + [pltpu.VMEM((total, rows), F32)] * 3 if ends else scores,
        compiler_params=pltpu.CompilerParams(
            vmem_limit_bytes=(len(offsets) + 40) * total * rows * 4
        ),
    )(where, query.reshape(total, size), *kv_parts, *(carried or ()))
    return out.reshape(rows, heads, size) if ends else out


def norm_kernel(
    where_ref, hidden_ref, gain_ref, router_ref, id_ref, slot_ref, log_ref, own_ref, normed_ref
):
    rows, _ = hidden_ref.shape
    chunk = own_ref.shape[1]
    hidden = hidden_ref[...].astype(F32)
    mean_square = jnp.mean(hidden * hidden, axis=1, keepdims=True)
    normed = (hidden * lax.rsqrt(mean_square + EPSILON) * gain_ref[...]).astype(BF16)
    normed_ref[...] = normed
    start = pl.multiple_of(where_ref[0] * chunk, 128)
    own_ref[0:rows, :] = normed_ref[:, pl.ds(start, chunk)]
    logits = lax.dot_general(
        router_ref[...], normed, (((1,), (1,)), ((), ())), preferred_element_type=F32
    )
    gates = 1.0 / (1.0 + jnp.exp(-logits))
    expert = lax.broadcasted_iota(jnp.int32, gates.shape, 0)
    chosen = [
        jnp.sum(jnp.where(id_ref[k : k + 1] == expert, gates, 0.0), axis=0, keepdims=True)
        for k in range(2)
    ]
    both = chosen[0] + chosen[1]
    decay = jnp.sum(log_ref[...], axis=1, keepdims=True)
    head = lax.broadcasted_iota(jnp.int32, log_ref.shape, 0)
    lane = lax.broadcasted_iota(jnp.int32, log_ref.shape, 1)
    decay = jnp.sum(jnp.where(head == lane, decay, 0.0), axis=0, keepdims=True)
    info = jnp.concatenate(
        [
            id_ref[...].astype(F32),
            slot_ref[...].astype(F32),
            chosen[0] / both,
            chosen[1] / both,
            decay,
            jnp.zeros_like(decay),
        ],
        axis=0,
    )
    parts = []
    for _ in range(3):
        part = info.astype(BF16).astype(F32)
        parts.append(part)
        info = info - part
    tail = jnp.concatenate(
        [
            jnp.concatenate([parts[0], parts[1]], axis=1),
            jnp.concatenate([parts[2], jnp.zeros_like(info)], axis=1),
        ],
        axis=0,
    )
    tail = jnp.concatenate([tail, jnp.zeros((16, chunk - 256), F32)], axis=1)
    own_ref[rows:, :] = tail.astype(BF16)


def info_of(block):
    block = block.astype(F32)
    return block[0:8, 0:128] + block[0:8, 128:256] + block[8:16, 0:128]


def norm_share(where, chunk, hidden, gain, router, ids, slots, log_decay):
    rows, width = hidden.shape
    assert rows == 128 and chunk >= 512
    return staged_call(
        norm_kernel,
        (where,),
        (),
        (hidden, gain, router, ids, slots, log_decay),
        [jax.ShapeDtypeStruct((rows + 16, chunk), BF16)],
        [pltpu.VMEM((rows, width), BF16)],
    )[0]


def expert_kernel(
    offsets,
    where_ref,
    info_ref,
    left_ref,
    right_ref,
    gate_up_ref,
    down_ref,
    keep0_ref,
    keep1_ref,
    send0_ref,
    send1_ref,
    rows_ref,
    hot_ref,
    weight_ref,
):
    expert = pl.program_id(1)
    experts = pl.num_programs(1)
    me = where_ref[0]
    first = where_ref[1]
    far, _, nz, tokens, half = keep0_ref.shape
    parts = 2 * far
    local = rows_ref.shape[1]
    pairs = rows_ref.shape[0]

    def column(part, h):
        return pl.multiple_of((me ^ offsets[part]) * (2 * half) + h * half, 128)

    def pair_at(p):
        return (2 * p) // nz, (2 * p) % nz

    @pl.when(expert == 0)
    def _():
        for p in range(pairs):
            mx, mz = pair_at(p)
            info = jnp.concatenate([info_of(info_ref[mx, mz]), info_of(info_ref[mx, mz + 1])], axis=1)
            info_id = info[0:2].astype(jnp.int32)
            info_slot = info[2:4].astype(jnp.int32)
            block = lax.broadcasted_iota(jnp.int32, (1, 2 * tokens), 1) // tokens
            row = lax.broadcasted_iota(jnp.int32, (2 * CAP, 2 * tokens), 0)
            for e in range(local):
                match = []
                for k in range(2):
                    live = (info_slot[k : k + 1] >= 0) & (info_id[k : k + 1] == first + e)
                    code = jnp.where(live, block * CAP + info_slot[k : k + 1], -1)
                    match.append(row == code)
                hot_ref[p, e] = (match[0] | match[1]).astype(F32).astype(BF16)
                share = jnp.where(match[0], info[4:5], 0.0) + jnp.where(match[1], info[5:6], 0.0)
                weight_ref[p, e] = jnp.broadcast_to(
                    jnp.sum(share, axis=1, keepdims=True), (2 * CAP, 128)
                )
            hot = hot_ref[p].reshape(local * 2 * CAP, 2 * tokens)
            for part in range(parts):
                core, high = part // far, part % far
                for h in range(2):
                    if h == 0:
                        piece = left_ref[core, high, mx, mz : mz + 2]
                    else:
                        piece = right_ref[core, mx, high, mz : mz + 2]
                    piece = piece.reshape(2 * tokens, half)
                    picked = jnp.dot(hot, piece, preferred_element_type=F32).astype(BF16)
                    rows_ref[p, :, :, pl.ds(column(part, h), half)] = picked.reshape(
                        local, 2 * CAP, half
                    )

    rows = rows_ref[:, expert].reshape(pairs * 2 * CAP, rows_ref.shape[3])
    nt = (((1,), (1,)), ((), ()))
    gate = lax.dot_general(rows, gate_up_ref[0], nt, preferred_element_type=F32)
    up = lax.dot_general(rows, gate_up_ref[1], nt, preferred_element_type=F32)
    hidden = (gate / (1.0 + jnp.exp(-gate)) * up).astype(BF16)
    value = jnp.dot(hidden, down_ref[...], preferred_element_type=F32)
    for p in range(pairs):
        scaled = value[p * 2 * CAP : (p + 1) * 2 * CAP] * weight_ref[p, expert][:, :1]
        rows_ref[p, expert] = scaled.astype(BF16)

    @pl.when(expert == experts - 1)
    def _():
        for p in range(pairs):
            mx, mz = pair_at(p)
            hot = hot_ref[p].reshape(local * 2 * CAP, 2 * tokens)
            for part in range(parts):
                core, high = part // far, part % far
                for h in range(2):
                    value = rows_ref[p, :, :, pl.ds(column(part, h), half)]
                    value = value.reshape(local * 2 * CAP, half)
                    total = lax.dot_general(
                        hot, value, (((0,), (0,)), ((), ())), preferred_element_type=F32
                    )
                    total = total.astype(BF16).reshape(2, tokens, half)
                    if h == 0:
                        target = send0_ref if core else keep0_ref
                        target[high, mx, mz : mz + 2] = total
                    else:
                        target = send1_ref if core else keep1_ref
                        target[mx, high, mz : mz + 2] = total


def experts_apply(offsets, where, info, left, right, gate_up, down):
    nx, nz = info.shape[:2]
    _, far, _, _, tokens, half = left.shape
    local, _, units, width = gate_up.shape
    gx = max(1, 8 // nz)
    pairs = gx * nz // 2
    once = pl.Buffered(1)
    shape0 = jax.ShapeDtypeStruct((far, nx, nz, tokens, half), BF16)
    shape1 = jax.ShapeDtypeStruct((nx, far, nz, tokens, half), BF16)
    spec0 = pl.BlockSpec((far, gx, nz, tokens, half), lambda g, e, w: (0, g, 0, 0, 0))
    spec1 = pl.BlockSpec((gx, far, nz, tokens, half), lambda g, e, w: (g, 0, 0, 0, 0))
    return pl.pallas_call(
        functools.partial(expert_kernel, offsets),
        out_shape=[shape0, shape1, shape0, shape1],
        grid_spec=pltpu.PrefetchScalarGridSpec(
            num_scalar_prefetch=1,
            grid=(nx // gx, local),
            in_specs=[
                pl.BlockSpec((gx, nz, 16, 256), lambda g, e, w: (g, 0, 0, 0)),
                pl.BlockSpec(
                    (2, far, gx, nz, tokens, half),
                    lambda g, e, w: (0, 0, g, 0, 0, 0),
                    pipeline_mode=once,
                ),
                pl.BlockSpec(
                    (2, gx, far, nz, tokens, half),
                    lambda g, e, w: (0, g, 0, 0, 0, 0),
                    pipeline_mode=once,
                ),
                pl.BlockSpec((None, 2, units, width), lambda g, e, w: (e, 0, 0, 0)),
                pl.BlockSpec((None, units, width), lambda g, e, w: (e, 0, 0)),
            ],
            out_specs=[spec0, spec1, spec0, spec1],
            scratch_shapes=[
                pltpu.VMEM((pairs, local, 2 * CAP, width), BF16),
                pltpu.VMEM((pairs, local, 2 * CAP, 2 * tokens), BF16),
                pltpu.VMEM((pairs, local, 2 * CAP, 128), F32),
            ],
        ),
        compiler_params=pltpu.CompilerParams(vmem_limit_bytes=60 * 1024 * 1024),
        name="experts",
    )(where, info, left, right, gate_up, down)


def matches(info_ref, blocks, first, local):
    info = jnp.concatenate([info_of(info_ref[b]) for b in blocks], axis=1)
    tokens = info_ref.shape[2] // 2
    ids, slots = info[0:2].astype(jnp.int32), info[2:4].astype(jnp.int32)
    block = lax.broadcasted_iota(jnp.int32, (1, 2 * tokens), 1) // tokens
    row = lax.broadcasted_iota(jnp.int32, (2 * CAP, 2 * tokens), 0)
    for e in range(local):
        found = []
        for k in range(2):
            live = (slots[k : k + 1] >= 0) & (ids[k : k + 1] == first + e)
            found.append(row == jnp.where(live, block * CAP + slots[k : k + 1], -1))
        share = jnp.where(found[0], info[4:5], 0.0) + jnp.where(found[1], info[5:6], 0.0)
        yield (found[0] | found[1]).astype(F32).astype(BF16), jnp.sum(share, axis=1, keepdims=True)


def column_of(me, offset, h, half):
    return pl.multiple_of((me ^ offset) * (2 * half) + h * half, 128)


def combine(me, offsets, hot, value_of, keep_ref, send_ref, xo):
    tokens, half = keep_ref.shape[-2:]
    for core in range(2):
        for yi in range(2):
            for h in range(2):
                value = value_of(column_of(me, offsets[core][yi], h, half), half)
                total = lax.dot_general(
                    hot, value, (((0,), (0,)), ((), ())), preferred_element_type=F32
                )
                target = send_ref if core else keep_ref
                place = (h, yi, xo) if h == 0 else (h, xo, yi)
                target[place] = total.astype(BF16).reshape(2, tokens, half)


def paired(both):
    count, width = both.shape
    lane = lax.broadcasted_iota(jnp.int32, (count, 128), 1)
    low = lane < 64
    even = jnp.where(low, 2 * lane, 2 * lane - 128)
    take = lambda a, i: jnp.take_along_axis(a, i, axis=1, mode="promise_in_bounds")
    hidden = []
    for c in range(0, width, 256):
        one = both[:, c : c + 128]
        two = both[:, c + 128 : c + 256] if c + 128 < width else one
        gate = jnp.where(low, take(one, even), take(two, even))
        up = jnp.where(low, take(one, even + 1), take(two, even + 1))
        unit = (gate / (1.0 + jnp.exp(-gate)) * up).astype(BF16)
        hidden.append(unit[:, : (width - c) // 2] if width - c < 256 else unit)
    return jnp.concatenate(hidden, axis=1)


def gather_kernel(offsets, *refs):
    where_ref, gate_up_ref, down_ref = refs[:3]
    pieces = refs[3:19]
    results = refs[19:23]
    all_ref, rows_ref, hot_ref, weight_ref, wide_ref, tall_ref, info_ref = refs[23:30]
    piece_sem, wide_sem, tall_sem, info_sem = refs[30:]
    me, first = where_ref[0], where_ref[1]
    pairs, local, places, width = rows_ref.shape
    tokens, half = all_ref.shape[2], pieces[0].shape[-1]
    units = down_ref.shape[1]
    count = pairs * places

    def fetch(e, slot):
        return (
            pltpu.make_async_copy(gate_up_ref.at[e], wide_ref.at[slot], wide_sem.at[slot]),
            pltpu.make_async_copy(down_ref.at[e], tall_ref.at[slot], tall_sem.at[slot]),
        )

    copies = []
    for p in range(pairs):
        g, xo = p // 2, p % 2
        for core in range(2):
            for yi in range(2):
                for h in range(2):
                    if h == 0:
                        source = pieces[8 * g + 2 * core + yi].at[xo, :, 0:tokens]
                    else:
                        source = pieces[8 * g + 4 + 2 * core + xo].at[yi]
                    column = column_of(me, offsets[core][yi], h, half)
                    copies.append(
                        pltpu.make_async_copy(
                            source,
                            all_ref.at[p, :, :, pl.ds(column, half)],
                            piece_sem.at[len(copies)],
                        )
                    )
    notes = [
        pltpu.make_async_copy(
            pieces[b // 4 * 8].at[b // 2 % 2, b % 2, tokens : tokens + 16],
            info_ref.at[b],
            info_sem.at[b],
        )
        for b in range(2 * pairs)
    ]
    for copy in notes + copies:
        copy.start()
    for slot in range(2):
        if slot < local:
            for copy in fetch(slot, slot):
                copy.start()
    for copy in notes:
        copy.wait()
    for p in range(pairs):
        for e, (hot, weight) in enumerate(matches(info_ref, (2 * p, 2 * p + 1), first, local)):
            hot_ref[p, e] = hot
            weight_ref[p, e] = jnp.broadcast_to(weight, (places, 128))
    for p in range(pairs):
        for copy in copies[8 * p : 8 * p + 8]:
            copy.wait()
        hot = hot_ref[p].reshape(local * places, 2 * tokens)
        picked = jnp.dot(
            hot, all_ref[p].reshape(2 * tokens, width), preferred_element_type=F32
        ).astype(BF16)
        rows_ref[p] = picked.reshape(local, places, width)

    def one_expert(e, _):
        slot = lax.rem(e, 2)
        for copy in fetch(e, slot):
            copy.wait()
        rows = rows_ref[:, e].reshape(count, width)
        wide = wide_ref[slot].reshape(2 * units, width)
        both = lax.dot_general(
            rows, wide, (((1,), (1,)), ((), ())), preferred_element_type=F32
        )
        value = jnp.dot(paired(both), tall_ref[slot], preferred_element_type=F32)
        for p in range(pairs):
            scaled = value[p * places : (p + 1) * places] * weight_ref[p, e][:, :1]
            rows_ref[p, e] = scaled.astype(BF16)

        @pl.when(e + 2 < local)
        def _():
            for copy in fetch(e + 2, slot):
                copy.start()

        return 0

    lax.fori_loop(0, local, one_expert, 0)
    for p in range(pairs):
        combine(
            me,
            offsets,
            hot_ref[p].reshape(local * places, 2 * tokens),
            lambda column, half: rows_ref[p, :, :, pl.ds(column, half)].reshape(
                local * places, half
            ),
            *results[p // 2 * 2 : p // 2 * 2 + 2],
            p % 2,
        )


def experts_gather(offsets, where, pieces, gate_up, down):
    half = pieces[0].shape[-1]
    tokens = pieces[4].shape[-2]
    local, units, _, width = gate_up.shape
    pairs, places = 4, 2 * CAP
    result = jax.ShapeDtypeStruct((2, 2, 2, 2, tokens, half), BF16)
    smem = pl.BlockSpec(memory_space=pltpu.SMEM)
    vmem = pl.BlockSpec(memory_space=pltpu.VMEM)
    hbm = pl.BlockSpec(memory_space=pl.ANY)
    return pl.pallas_call(
        functools.partial(gather_kernel, offsets),
        out_shape=[result] * 4,
        in_specs=[smem, hbm, hbm] + [hbm] * len(pieces),
        out_specs=[vmem] * 4,
        scratch_shapes=[
            pltpu.VMEM((pairs, 2, tokens, width), BF16),
            pltpu.VMEM((pairs, local, places, width), BF16),
            pltpu.VMEM((pairs, local, places, 2 * tokens), BF16),
            pltpu.VMEM((pairs, local, places, 128), F32),
            pltpu.VMEM((2, units, 2, width), BF16),
            pltpu.VMEM((2, units, width), BF16),
            pltpu.VMEM((2 * pairs, 16, 2 * 128), BF16),
            pltpu.SemaphoreType.DMA((8 * pairs,)),
            pltpu.SemaphoreType.DMA((2,)),
            pltpu.SemaphoreType.DMA((2,)),
            pltpu.SemaphoreType.DMA((2 * pairs,)),
        ],
        compiler_params=pltpu.CompilerParams(vmem_limit_bytes=44 * 1024 * 1024),
        name="experts",
    )(where, gate_up, down, *pieces)


def group_bits():
    far, near = bits_of(lax.axis_size(SEQ))
    (side,) = bits_of(lax.axis_size(EXP))
    high, core = bits_of(lax.axis_size(TP))
    return far, near, side, high, core


def spread_near(block):
    _, _, side, high, core = group_bits()
    half = block.shape[-1] // 2
    left, right = block[..., :half], block[..., :-16, half:]
    left = jnp.stack([left, swap(left, EXP, side)])
    right = jnp.stack([right, swap(right, TP, high)])
    left2 = swap(left, TP, high)
    right2 = swap(right, EXP, side)
    first = [swap(left, TP, core), swap(right, TP, core)]
    second = [swap(left2, TP, core), swap(right2, TP, core)]
    return [left, left2, first[0], second[0], right, right2, first[1], second[1]]


def fold(kept, sent, axis, bit):
    return kept + swap(sent.astype(BF16), axis, bit).astype(F32)


HIGHEST = lax.Precision.HIGHEST


def running_sum(log_ref, rows, columns):
    i = lax.broadcasted_iota(jnp.int32, (rows, rows), 0)
    j = lax.broadcasted_iota(jnp.int32, (rows, rows), 1)
    decay = log_ref[...]
    if columns:
        ones = (j <= i).astype(F32)
        return lax.dot_general(
            ones, decay, (((1,), (1,)), ((), ())), precision=HIGHEST, preferred_element_type=F32
        )
    ones = (i <= j).astype(F32)
    return jnp.dot(decay, ones, precision=HIGHEST, preferred_element_type=F32)


def group_rows(ref, g, groups):
    count = ref.shape[0]
    row = lax.broadcasted_iota(jnp.int32, (count // groups, count), 0)
    column = lax.broadcasted_iota(jnp.int32, (count // groups, count), 1)
    pick = (column == row * groups + g).astype(F32).astype(BF16)
    return jnp.dot(pick, ref[...], preferred_element_type=F32)


def state_kernel(
    input_ref,
    inflow_ref,
    readout_ref,
    step_ref,
    log_ref,
    key_ref,
    value_ref,
    intra_ref,
    state_ref,
    sent_ref,
    kv_ref,
):
    shared = key_ref.shape[0] // input_ref.shape[0]
    for n, ref in enumerate((key_ref, value_ref)):
        for h in range(shared):
            start = (n * shared + h) * input_ref.shape[0]
            kv_ref[start : start + input_ref.shape[0]] = group_rows(ref, h, shared).astype(BF16)
    rows = input_ref.shape[0]
    heads = step_ref.shape[0]
    groups = inflow_ref.shape[0] // rows
    per_group = heads // groups
    across = running_sum(log_ref, rows, False)
    down = running_sum(log_ref, rows, True)
    step = step_ref[...]
    i = lax.broadcasted_iota(jnp.int32, (rows, rows), 0)
    j = lax.broadcasted_iota(jnp.int32, (rows, rows), 1)
    causal = j <= i
    weight = jnp.transpose(jnp.exp(across[:, rows - 1 :] - across) * step)
    for g in range(groups):
        wide = group_rows(inflow_ref, g, groups)
        both = lax.dot_general(
            group_rows(readout_ref, g, groups).astype(BF16),
            wide.astype(BF16),
            (((1,), (1,)), ((), ())),
            preferred_element_type=F32,
        )
        for pair in range(0, per_group, 2):
            first = g * per_group + pair
            columns = slice(first * HP, (first + 2) * HP)
            inputs = input_ref[:, columns]
            intra, state = [], []
            for h in (first, first + 1):
                gap = jnp.where(causal, down[:, h : h + 1] - across[h : h + 1], 0.0)
                decay = jnp.where(causal, jnp.exp(gap), 0.0)
                mixing = (decay * both * step[h : h + 1]).astype(BF16)
                intra.append(jnp.dot(mixing, inputs, preferred_element_type=F32))
                weighted = (weight[:, h : h + 1] * wide).astype(BF16)
                state.append(
                    lax.dot_general(
                        weighted, inputs, (((0,), (0,)), ((), ())), preferred_element_type=F32
                    )
                )
            left = lax.broadcasted_iota(jnp.int32, (rows, 2 * HP), 1) < HP
            intra_ref[:, columns] = jnp.where(left, intra[0], intra[1])
            left = lax.broadcasted_iota(jnp.int32, (NS, 2 * HP), 1) < HP
            block = jnp.where(left, state[0], state[1])
            state_ref[:, columns] = block
            sent_ref[:, columns] = block.astype(BF16)


def state_local(inputs, inflow, readout, step, log_decay, keys, values):
    rows, channels = inputs.shape
    assert rows == STRETCH
    return staged_call(
        state_kernel,
        (),
        (),
        (inputs, inflow, readout, step, log_decay, keys, values),
        [
            jax.ShapeDtypeStruct((rows, channels), F32),
            jax.ShapeDtypeStruct((NS, channels), F32),
            jax.ShapeDtypeStruct((NS, channels), BF16),
            jax.ShapeDtypeStruct((2 * keys.shape[0], keys.shape[1]), BF16),
        ],
    )


def lanes_of(factors, heads):
    left = lax.broadcasted_iota(jnp.int32, (1, 2 * HP), 1) < HP
    return jnp.concatenate(
        [
            jnp.where(left, factors[:, h : h + 1], factors[:, h + 1 : h + 2])
            for h in range(0, heads, 2)
        ],
        axis=1,
    )


def decay_between(place, total_ref, order, span, heads):
    row = lambda m: info_of(total_ref[order[m]])[6:7]
    upper = (place & span) != 0
    lead = own = jnp.zeros_like(row(0))
    theirs = jnp.zeros_like(own)
    for m in range(span):
        lead = lead + jnp.where((place ^ m) < place, row(m), 0.0)
        own = own + row(m)
        theirs = theirs + row(span + m)
    lead, own, theirs = jnp.exp(lead), jnp.exp(own), jnp.exp(theirs)
    return (
        lanes_of(jnp.where(upper, lead, 0.0), heads),
        lanes_of(jnp.where(upper, own, 1.0), heads),
        lanes_of(jnp.where(upper, 1.0, theirs), heads),
    )


def scan_kernel(order, span, heads, where_ref, total_ref, other_ref, state_ref, *refs):
    entering_ref = refs[0] if len(refs) == 4 else None
    new_entering_ref, new_state_ref, sent_ref = refs[-3:]
    lead, own, theirs = decay_between(where_ref[2], total_ref, order, span, heads)
    other = other_ref[...].astype(F32)
    entering = lead * other
    if entering_ref is not None:
        entering = entering + entering_ref[...]
    new_entering_ref[...] = entering
    state = own * other + theirs * state_ref[...]
    new_state_ref[...] = state
    sent_ref[...] = state.astype(BF16)


def scan_step(order, span, heads, where, totals, other, state, *entering):
    vmem = pl.BlockSpec(memory_space=pltpu.VMEM)
    smem = pl.BlockSpec(memory_space=pltpu.SMEM)
    like = jax.ShapeDtypeStruct(state.shape, F32)
    return pl.pallas_call(
        functools.partial(scan_kernel, order, span, heads),
        out_shape=[like, like, jax.ShapeDtypeStruct(state.shape, BF16)],
        in_specs=[smem] + [vmem] * (3 + len(entering)),
        out_specs=[vmem] * 3,
        compiler_params=pltpu.CompilerParams(vmem_limit_bytes=20 * 1024 * 1024),
    )(where, totals, other, state, *entering)


def span_route(span):
    nx, nz = lax.axis_size(EXP), lax.axis_size(SEQ)
    axis, bit = (EXP, span) if span < nx else (SEQ, span // nx)
    both = span * 2 < nx * nz
    pairs = [(i, i ^ bit) for i in range(lax.axis_size(axis)) if both or not i & bit]
    return axis, pairs


def finish_kernel(
    order, span, where_ref, total_ref, other_ref, entering_ref, intra_ref, readout_ref, log_ref, input_ref, gate_ref, skip_ref, gain_ref, out_ref
):
    rows, channels = input_ref.shape
    heads = log_ref.shape[0]
    groups = readout_ref.shape[0] // rows
    width = channels // groups
    grown = jnp.exp(running_sum(log_ref, rows, True))
    lead, _, _ = decay_between(where_ref[2], total_ref, order, span, heads)
    left = lax.broadcasted_iota(jnp.int32, (rows, 2 * HP), 1) < HP
    for g in range(groups):
        columns = slice(g * width, (g + 1) * width)
        inter = jnp.dot(
            group_rows(readout_ref, g, groups),
            lead[:, columns] * other_ref[:, columns].astype(F32) + entering_ref[:, columns],
            precision=HIGHEST,
            preferred_element_type=F32,
        )
        first = g * (heads // groups)
        factor = jnp.concatenate(
            [
                jnp.where(left, grown[:, h : h + 1], grown[:, h + 1 : h + 2])
                for h in range(first, first + heads // groups, 2)
            ],
            axis=1,
        )
        mixed = (
            intra_ref[:, columns]
            + factor * inter
            + skip_ref[:, columns] * input_ref[:, columns].astype(F32)
        )
        gate = gate_ref[:, columns].astype(F32)
        gated = mixed * (gate / (1.0 + jnp.exp(-gate)))
        mean_square = jnp.mean(gated * gated, axis=1, keepdims=True)
        normed = gated * lax.rsqrt(mean_square + EPSILON)
        out_ref[:, columns] = (normed * gain_ref[:, columns]).astype(BF16)


def state_finish(order, span, where, totals, other, entering, intra, *arrays):
    return staged_call(
        functools.partial(finish_kernel, order, span),
        (where,),
        (totals, other, entering, intra),
        arrays,
        [jax.ShapeDtypeStruct(arrays[2].shape, BF16)],
    )[0]


def routed_in_general(own, gate_up, down_proj):
    nz, nx, nt = lax.axis_size(SEQ), lax.axis_size(EXP), lax.axis_size(TP)
    x, t = lax.axis_index(EXP), lax.axis_index(TP)
    info, own = own[-16:, :256], own[:-16]
    rows, chunk = own.shape
    half = chunk // 2
    tp_bits = bits_of(nt)
    seq_stages = stages_of(SEQ, bits_of(nz))
    exp_stages = stages_of(EXP, bits_of(nx))
    far_stages, core_stages = stages_of(TP, tp_bits[:-1]), stages_of(TP, tp_bits[-1:])

    piece = spread(own, seq_stages)
    info_all = spread(info, seq_stages + exp_stages)
    left = spread(piece[..., :half], exp_stages + far_stages + core_stages)
    right = spread(piece[..., half:], far_stages + exp_stages + core_stages)
    left = left.reshape(2, nt // 2, nx, nz, rows, half)
    right = right.reshape(2, nx, nt // 2, nz, rows, half)
    info_all = info_all.reshape(nx, nz, 16, 256)

    where = jnp.stack([t, x * gate_up.shape[0]]).astype(jnp.int32)
    keep0, keep1, send0, send1 = experts_apply(
        offsets_of(tp_bits), where, info_all, left, right, jnp.swapaxes(gate_up, 1, 2), down_proj
    )

    def settle(kept, stages):
        for axis, bit in stages:
            count = kept.shape[0] // 2
            kept = kept[:count] + swap(kept[count:].astype(BF16), axis, bit).astype(F32)
        return kept

    def join(kept, sent):
        kept = kept.astype(F32) + swap(sent, *core_stages[0]).astype(F32)
        return kept.reshape(-1, rows, half)

    kept0 = settle(join(keep0, send0), far_stages[::-1] + exp_stages[::-1])
    kept1 = settle(join(keep1, send1), exp_stages[::-1] + far_stages[::-1])
    kept = settle(jnp.concatenate([kept0, kept1], axis=-1), seq_stages[::-1])
    routed_out = kept.reshape(rows, chunk).astype(BF16)
    order = [
        offsets_of(bits_of(nx)).index(i) * nz + offsets_of(bits_of(nz)).index(k)
        for k in range(nz)
        for i in range(nx)
    ]
    return routed_out, info_all.reshape(-1, 16, 256), order


def local(
    query_heads,
    key_heads,
    value_head_rows,
    state_input,
    state_gate,
    state_inflow,
    state_readout,
    step_size,
    log_decay,
    skip_scale,
    state_gain,
    hidden_in,
    mlp_gain,
    router_weight,
    expert_ids,
    slot_index,
    gate_up,
    down_proj,
):
    nz, nx, nt = lax.axis_size(SEQ), lax.axis_size(EXP), lax.axis_size(TP)
    z, x, t = lax.axis_index(SEQ), lax.axis_index(EXP), lax.axis_index(TP)
    _, width = hidden_in.shape
    chunk = width // nt
    seq_stages = stages_of(SEQ, bits_of(nz))
    exp_stages = stages_of(EXP, bits_of(nx))

    where = jnp.stack([t, x * gate_up.shape[0], z * nx + x]).astype(jnp.int32)
    own = norm_share(
        where,
        chunk,
        hidden_in,
        mlp_gain[None],
        router_weight.T,
        expert_ids.T,
        slot_index.T,
        log_decay.T,
    )
    flat = lambda a: a.reshape(-1, a.shape[2])
    heads = step_size.shape[1]
    inflow, readout = flat(state_inflow), flat(state_readout)
    intra, state, sent, kv = state_local(
        state_input,
        inflow,
        readout,
        step_size.T,
        log_decay.T,
        flat(key_heads),
        flat(value_head_rows),
    )
    finish_args = (
        intra,
        readout,
        log_decay.T,
        state_input,
        state_gate,
        jnp.repeat(skip_scale, HP)[None],
        state_gain[None],
    )

    if (nz, nx, nt) != (4, 2, 4):
        routed_out, info_all, order = routed_in_general(own, gate_up, down_proj)
        stages = seq_stages + exp_stages
        kv_own = spread(kv, stages[:-1])
        kv_parts = [a.reshape(-1, *kv.shape) for a in (kv_own, swap(kv_own, *stages[-1]))]
        far = [o * nx for o in offsets_of(bits_of(nz))]
        window_out = attention(
            query_heads, kv_parts, [i ^ o for i in offsets_of(bits_of(nx)) for o in far], where
        )
        entering, span = (), 1
        while span * 2 < nx * nz:
            other = lax.ppermute(sent, *span_route(span))
            *entering, state, sent = scan_step(
                order, span, heads, where, info_all, other, state, *entering
            )
            span *= 2
        other = lax.ppermute(sent, *span_route(span))
        state_out = state_finish(order, span, where, info_all, other, *entering, *finish_args)
        return window_out, state_out, routed_out

    return in_groups(
        where, own, kv, sent, state, query_heads, finish_args, gate_up, down_proj
    )


def in_groups(where, own, kv, sent, state, query_heads, finish_args, gate_up, down_proj):
    nz, nx = lax.axis_size(SEQ), lax.axis_size(EXP)
    heads = finish_args[2].shape[0]
    far, near, side, high, core = group_bits()
    order = [(k >> 1 << 2) | (i << 1) | (k & 1) for k in range(nz) for i in range(nx)]
    beyond = swap(own, SEQ, far)
    beside = swap(own, SEQ, near)
    here = jnp.stack([own, beside])
    kv_own = jnp.stack([kv, swap(kv, SEQ, far)])
    kv_own = jnp.stack([kv_own, swap(kv_own, SEQ, near)])
    there = jnp.stack([beyond, swap(beyond, SEQ, near)])
    pieces_a = spread_near(here)
    pieces_b = spread_near(there)
    info_all = jnp.concatenate(
        [p[0][..., -16:, :256].reshape(-1, 16, 256) for p in (pieces_a, pieces_b)], axis=0
    )
    other = lax.ppermute(sent, *span_route(1))
    *entering, state, sent = scan_step(order, 1, heads, where, info_all, other, state)
    other2 = lax.ppermute(sent, *span_route(2))
    kv_other = swap(kv_own, EXP, side)

    offsets = ((0, high), (core, core ^ high))
    keep_a, send_a, keep_b, send_b = experts_gather(
        offsets, where, pieces_a + pieces_b, gate_up, down_proj
    )

    kept_b = fold(keep_b.astype(F32), send_b, TP, core)
    kept_a = fold(keep_a.astype(F32), send_a, TP, core)
    *entering, state, sent = scan_step(order, 2, heads, where, info_all, other2, state, *entering)
    other4 = lax.ppermute(sent, *span_route(4))
    firsts, routed = [], []
    for name, kept in (("b", kept_b), ("a", kept_a)):
        left = fold(kept[0, 0], kept[0, 1], TP, high)
        right = fold(kept[1, 0], kept[1, 1], EXP, side)
        firsts.append((name, left, right))
    kv_own, kv_other = [a.reshape(-1, *kv.shape) for a in (kv_own, kv_other)]
    offsets = [n * nx ^ f * nx for n in (0, near) for f in (0, far)]
    carried = attention(query_heads, [kv_own], offsets, where, ends=False)
    window_out = attention(query_heads, [kv_other], [o ^ side for o in offsets], where, carried)
    state_out = state_finish(order, 4, where, info_all, other4, *entering, *finish_args)
    for name, left, right in firsts:
        left = fold(left[0], left[1], EXP, side)
        right = fold(right[0], right[1], TP, high)
        both = jnp.concatenate([left, right], axis=-1)
        routed.append(fold(both[0], both[1], SEQ, near))
    routed_out = fold(routed[1], routed[0], SEQ, far).astype(BF16)
    return window_out, state_out, routed_out


def solution(mesh):
    block = (SEQ, EXP)
    program = jax.shard_map(
        local,
        mesh=mesh,
        in_specs=(
            P(block, TP, None),
            P(block, TP, None),
            P(block, TP, None),
            P(block, TP),
            P(block, TP),
            P(block, TP, None),
            P(block, TP, None),
            P(block, TP),
            P(block, TP),
            P(TP),
            P(TP),
            P(block, None),
            P(),
            P(),
            P(block, None),
            P(block, None),
            P(EXP, (SEQ, TP), None, None),
            P(EXP, (SEQ, TP), None),
        ),
        out_specs=(P(block, TP, None), P(block, TP), P(block, TP)),
        check_vma=False,
    )
    if tuple(mesh.shape[a] for a in (SEQ, EXP, TP)) != (4, 2, 4):
        return program
    return program
```

```python
import functools
import math

import jax
import jax.numpy as jnp
from jax import lax
from jax.experimental import pallas as pl
from jax.experimental.pallas import tpu as pltpu
from jax.sharding import PartitionSpec as P

SEQ, EXP, TP = "seq", "exp", "tp"
WINDOW = 4096
HP = 64
NS = 128
STRETCH = 128
CAP = 40
EPSILON = 1e-05
F32 = jnp.float32
BF16 = jnp.bfloat16


def bits_of(count):
    assert count & (count - 1) == 0
    return [1 << b for b in reversed(range(count.bit_length() - 1))]


def swap(block, axis, bit):
    return lax.ppermute(block, axis, [(i, i ^ bit) for i in range(lax.axis_size(axis))])


def spread(block, stages):
    for axis, bit in stages:
        block = jnp.stack([block, swap(block, axis, bit)])
    return block


def stages_of(axis, bits):
    return [(axis, bit) for bit in bits]


def offsets_of(bits):
    offsets = [0]
    for bit in bits:
        offsets = offsets + [o ^ bit for o in offsets]
    return offsets


def staged_call(body, scalars, near, arrays, out_shape, scratch=(), vmem=20):
    count, outs = len(arrays), len(out_shape)

    def kernel(*refs):
        inside = list(refs)
        first, inside = inside[: len(scalars) + len(near)], inside[len(scalars) + len(near) :]
        sources, inside = inside[:count], inside[count:]
        results, inside = inside[:outs], inside[outs:]
        targets, inside = inside[:count], inside[count:]
        sem, extra = inside[0], inside[1:]
        copies = [
            pltpu.make_async_copy(source, target, sem.at[i])
            for i, (source, target) in enumerate(zip(sources, targets))
        ]
        for copy in copies:
            copy.start()
        for copy in copies:
            copy.wait()
        body(*first, *targets, *results, *extra)

    smem = pl.BlockSpec(memory_space=pltpu.SMEM)
    local = pl.BlockSpec(memory_space=pltpu.VMEM)
    return pl.pallas_call(
        kernel,
        out_shape=out_shape,
        in_specs=[smem] * len(scalars)
        + [local] * len(near)
        + [pl.BlockSpec(memory_space=pltpu.HBM)] * count,
        out_specs=[local] * outs,
        scratch_shapes=[pltpu.VMEM(a.shape, a.dtype) for a in arrays]
        + [pltpu.SemaphoreType.DMA((count,))]
        + list(scratch),
        compiler_params=pltpu.CompilerParams(vmem_limit_bytes=vmem * 1024 * 1024),
    )(*scalars, *near, *[pltpu.with_memory_space_constraint(a, pltpu.HBM) for a in arrays])


def attention_kernel(offsets, begins, ends, where_ref, query_ref, *refs):
    count = len(refs) - (5 if ends else 4) - (0 if begins else 3)
    kv_refs, refs = refs[:count], refs[count:]
    if not begins:
        old_top_ref, old_sum_ref, old_acc_ref, *refs = refs
    if ends:
        out_ref, *refs = refs
        score_ref, top_ref, sum_ref, acc_ref = refs
    else:
        top_ref, sum_ref, acc_ref, score_ref = refs
    total, size = query_ref.shape
    wide = kv_refs[0].shape[1] // 2
    keys = wide // 2
    heads = total // keys
    mine = where_ref[2]
    scale = math.log2(math.e) / math.sqrt(size)
    row = lax.broadcasted_iota(jnp.int32, (total, keys), 0)
    column = lax.broadcasted_iota(jnp.int32, (total, keys), 1)
    lower = lax.rem(row, heads) < heads // 2
    behind = row // heads - column
    blocks = [(kv_ref, b) for kv_ref in kv_refs for b in range(kv_ref.shape[0])]
    gaps = [(mine - (mine ^ offset)) * keys for offset in offsets]
    seen = [(gap >= 0) & (gap - (keys - 1) < WINDOW) for gap in gaps]
    top_ref[...] = jnp.full_like(top_ref, -jnp.inf) if begins else old_top_ref[...]

    def scores(at):
        kv_ref, b = blocks[at]
        score = lax.dot_general(
            query_ref[...], kv_ref[b, :wide], (((1,), (1,)), ((), ())), preferred_element_type=F32
        )
        return jnp.where(lower, score[:, :keys], score[:, keys:])

    for at, gap in enumerate(gaps):
        inside = (gap >= keys - 1) & (gap + keys - 1 < WINDOW)

        @pl.when(inside)
        def _(at=at):
            score = scores(at)
            score_ref[at] = score
            top_ref[...] = jnp.maximum(top_ref[...], score)

        @pl.when(seen[at] & jnp.logical_not(inside))
        def _(at=at, gap=gap):
            distance = behind + gap
            score = jnp.where((distance >= 0) & (distance < WINDOW), scores(at), -jnp.inf)
            score_ref[at] = score
            top_ref[...] = jnp.maximum(top_ref[...], score)

    top = jnp.max(top_ref[...], axis=1, keepdims=True)
    top_ref[...] = jnp.broadcast_to(top, (total, keys))
    if begins:
        sum_ref[...] = jnp.zeros_like(sum_ref)
        acc_ref[...] = jnp.zeros_like(acc_ref)
    else:
        shrink = jnp.exp2((old_top_ref[...] - top_ref[...]) * scale)
        sum_ref[...] = old_sum_ref[...] * shrink
        acc_ref[...] = old_acc_ref[...] * shrink

    for at, (kv_ref, b) in enumerate(blocks):

        @pl.when(seen[at])
        def _(at=at, kv_ref=kv_ref, b=b):
            weight = jnp.exp2((score_ref[at] - top_ref[...]) * scale)
            sum_ref[...] += weight
            weight = jnp.concatenate(
                [jnp.where(lower, weight, 0.0), jnp.where(lower, 0.0, weight)], axis=1
            )
            acc_ref[...] += jnp.dot(
                weight.astype(BF16), kv_ref[b, wide:], preferred_element_type=F32
            )

    if ends:
        out_ref[...] = (acc_ref[...] / jnp.sum(sum_ref[...], axis=1, keepdims=True)).astype(BF16)


def attention(query, kv_parts, offsets, where, carried=None, ends=True):
    rows, heads, size = query.shape
    assert kv_parts[0].shape[1] == 4 * rows and size == rows
    total = rows * heads
    begins = carried is None
    vmem = pl.BlockSpec(memory_space=pltpu.VMEM)
    state = [jax.ShapeDtypeStruct((total, rows), F32)] * 3
    scores = [pltpu.VMEM((len(offsets), total, rows), F32)]
    out = pl.pallas_call(
        functools.partial(attention_kernel, offsets, begins, ends),
        out_shape=jax.ShapeDtypeStruct((total, size), BF16) if ends else state,
        in_specs=[pl.BlockSpec(memory_space=pltpu.SMEM), vmem]
        + [vmem] * (len(kv_parts) + (0 if begins else 3)),
        out_specs=vmem if ends else [vmem] * 3,
        scratch_shapes=scores + [pltpu.VMEM((total, rows), F32)] * 3 if ends else scores,
        compiler_params=pltpu.CompilerParams(
            vmem_limit_bytes=(len(offsets) + 40) * total * rows * 4
        ),
    )(where, query.reshape(total, size), *kv_parts, *(carried or ()))
    return out.reshape(rows, heads, size) if ends else out


def norm_kernel(
    high,
    where_ref,
    hidden_ref,
    gain_ref,
    router_ref,
    id_ref,
    slot_ref,
    log_ref,
    own_ref,
    known_ref,
    normed_ref,
):
    rows, _ = hidden_ref.shape
    chunk = own_ref.shape[1]
    hidden = hidden_ref[...].astype(F32)
    mean_square = jnp.mean(hidden * hidden, axis=1, keepdims=True)
    normed = (hidden * lax.rsqrt(mean_square + EPSILON) * gain_ref[...]).astype(BF16)
    normed_ref[...] = normed
    start = pl.multiple_of(where_ref[0] * chunk, 128)
    own_ref[0:rows, :] = normed_ref[:, pl.ds(start, chunk)]
    known_ref[...] = normed_ref[:, pl.ds(column_of(where_ref[0], high, 1, chunk // 2), chunk // 2)]
    logits = lax.dot_general(
        router_ref[...], normed, (((1,), (1,)), ((), ())), preferred_element_type=F32
    )
    gates = 1.0 / (1.0 + jnp.exp(-logits))
    expert = lax.broadcasted_iota(jnp.int32, gates.shape, 0)
    chosen = [
        jnp.sum(jnp.where(id_ref[k : k + 1] == expert, gates, 0.0), axis=0, keepdims=True)
        for k in range(2)
    ]
    both = chosen[0] + chosen[1]
    decay = jnp.sum(log_ref[...], axis=1, keepdims=True)
    head = lax.broadcasted_iota(jnp.int32, log_ref.shape, 0)
    lane = lax.broadcasted_iota(jnp.int32, log_ref.shape, 1)
    decay = jnp.sum(jnp.where(head == lane, decay, 0.0), axis=0, keepdims=True)
    info = jnp.concatenate(
        [
            id_ref[...].astype(F32),
            slot_ref[...].astype(F32),
            chosen[0] / both,
            chosen[1] / both,
            decay,
            jnp.zeros_like(decay),
        ],
        axis=0,
    )
    parts = []
    for _ in range(3):
        part = info.astype(BF16).astype(F32)
        parts.append(part)
        info = info - part
    tail = jnp.concatenate(
        [
            jnp.concatenate([parts[0], parts[1]], axis=1),
            jnp.concatenate([parts[2], jnp.zeros_like(info)], axis=1),
        ],
        axis=0,
    )
    tail = jnp.concatenate([tail, jnp.zeros((16, chunk - 256), F32)], axis=1)
    own_ref[rows:, :] = tail.astype(BF16)


def info_of(block):
    block = block.astype(F32)
    return block[0:8, 0:128] + block[0:8, 128:256] + block[8:16, 0:128]


def norm_share(where, high, chunk, hidden, gain, router, ids, slots, log_decay):
    rows, width = hidden.shape
    assert rows == 128 and chunk >= 512
    return staged_call(
        functools.partial(norm_kernel, high),
        (where,),
        (),
        (hidden, gain, router, ids, slots, log_decay),
        [
            jax.ShapeDtypeStruct((rows + 16, chunk), BF16),
            jax.ShapeDtypeStruct((rows, chunk // 2), BF16),
        ],
        [pltpu.VMEM((rows, width), BF16)],
    )


def expert_kernel(
    offsets,
    where_ref,
    info_ref,
    left_ref,
    right_ref,
    gate_up_ref,
    down_ref,
    keep0_ref,
    keep1_ref,
    send0_ref,
    send1_ref,
    rows_ref,
    hot_ref,
    weight_ref,
):
    expert = pl.program_id(1)
    experts = pl.num_programs(1)
    me = where_ref[0]
    first = where_ref[1]
    far, _, nz, tokens, half = keep0_ref.shape
    parts = 2 * far
    local = rows_ref.shape[1]
    pairs = rows_ref.shape[0]

    def column(part, h):
        return pl.multiple_of((me ^ offsets[part]) * (2 * half) + h * half, 128)

    def pair_at(p):
        return (2 * p) // nz, (2 * p) % nz

    @pl.when(expert == 0)
    def _():
        for p in range(pairs):
            mx, mz = pair_at(p)
            info = jnp.concatenate([info_of(info_ref[mx, mz]), info_of(info_ref[mx, mz + 1])], axis=1)
            info_id = info[0:2].astype(jnp.int32)
            info_slot = info[2:4].astype(jnp.int32)
            block = lax.broadcasted_iota(jnp.int32, (1, 2 * tokens), 1) // tokens
            row = lax.broadcasted_iota(jnp.int32, (2 * CAP, 2 * tokens), 0)
            for e in range(local):
                match = []
                for k in range(2):
                    live = (info_slot[k : k + 1] >= 0) & (info_id[k : k + 1] == first + e)
                    code = jnp.where(live, block * CAP + info_slot[k : k + 1], -1)
                    match.append(row == code)
                hot_ref[p, e] = (match[0] | match[1]).astype(F32).astype(BF16)
                share = jnp.where(match[0], info[4:5], 0.0) + jnp.where(match[1], info[5:6], 0.0)
                weight_ref[p, e] = jnp.broadcast_to(
                    jnp.sum(share, axis=1, keepdims=True), (2 * CAP, 128)
                )
            hot = hot_ref[p].reshape(local * 2 * CAP, 2 * tokens)
            for part in range(parts):
                core, high = part // far, part % far
                for h in range(2):
                    if h == 0:
                        piece = left_ref[core, high, mx, mz : mz + 2]
                    else:
                        piece = right_ref[core, mx, high, mz : mz + 2]
                    piece = piece.reshape(2 * tokens, half)
                    picked = jnp.dot(hot, piece, preferred_element_type=F32).astype(BF16)
                    rows_ref[p, :, :, pl.ds(column(part, h), half)] = picked.reshape(
                        local, 2 * CAP, half
                    )

    rows = rows_ref[:, expert].reshape(pairs * 2 * CAP, rows_ref.shape[3])
    nt = (((1,), (1,)), ((), ()))
    gate = lax.dot_general(rows, gate_up_ref[0], nt, preferred_element_type=F32)
    up = lax.dot_general(rows, gate_up_ref[1], nt, preferred_element_type=F32)
    hidden = (gate / (1.0 + jnp.exp(-gate)) * up).astype(BF16)
    value = jnp.dot(hidden, down_ref[...], preferred_element_type=F32)
    for p in range(pairs):
        scaled = value[p * 2 * CAP : (p + 1) * 2 * CAP] * weight_ref[p, expert][:, :1]
        rows_ref[p, expert] = scaled.astype(BF16)

    @pl.when(expert == experts - 1)
    def _():
        for p in range(pairs):
            mx, mz = pair_at(p)
            hot = hot_ref[p].reshape(local * 2 * CAP, 2 * tokens)
            for part in range(parts):
                core, high = part // far, part % far
                for h in range(2):
                    value = rows_ref[p, :, :, pl.ds(column(part, h), half)]
                    value = value.reshape(local * 2 * CAP, half)
                    total = lax.dot_general(
                        hot, value, (((0,), (0,)), ((), ())), preferred_element_type=F32
                    )
                    total = total.astype(BF16).reshape(2, tokens, half)
                    if h == 0:
                        target = send0_ref if core else keep0_ref
                        target[high, mx, mz : mz + 2] = total
                    else:
                        target = send1_ref if core else keep1_ref
                        target[mx, high, mz : mz + 2] = total


def experts_apply(offsets, where, info, left, right, gate_up, down):
    nx, nz = info.shape[:2]
    _, far, _, _, tokens, half = left.shape
    local, _, units, width = gate_up.shape
    gx = max(1, 8 // nz)
    pairs = gx * nz // 2
    once = pl.Buffered(1)
    shape0 = jax.ShapeDtypeStruct((far, nx, nz, tokens, half), BF16)
    shape1 = jax.ShapeDtypeStruct((nx, far, nz, tokens, half), BF16)
    spec0 = pl.BlockSpec((far, gx, nz, tokens, half), lambda g, e, w: (0, g, 0, 0, 0))
    spec1 = pl.BlockSpec((gx, far, nz, tokens, half), lambda g, e, w: (g, 0, 0, 0, 0))
    return pl.pallas_call(
        functools.partial(expert_kernel, offsets),
        out_shape=[shape0, shape1, shape0, shape1],
        grid_spec=pltpu.PrefetchScalarGridSpec(
            num_scalar_prefetch=1,
            grid=(nx // gx, local),
            in_specs=[
                pl.BlockSpec((gx, nz, 16, 256), lambda g, e, w: (g, 0, 0, 0)),
                pl.BlockSpec(
                    (2, far, gx, nz, tokens, half),
                    lambda g, e, w: (0, 0, g, 0, 0, 0),
                    pipeline_mode=once,
                ),
                pl.BlockSpec(
                    (2, gx, far, nz, tokens, half),
                    lambda g, e, w: (0, g, 0, 0, 0, 0),
                    pipeline_mode=once,
                ),
                pl.BlockSpec((None, 2, units, width), lambda g, e, w: (e, 0, 0, 0)),
                pl.BlockSpec((None, units, width), lambda g, e, w: (e, 0, 0)),
            ],
            out_specs=[spec0, spec1, spec0, spec1],
            scratch_shapes=[
                pltpu.VMEM((pairs, local, 2 * CAP, width), BF16),
                pltpu.VMEM((pairs, local, 2 * CAP, 2 * tokens), BF16),
                pltpu.VMEM((pairs, local, 2 * CAP, 128), F32),
            ],
        ),
        compiler_params=pltpu.CompilerParams(vmem_limit_bytes=60 * 1024 * 1024),
        name="experts",
    )(where, info, left, right, gate_up, down)


def matches(info_ref, blocks, first, local):
    info = jnp.concatenate([info_of(info_ref[b]) for b in blocks], axis=1)
    tokens = info_ref.shape[2] // 2
    ids, slots = info[0:2].astype(jnp.int32), info[2:4].astype(jnp.int32)
    block = lax.broadcasted_iota(jnp.int32, (1, 2 * tokens), 1) // tokens
    row = lax.broadcasted_iota(jnp.int32, (2 * CAP, 2 * tokens), 0)
    for e in range(local):
        found = []
        for k in range(2):
            live = (slots[k : k + 1] >= 0) & (ids[k : k + 1] == first + e)
            found.append(row == jnp.where(live, block * CAP + slots[k : k + 1], -1))
        share = jnp.where(found[0], info[4:5], 0.0) + jnp.where(found[1], info[5:6], 0.0)
        yield (found[0] | found[1]).astype(F32).astype(BF16), jnp.sum(share, axis=1, keepdims=True)


def column_of(me, offset, h, half):
    return pl.multiple_of((me ^ offset) * (2 * half) + h * half, 128)


def combine(me, offsets, hot, value_of, keep_ref, send_ref, xo):
    tokens, half = keep_ref.shape[-2:]
    for core in range(2):
        for yi in range(2):
            for h in range(2):
                value = value_of(column_of(me, offsets[core][yi], h, half), half)
                total = lax.dot_general(
                    hot, value, (((0,), (0,)), ((), ())), preferred_element_type=F32
                )
                target = send_ref if core else keep_ref
                place = (h, yi, xo) if h == 0 else (h, xo, yi)
                target[place] = total.astype(BF16).reshape(2, tokens, half)


def paired(both):
    count, width = both.shape
    lane = lax.broadcasted_iota(jnp.int32, (count, 128), 1)
    low = lane < 64
    even = jnp.where(low, 2 * lane, 2 * lane - 128)
    take = lambda a, i: jnp.take_along_axis(a, i, axis=1, mode="promise_in_bounds")
    hidden = []
    for c in range(0, width, 256):
        one = both[:, c : c + 128]
        two = both[:, c + 128 : c + 256] if c + 128 < width else one
        gate = jnp.where(low, take(one, even), take(two, even))
        up = jnp.where(low, take(one, even + 1), take(two, even + 1))
        unit = (gate / (1.0 + jnp.exp(-gate)) * up).astype(BF16)
        hidden.append(unit[:, : (width - c) // 2] if width - c < 256 else unit)
    return jnp.concatenate(hidden, axis=1)


def gather_kernel(offsets, *refs):
    where_ref, info_ref, gate_up_ref, down_ref = refs[:4]
    pieces = refs[4:20]
    results = refs[20:24]
    all_ref, rows_ref, hot_ref, weight_ref, wide_ref, tall_ref = refs[24:30]
    piece_sem, wide_sem, tall_sem = refs[30:]
    me, first = where_ref[0], where_ref[1]
    pairs, local, places, width = rows_ref.shape
    tokens, half = all_ref.shape[2], pieces[0].shape[-1]
    units = down_ref.shape[1]
    count = pairs * places

    def fetch(e, slot):
        return (
            pltpu.make_async_copy(gate_up_ref.at[e], wide_ref.at[slot], wide_sem.at[slot]),
            pltpu.make_async_copy(down_ref.at[e], tall_ref.at[slot], tall_sem.at[slot]),
        )

    copies = []
    for p in range(pairs):
        g, xo = p // 2, p % 2
        for core in range(2):
            for yi in range(2):
                for h in range(2):
                    if h == 0:
                        source = pieces[8 * g + 2 * core + yi].at[xo]
                    else:
                        source = pieces[8 * g + 4 + 2 * core + xo].at[yi]
                    column = column_of(me, offsets[core][yi], h, half)
                    copies.append(
                        pltpu.make_async_copy(
                            source,
                            all_ref.at[p, :, :, pl.ds(column, half)],
                            piece_sem.at[len(copies)],
                        )
                    )
    for copy in copies:
        copy.start()
    for slot in range(2):
        if slot < local:
            for copy in fetch(slot, slot):
                copy.start()
    for p in range(pairs):
        for e, (hot, weight) in enumerate(matches(info_ref, (2 * p, 2 * p + 1), first, local)):
            hot_ref[p, e] = hot
            weight_ref[p, e] = jnp.broadcast_to(weight, (places, 128))
    for p in range(pairs):
        for copy in copies[8 * p : 8 * p + 8]:
            copy.wait()
        hot = hot_ref[p].reshape(local * places, 2 * tokens)
        picked = jnp.dot(
            hot, all_ref[p].reshape(2 * tokens, width), preferred_element_type=F32
        ).astype(BF16)
        rows_ref[p] = picked.reshape(local, places, width)

    def one_expert(e, _):
        slot = lax.rem(e, 2)
        for copy in fetch(e, slot):
            copy.wait()
        rows = rows_ref[:, e].reshape(count, width)
        wide = wide_ref[slot].reshape(2 * units, width)
        both = lax.dot_general(
            rows, wide, (((1,), (1,)), ((), ())), preferred_element_type=F32
        )
        value = jnp.dot(paired(both), tall_ref[slot], preferred_element_type=F32)
        for p in range(pairs):
            scaled = value[p * places : (p + 1) * places] * weight_ref[p, e][:, :1]
            rows_ref[p, e] = scaled.astype(BF16)

        @pl.when(e + 2 < local)
        def _():
            for copy in fetch(e + 2, slot):
                copy.start()

        return 0

    lax.fori_loop(0, local, one_expert, 0)
    for p in range(pairs):
        combine(
            me,
            offsets,
            hot_ref[p].reshape(local * places, 2 * tokens),
            lambda column, half: rows_ref[p, :, :, pl.ds(column, half)].reshape(
                local * places, half
            ),
            *results[p // 2 * 2 : p // 2 * 2 + 2],
            p % 2,
        )


def experts_gather(offsets, where, info, pieces, gate_up, down):
    half = pieces[0].shape[-1]
    tokens = pieces[4].shape[-2]
    local, units, _, width = gate_up.shape
    pairs, places = 4, 2 * CAP
    result = jax.ShapeDtypeStruct((2, 2, 2, 2, tokens, half), BF16)
    smem = pl.BlockSpec(memory_space=pltpu.SMEM)
    vmem = pl.BlockSpec(memory_space=pltpu.VMEM)
    hbm = pl.BlockSpec(memory_space=pl.ANY)
    return pl.pallas_call(
        functools.partial(gather_kernel, offsets),
        out_shape=[result] * 4,
        in_specs=[smem, vmem, hbm, hbm] + [hbm] * len(pieces),
        out_specs=[vmem] * 4,
        scratch_shapes=[
            pltpu.VMEM((pairs, 2, tokens, width), BF16),
            pltpu.VMEM((pairs, local, places, width), BF16),
            pltpu.VMEM((pairs, local, places, 2 * tokens), BF16),
            pltpu.VMEM((pairs, local, places, 128), F32),
            pltpu.VMEM((2, units, 2, width), BF16),
            pltpu.VMEM((2, units, width), BF16),
            pltpu.SemaphoreType.DMA((8 * pairs,)),
            pltpu.SemaphoreType.DMA((2,)),
            pltpu.SemaphoreType.DMA((2,)),
        ],
        compiler_params=pltpu.CompilerParams(vmem_limit_bytes=44 * 1024 * 1024),
        name="experts",
    )(where, info, gate_up, down, *pieces)


def group_bits():
    far, near = bits_of(lax.axis_size(SEQ))
    (side,) = bits_of(lax.axis_size(EXP))
    high, core = bits_of(lax.axis_size(TP))
    return far, near, side, high, core


def spread_near(block, known=None):
    _, _, side, high, core = group_bits()
    half = block.shape[-1] // 2
    left, right = block[..., :half], block[..., :-16, half:]
    both = [left, swap(left, EXP, side)]
    info = jnp.stack([b[..., -16:, :256] for b in both])
    left = jnp.stack([b[..., :-16, :] for b in both])
    if known is None:
        other = swap(right, TP, high)
    else:
        other = jnp.concatenate([known[None], swap(right[1:], TP, high)])
    right = jnp.stack([right, other])
    left2 = swap(left, TP, high)
    right2 = swap(right, EXP, side)
    first = [swap(left, TP, core), swap(right, TP, core)]
    second = [swap(left2, TP, core), swap(right2, TP, core)]
    return [left, left2, first[0], second[0], right, right2, first[1], second[1]], info


def fold(kept, sent, axis, bit):
    return kept + swap(sent.astype(BF16), axis, bit).astype(F32)


HIGHEST = lax.Precision.HIGHEST


def running_sum(log_ref, rows, columns):
    i = lax.broadcasted_iota(jnp.int32, (rows, rows), 0)
    j = lax.broadcasted_iota(jnp.int32, (rows, rows), 1)
    decay = log_ref[...]
    if columns:
        ones = (j <= i).astype(F32)
        return lax.dot_general(
            ones, decay, (((1,), (1,)), ((), ())), precision=HIGHEST, preferred_element_type=F32
        )
    ones = (i <= j).astype(F32)
    return jnp.dot(decay, ones, precision=HIGHEST, preferred_element_type=F32)


def group_rows(ref, g, groups):
    count = ref.shape[0]
    row = lax.broadcasted_iota(jnp.int32, (count // groups, count), 0)
    column = lax.broadcasted_iota(jnp.int32, (count // groups, count), 1)
    pick = (column == row * groups + g).astype(F32).astype(BF16)
    return jnp.dot(pick, ref[...], preferred_element_type=F32)


def state_kernel(
    input_ref,
    inflow_ref,
    readout_ref,
    step_ref,
    log_ref,
    key_ref,
    value_ref,
    intra_ref,
    state_ref,
    sent_ref,
    kv_ref,
):
    shared = key_ref.shape[0] // input_ref.shape[0]
    for n, ref in enumerate((key_ref, value_ref)):
        for h in range(shared):
            start = (n * shared + h) * input_ref.shape[0]
            kv_ref[start : start + input_ref.shape[0]] = group_rows(ref, h, shared).astype(BF16)
    rows = input_ref.shape[0]
    heads = step_ref.shape[0]
    groups = inflow_ref.shape[0] // rows
    per_group = heads // groups
    across = running_sum(log_ref, rows, False)
    down = running_sum(log_ref, rows, True)
    step = step_ref[...]
    i = lax.broadcasted_iota(jnp.int32, (rows, rows), 0)
    j = lax.broadcasted_iota(jnp.int32, (rows, rows), 1)
    causal = j <= i
    weight = jnp.transpose(jnp.exp(across[:, rows - 1 :] - across) * step)
    for g in range(groups):
        wide = group_rows(inflow_ref, g, groups)
        both = lax.dot_general(
            group_rows(readout_ref, g, groups).astype(BF16),
            wide.astype(BF16),
            (((1,), (1,)), ((), ())),
            preferred_element_type=F32,
        )
        for pair in range(0, per_group, 2):
            first = g * per_group + pair
            columns = slice(first * HP, (first + 2) * HP)
            inputs = input_ref[:, columns]
            intra, state = [], []
            for h in (first, first + 1):
                gap = jnp.where(causal, down[:, h : h + 1] - across[h : h + 1], 0.0)
                decay = jnp.where(causal, jnp.exp(gap), 0.0)
                mixing = (decay * both * step[h : h + 1]).astype(BF16)
                intra.append(jnp.dot(mixing, inputs, preferred_element_type=F32))
                weighted = (weight[:, h : h + 1] * wide).astype(BF16)
                state.append(
                    lax.dot_general(
                        weighted, inputs, (((0,), (0,)), ((), ())), preferred_element_type=F32
                    )
                )
            left = lax.broadcasted_iota(jnp.int32, (rows, 2 * HP), 1) < HP
            intra_ref[:, columns] = jnp.where(left, intra[0], intra[1])
            left = lax.broadcasted_iota(jnp.int32, (NS, 2 * HP), 1) < HP
            block = jnp.where(left, state[0], state[1])
            state_ref[:, columns] = block
            sent_ref[:, columns] = block.astype(BF16)


def state_local(inputs, inflow, readout, step, log_decay, keys, values):
    rows, channels = inputs.shape
    assert rows == STRETCH
    return staged_call(
        state_kernel,
        (),
        (),
        (inputs, inflow, readout, step, log_decay, keys, values),
        [
            jax.ShapeDtypeStruct((rows, channels), F32),
            jax.ShapeDtypeStruct((NS, channels), F32),
            jax.ShapeDtypeStruct((NS, channels), BF16),
            jax.ShapeDtypeStruct((2 * keys.shape[0], keys.shape[1]), BF16),
        ],
    )


def lanes_of(factors, heads):
    left = lax.broadcasted_iota(jnp.int32, (1, 2 * HP), 1) < HP
    return jnp.concatenate(
        [
            jnp.where(left, factors[:, h : h + 1], factors[:, h + 1 : h + 2])
            for h in range(0, heads, 2)
        ],
        axis=1,
    )


def decay_between(place, total_ref, order, span, heads):
    row = lambda m: info_of(total_ref[order[m]])[6:7]
    upper = (place & span) != 0
    lead = own = jnp.zeros_like(row(0))
    theirs = jnp.zeros_like(own)
    for m in range(span):
        lead = lead + jnp.where((place ^ m) < place, row(m), 0.0)
        own = own + row(m)
        theirs = theirs + row(span + m)
    lead, own, theirs = jnp.exp(lead), jnp.exp(own), jnp.exp(theirs)
    return (
        lanes_of(jnp.where(upper, lead, 0.0), heads),
        lanes_of(jnp.where(upper, own, 1.0), heads),
        lanes_of(jnp.where(upper, 1.0, theirs), heads),
    )


def scan_kernel(order, span, heads, where_ref, total_ref, other_ref, state_ref, *refs):
    entering_ref = refs[0] if len(refs) == 4 else None
    new_entering_ref, new_state_ref, sent_ref = refs[-3:]
    lead, own, theirs = decay_between(where_ref[2], total_ref, order, span, heads)
    other = other_ref[...].astype(F32)
    entering = lead * other
    if entering_ref is not None:
        entering = entering + entering_ref[...]
    new_entering_ref[...] = entering
    state = own * other + theirs * state_ref[...]
    new_state_ref[...] = state
    sent_ref[...] = state.astype(BF16)


def scan_step(order, span, heads, where, totals, other, state, *entering):
    vmem = pl.BlockSpec(memory_space=pltpu.VMEM)
    smem = pl.BlockSpec(memory_space=pltpu.SMEM)
    like = jax.ShapeDtypeStruct(state.shape, F32)
    return pl.pallas_call(
        functools.partial(scan_kernel, order, span, heads),
        out_shape=[like, like, jax.ShapeDtypeStruct(state.shape, BF16)],
        in_specs=[smem] + [vmem] * (3 + len(entering)),
        out_specs=[vmem] * 3,
        compiler_params=pltpu.CompilerParams(vmem_limit_bytes=20 * 1024 * 1024),
    )(where, totals, other, state, *entering)


def span_route(span):
    nx, nz = lax.axis_size(EXP), lax.axis_size(SEQ)
    axis, bit = (EXP, span) if span < nx else (SEQ, span // nx)
    both = span * 2 < nx * nz
    pairs = [(i, i ^ bit) for i in range(lax.axis_size(axis)) if both or not i & bit]
    return axis, pairs


def finish_kernel(
    order, span, where_ref, total_ref, other_ref, entering_ref, intra_ref, readout_ref, log_ref, input_ref, gate_ref, skip_ref, gain_ref, out_ref
):
    rows, channels = input_ref.shape
    heads = log_ref.shape[0]
    groups = readout_ref.shape[0] // rows
    width = channels // groups
    grown = jnp.exp(running_sum(log_ref, rows, True))
    lead, _, _ = decay_between(where_ref[2], total_ref, order, span, heads)
    left = lax.broadcasted_iota(jnp.int32, (rows, 2 * HP), 1) < HP
    for g in range(groups):
        columns = slice(g * width, (g + 1) * width)
        inter = jnp.dot(
            group_rows(readout_ref, g, groups),
            lead[:, columns] * other_ref[:, columns].astype(F32) + entering_ref[:, columns],
            precision=HIGHEST,
            preferred_element_type=F32,
        )
        first = g * (heads // groups)
        factor = jnp.concatenate(
            [
                jnp.where(left, grown[:, h : h + 1], grown[:, h + 1 : h + 2])
                for h in range(first, first + heads // groups, 2)
            ],
            axis=1,
        )
        mixed = (
            intra_ref[:, columns]
            + factor * inter
            + skip_ref[:, columns] * input_ref[:, columns].astype(F32)
        )
        gate = gate_ref[:, columns].astype(F32)
        gated = mixed * (gate / (1.0 + jnp.exp(-gate)))
        mean_square = jnp.mean(gated * gated, axis=1, keepdims=True)
        normed = gated * lax.rsqrt(mean_square + EPSILON)
        out_ref[:, columns] = (normed * gain_ref[:, columns]).astype(BF16)


def state_finish(order, span, where, totals, other, entering, intra, *arrays):
    return staged_call(
        functools.partial(finish_kernel, order, span),
        (where,),
        (totals, other, entering, intra),
        arrays,
        [jax.ShapeDtypeStruct(arrays[2].shape, BF16)],
    )[0]


def routed_in_general(own, gate_up, down_proj):
    nz, nx, nt = lax.axis_size(SEQ), lax.axis_size(EXP), lax.axis_size(TP)
    x, t = lax.axis_index(EXP), lax.axis_index(TP)
    info, own = own[-16:, :256], own[:-16]
    rows, chunk = own.shape
    half = chunk // 2
    tp_bits = bits_of(nt)
    seq_stages = stages_of(SEQ, bits_of(nz))
    exp_stages = stages_of(EXP, bits_of(nx))
    far_stages, core_stages = stages_of(TP, tp_bits[:-1]), stages_of(TP, tp_bits[-1:])

    piece = spread(own, seq_stages)
    info_all = spread(info, seq_stages + exp_stages)
    left = spread(piece[..., :half], exp_stages + far_stages + core_stages)
    right = spread(piece[..., half:], far_stages + exp_stages + core_stages)
    left = left.reshape(2, nt // 2, nx, nz, rows, half)
    right = right.reshape(2, nx, nt // 2, nz, rows, half)
    info_all = info_all.reshape(nx, nz, 16, 256)

    where = jnp.stack([t, x * gate_up.shape[0]]).astype(jnp.int32)
    keep0, keep1, send0, send1 = experts_apply(
        offsets_of(tp_bits), where, info_all, left, right, jnp.swapaxes(gate_up, 1, 2), down_proj
    )

    def settle(kept, stages):
        for axis, bit in stages:
            count = kept.shape[0] // 2
            kept = kept[:count] + swap(kept[count:].astype(BF16), axis, bit).astype(F32)
        return kept

    def join(kept, sent):
        kept = kept.astype(F32) + swap(sent, *core_stages[0]).astype(F32)
        return kept.reshape(-1, rows, half)

    kept0 = settle(join(keep0, send0), far_stages[::-1] + exp_stages[::-1])
    kept1 = settle(join(keep1, send1), exp_stages[::-1] + far_stages[::-1])
    kept = settle(jnp.concatenate([kept0, kept1], axis=-1), seq_stages[::-1])
    routed_out = kept.reshape(rows, chunk).astype(BF16)
    order = [
        offsets_of(bits_of(nx)).index(i) * nz + offsets_of(bits_of(nz)).index(k)
        for k in range(nz)
        for i in range(nx)
    ]
    return routed_out, info_all.reshape(-1, 16, 256), order


def local(
    query_heads,
    key_heads,
    value_head_rows,
    state_input,
    state_gate,
    state_inflow,
    state_readout,
    step_size,
    log_decay,
    skip_scale,
    state_gain,
    hidden_in,
    mlp_gain,
    router_weight,
    expert_ids,
    slot_index,
    gate_up,
    down_proj,
):
    nz, nx, nt = lax.axis_size(SEQ), lax.axis_size(EXP), lax.axis_size(TP)
    z, x, t = lax.axis_index(SEQ), lax.axis_index(EXP), lax.axis_index(TP)
    _, width = hidden_in.shape
    chunk = width // nt
    seq_stages = stages_of(SEQ, bits_of(nz))
    exp_stages = stages_of(EXP, bits_of(nx))

    where = jnp.stack([t, x * gate_up.shape[0], z * nx + x]).astype(jnp.int32)
    own, known = norm_share(
        where,
        bits_of(nt)[0],
        chunk,
        hidden_in,
        mlp_gain[None],
        router_weight.T,
        expert_ids.T,
        slot_index.T,
        log_decay.T,
    )
    flat = lambda a: a.reshape(-1, a.shape[2])
    heads = step_size.shape[1]
    inflow, readout = flat(state_inflow), flat(state_readout)
    intra, state, sent, kv = state_local(
        state_input,
        inflow,
        readout,
        step_size.T,
        log_decay.T,
        flat(key_heads),
        flat(value_head_rows),
    )
    finish_args = (
        intra,
        readout,
        log_decay.T,
        state_input,
        state_gate,
        jnp.repeat(skip_scale, HP)[None],
        state_gain[None],
    )

    if (nz, nx, nt) != (4, 2, 4):
        routed_out, info_all, order = routed_in_general(own, gate_up, down_proj)
        stages = seq_stages + exp_stages
        kv_own = spread(kv, stages[:-1])
        kv_parts = [a.reshape(-1, *kv.shape) for a in (kv_own, swap(kv_own, *stages[-1]))]
        far = [o * nx for o in offsets_of(bits_of(nz))]
        window_out = attention(
            query_heads, kv_parts, [i ^ o for i in offsets_of(bits_of(nx)) for o in far], where
        )
        entering, span = (), 1
        while span * 2 < nx * nz:
            other = lax.ppermute(sent, *span_route(span))
            *entering, state, sent = scan_step(
                order, span, heads, where, info_all, other, state, *entering
            )
            span *= 2
        other = lax.ppermute(sent, *span_route(span))
        state_out = state_finish(order, span, where, info_all, other, *entering, *finish_args)
        return window_out, state_out, routed_out

    return in_groups(
        where, own, known, kv, sent, state, query_heads, finish_args, gate_up, down_proj
    )


def in_groups(where, own, known, kv, sent, state, query_heads, finish_args, gate_up, down_proj):
    nz, nx = lax.axis_size(SEQ), lax.axis_size(EXP)
    heads = finish_args[2].shape[0]
    far, near, side, high, core = group_bits()
    order = [(k >> 1 << 2) | (i << 1) | (k & 1) for k in range(nz) for i in range(nx)]
    beyond = swap(own, SEQ, far)
    beside = swap(own, SEQ, near)
    here = jnp.stack([own, beside])
    kv_own = jnp.stack([kv, swap(kv, SEQ, far)])
    kv_own = jnp.stack([kv_own, swap(kv_own, SEQ, near)])
    there = jnp.stack([beyond, swap(beyond, SEQ, near)])
    pieces_a, info_a = spread_near(here, known)
    pieces_b, info_b = spread_near(there)
    info_all = jnp.stack([info_a, info_b]).reshape(-1, 16, 256)
    other = lax.ppermute(sent, *span_route(1))
    *entering, state, sent = scan_step(order, 1, heads, where, info_all, other, state)
    other2 = lax.ppermute(sent, *span_route(2))
    kv_other = swap(kv_own, EXP, side)

    offsets = ((0, high), (core, core ^ high))
    keep_a, send_a, keep_b, send_b = experts_gather(
        offsets, where, info_all, pieces_a + pieces_b, gate_up, down_proj
    )

    kept_b = fold(keep_b.astype(F32), send_b, TP, core)
    kept_a = fold(keep_a.astype(F32), send_a, TP, core)
    *entering, state, sent = scan_step(order, 2, heads, where, info_all, other2, state, *entering)
    other4 = lax.ppermute(sent, *span_route(4))
    firsts, routed = [], []
    for name, kept in (("b", kept_b), ("a", kept_a)):
        left = fold(kept[0, 0], kept[0, 1], TP, high)
        right = fold(kept[1, 0], kept[1, 1], EXP, side)
        firsts.append((name, left, right))
    kv_own, kv_other = [a.reshape(-1, *kv.shape) for a in (kv_own, kv_other)]
    offsets = [n * nx ^ f * nx for n in (0, near) for f in (0, far)]
    carried = attention(query_heads, [kv_own], offsets, where, ends=False)
    window_out = attention(query_heads, [kv_other], [o ^ side for o in offsets], where, carried)
    state_out = state_finish(order, 4, where, info_all, other4, *entering, *finish_args)
    for name, left, right in firsts:
        left = fold(left[0], left[1], EXP, side)
        right = fold(right[0], right[1], TP, high)
        both = jnp.concatenate([left, right], axis=-1)
        routed.append(fold(both[0], both[1], SEQ, near))
    routed_out = fold(routed[1], routed[0], SEQ, far).astype(BF16)
    return window_out, state_out, routed_out


def solution(mesh):
    block = (SEQ, EXP)
    program = jax.shard_map(
        local,
        mesh=mesh,
        in_specs=(
            P(block, TP, None),
            P(block, TP, None),
            P(block, TP, None),
            P(block, TP),
            P(block, TP),
            P(block, TP, None),
            P(block, TP, None),
            P(block, TP),
            P(block, TP),
            P(TP),
            P(TP),
            P(block, None),
            P(),
            P(),
            P(block, None),
            P(block, None),
            P(EXP, (SEQ, TP), None, None),
            P(EXP, (SEQ, TP), None),
        ),
        out_specs=(P(block, TP, None), P(block, TP), P(block, TP)),
        check_vma=False,
    )
    if tuple(mesh.shape[a] for a in (SEQ, EXP, TP)) != (4, 2, 4):
        return program
    return program
```

```python
import functools
import math

import jax
import jax.numpy as jnp
from jax import lax
from jax.experimental import pallas as pl
from jax.experimental.pallas import tpu as pltpu
from jax.sharding import PartitionSpec as P

SEQ, EXP, TP = "seq", "exp", "tp"
WINDOW = 4096
HP = 64
NS = 128
STRETCH = 128
CAP = 40
EPSILON = 1e-05
F32 = jnp.float32
BF16 = jnp.bfloat16


def bits_of(count):
    assert count & (count - 1) == 0
    return [1 << b for b in reversed(range(count.bit_length() - 1))]


def swap(block, axis, bit):
    return lax.ppermute(block, axis, [(i, i ^ bit) for i in range(lax.axis_size(axis))])


def spread(block, stages):
    for axis, bit in stages:
        block = jnp.stack([block, swap(block, axis, bit)])
    return block


def stages_of(axis, bits):
    return [(axis, bit) for bit in bits]


def offsets_of(bits):
    offsets = [0]
    for bit in bits:
        offsets = offsets + [o ^ bit for o in offsets]
    return offsets


def staged_call(body, scalars, near, arrays, out_shape, scratch=(), vmem=20):
    count, outs = len(arrays), len(out_shape)

    def kernel(*refs):
        inside = list(refs)
        first, inside = inside[: len(scalars) + len(near)], inside[len(scalars) + len(near) :]
        sources, inside = inside[:count], inside[count:]
        results, inside = inside[:outs], inside[outs:]
        targets, inside = inside[:count], inside[count:]
        sem, extra = inside[0], inside[1:]
        copies = [
            pltpu.make_async_copy(source, target, sem.at[i])
            for i, (source, target) in enumerate(zip(sources, targets))
        ]
        for copy in copies:
            copy.start()
        for copy in copies:
            copy.wait()
        body(*first, *targets, *results, *extra)

    smem = pl.BlockSpec(memory_space=pltpu.SMEM)
    local = pl.BlockSpec(memory_space=pltpu.VMEM)
    return pl.pallas_call(
        kernel,
        out_shape=out_shape,
        in_specs=[smem] * len(scalars)
        + [local] * len(near)
        + [pl.BlockSpec(memory_space=pltpu.HBM)] * count,
        out_specs=[local] * outs,
        scratch_shapes=[pltpu.VMEM(a.shape, a.dtype) for a in arrays]
        + [pltpu.SemaphoreType.DMA((count,))]
        + list(scratch),
        compiler_params=pltpu.CompilerParams(vmem_limit_bytes=vmem * 1024 * 1024),
    )(*scalars, *near, *[pltpu.with_memory_space_constraint(a, pltpu.HBM) for a in arrays])


def attention_kernel(offsets, begins, ends, where_ref, query_ref, *refs):
    count = len(refs) - (5 if ends else 4) - (0 if begins else 3)
    kv_refs, refs = refs[:count], refs[count:]
    if not begins:
        old_top_ref, old_sum_ref, old_acc_ref, *refs = refs
    if ends:
        out_ref, *refs = refs
        score_ref, top_ref, sum_ref, acc_ref = refs
    else:
        top_ref, sum_ref, acc_ref, score_ref = refs
    total, size = query_ref.shape
    wide = kv_refs[0].shape[1] // 2
    keys = wide // 2
    heads = total // keys
    mine = where_ref[2]
    scale = math.log2(math.e) / math.sqrt(size)
    row = lax.broadcasted_iota(jnp.int32, (total, keys), 0)
    column = lax.broadcasted_iota(jnp.int32, (total, keys), 1)
    lower = lax.rem(row, heads) < heads // 2
    behind = row // heads - column
    blocks = [(kv_ref, b) for kv_ref in kv_refs for b in range(kv_ref.shape[0])]
    gaps = [(mine - (mine ^ offset)) * keys for offset in offsets]
    seen = [(gap >= 0) & (gap - (keys - 1) < WINDOW) for gap in gaps]
    top_ref[...] = jnp.full_like(top_ref, -jnp.inf) if begins else old_top_ref[...]

    def scores(at):
        kv_ref, b = blocks[at]
        score = lax.dot_general(
            query_ref[...], kv_ref[b, :wide], (((1,), (1,)), ((), ())), preferred_element_type=F32
        )
        return jnp.where(lower, score[:, :keys], score[:, keys:])

    for at, gap in enumerate(gaps):
        inside = (gap >= keys - 1) & (gap + keys - 1 < WINDOW)

        @pl.when(inside)
        def _(at=at):
            score = scores(at)
            score_ref[at] = score
            top_ref[...] = jnp.maximum(top_ref[...], score)

        @pl.when(seen[at] & jnp.logical_not(inside))
        def _(at=at, gap=gap):
            distance = behind + gap
            score = jnp.where((distance >= 0) & (distance < WINDOW), scores(at), -jnp.inf)
            score_ref[at] = score
            top_ref[...] = jnp.maximum(top_ref[...], score)

    top = jnp.max(top_ref[...], axis=1, keepdims=True)
    top_ref[...] = jnp.broadcast_to(top, (total, keys))
    if begins:
        sum_ref[...] = jnp.zeros_like(sum_ref)
        acc_ref[...] = jnp.zeros_like(acc_ref)
    else:
        shrink = jnp.exp2((old_top_ref[...] - top_ref[...]) * scale)
        sum_ref[...] = old_sum_ref[...] * shrink
        acc_ref[...] = old_acc_ref[...] * shrink

    for at, (kv_ref, b) in enumerate(blocks):

        @pl.when(seen[at])
        def _(at=at, kv_ref=kv_ref, b=b):
            weight = jnp.exp2((score_ref[at] - top_ref[...]) * scale)
            sum_ref[...] += weight
            weight = jnp.concatenate(
                [jnp.where(lower, weight, 0.0), jnp.where(lower, 0.0, weight)], axis=1
            )
            acc_ref[...] += jnp.dot(
                weight.astype(BF16), kv_ref[b, wide:], preferred_element_type=F32
            )

    if ends:
        out_ref[...] = (acc_ref[...] / jnp.sum(sum_ref[...], axis=1, keepdims=True)).astype(BF16)


def attention(query, kv_parts, offsets, where, carried=None, ends=True):
    rows, heads, size = query.shape
    assert kv_parts[0].shape[1] == 4 * rows and size == rows
    total = rows * heads
    begins = carried is None
    vmem = pl.BlockSpec(memory_space=pltpu.VMEM)
    state = [jax.ShapeDtypeStruct((total, rows), F32)] * 3
    scores = [pltpu.VMEM((len(offsets), total, rows), F32)]
    out = pl.pallas_call(
        functools.partial(attention_kernel, offsets, begins, ends),
        out_shape=jax.ShapeDtypeStruct((total, size), BF16) if ends else state,
        in_specs=[pl.BlockSpec(memory_space=pltpu.SMEM), vmem]
        + [vmem] * (len(kv_parts) + (0 if begins else 3)),
        out_specs=vmem if ends else [vmem] * 3,
        scratch_shapes=scores + [pltpu.VMEM((total, rows), F32)] * 3 if ends else scores,
        compiler_params=pltpu.CompilerParams(
            vmem_limit_bytes=(len(offsets) + 40) * total * rows * 4
        ),
    )(where, query.reshape(total, size), *kv_parts, *(carried or ()))
    return out.reshape(rows, heads, size) if ends else out


def norm_kernel(
    high,
    where_ref,
    hidden_ref,
    gain_ref,
    router_ref,
    id_ref,
    slot_ref,
    log_ref,
    own_ref,
    known_ref,
    normed_ref,
):
    rows, _ = hidden_ref.shape
    chunk = own_ref.shape[1]
    hidden = hidden_ref[...].astype(F32)
    mean_square = jnp.mean(hidden * hidden, axis=1, keepdims=True)
    normed = (hidden * lax.rsqrt(mean_square + EPSILON) * gain_ref[...]).astype(BF16)
    normed_ref[...] = normed
    start = pl.multiple_of(where_ref[0] * chunk, 128)
    own_ref[0:rows, :] = normed_ref[:, pl.ds(start, chunk)]
    known_ref[...] = normed_ref[:, pl.ds(column_of(where_ref[0], high, 1, chunk // 2), chunk // 2)]
    logits = lax.dot_general(
        router_ref[...], normed, (((1,), (1,)), ((), ())), preferred_element_type=F32
    )
    gates = 1.0 / (1.0 + jnp.exp(-logits))
    expert = lax.broadcasted_iota(jnp.int32, gates.shape, 0)
    chosen = [
        jnp.sum(jnp.where(id_ref[k : k + 1] == expert, gates, 0.0), axis=0, keepdims=True)
        for k in range(2)
    ]
    both = chosen[0] + chosen[1]
    decay = jnp.sum(log_ref[...], axis=1, keepdims=True)
    head = lax.broadcasted_iota(jnp.int32, log_ref.shape, 0)
    lane = lax.broadcasted_iota(jnp.int32, log_ref.shape, 1)
    decay = jnp.sum(jnp.where(head == lane, decay, 0.0), axis=0, keepdims=True)
    info = jnp.concatenate(
        [
            id_ref[...].astype(F32),
            slot_ref[...].astype(F32),
            chosen[0] / both,
            chosen[1] / both,
            decay,
            jnp.zeros_like(decay),
        ],
        axis=0,
    )
    parts = []
    for _ in range(3):
        part = info.astype(BF16).astype(F32)
        parts.append(part)
        info = info - part
    tail = jnp.concatenate(
        [
            jnp.concatenate([parts[0], parts[1]], axis=1),
            jnp.concatenate([parts[2], jnp.zeros_like(info)], axis=1),
        ],
        axis=0,
    )
    tail = jnp.concatenate([tail, jnp.zeros((16, chunk - 256), F32)], axis=1)
    own_ref[rows:, :] = tail.astype(BF16)


def info_of(block):
    block = block.astype(F32)
    return block[0:8, 0:128] + block[0:8, 128:256] + block[8:16, 0:128]


def norm_share(where, high, chunk, hidden, gain, router, ids, slots, log_decay):
    rows, width = hidden.shape
    assert rows == 128 and chunk >= 512
    return staged_call(
        functools.partial(norm_kernel, high),
        (where,),
        (),
        (hidden, gain, router, ids, slots, log_decay),
        [
            jax.ShapeDtypeStruct((rows + 16, chunk), BF16),
            jax.ShapeDtypeStruct((rows, chunk // 2), BF16),
        ],
        [pltpu.VMEM((rows, width), BF16)],
    )


def expert_kernel(
    offsets,
    where_ref,
    info_ref,
    left_ref,
    right_ref,
    gate_up_ref,
    down_ref,
    keep0_ref,
    keep1_ref,
    send0_ref,
    send1_ref,
    rows_ref,
    hot_ref,
    weight_ref,
):
    expert = pl.program_id(1)
    experts = pl.num_programs(1)
    me = where_ref[0]
    first = where_ref[1]
    far, _, nz, tokens, half = keep0_ref.shape
    parts = 2 * far
    local = rows_ref.shape[1]
    pairs = rows_ref.shape[0]

    def column(part, h):
        return pl.multiple_of((me ^ offsets[part]) * (2 * half) + h * half, 128)

    def pair_at(p):
        return (2 * p) // nz, (2 * p) % nz

    @pl.when(expert == 0)
    def _():
        for p in range(pairs):
            mx, mz = pair_at(p)
            info = jnp.concatenate([info_of(info_ref[mx, mz]), info_of(info_ref[mx, mz + 1])], axis=1)
            info_id = info[0:2].astype(jnp.int32)
            info_slot = info[2:4].astype(jnp.int32)
            block = lax.broadcasted_iota(jnp.int32, (1, 2 * tokens), 1) // tokens
            row = lax.broadcasted_iota(jnp.int32, (2 * CAP, 2 * tokens), 0)
            for e in range(local):
                match = []
                for k in range(2):
                    live = (info_slot[k : k + 1] >= 0) & (info_id[k : k + 1] == first + e)
                    code = jnp.where(live, block * CAP + info_slot[k : k + 1], -1)
                    match.append(row == code)
                hot_ref[p, e] = (match[0] | match[1]).astype(F32).astype(BF16)
                share = jnp.where(match[0], info[4:5], 0.0) + jnp.where(match[1], info[5:6], 0.0)
                weight_ref[p, e] = jnp.broadcast_to(
                    jnp.sum(share, axis=1, keepdims=True), (2 * CAP, 128)
                )
            hot = hot_ref[p].reshape(local * 2 * CAP, 2 * tokens)
            for part in range(parts):
                core, high = part // far, part % far
                for h in range(2):
                    if h == 0:
                        piece = left_ref[core, high, mx, mz : mz + 2]
                    else:
                        piece = right_ref[core, mx, high, mz : mz + 2]
                    piece = piece.reshape(2 * tokens, half)
                    picked = jnp.dot(hot, piece, preferred_element_type=F32).astype(BF16)
                    rows_ref[p, :, :, pl.ds(column(part, h), half)] = picked.reshape(
                        local, 2 * CAP, half
                    )

    rows = rows_ref[:, expert].reshape(pairs * 2 * CAP, rows_ref.shape[3])
    nt = (((1,), (1,)), ((), ()))
    gate = lax.dot_general(rows, gate_up_ref[0], nt, preferred_element_type=F32)
    up = lax.dot_general(rows, gate_up_ref[1], nt, preferred_element_type=F32)
    hidden = (gate / (1.0 + jnp.exp(-gate)) * up).astype(BF16)
    value = jnp.dot(hidden, down_ref[...], preferred_element_type=F32)
    for p in range(pairs):
        scaled = value[p * 2 * CAP : (p + 1) * 2 * CAP] * weight_ref[p, expert][:, :1]
        rows_ref[p, expert] = scaled.astype(BF16)

    @pl.when(expert == experts - 1)
    def _():
        for p in range(pairs):
            mx, mz = pair_at(p)
            hot = hot_ref[p].reshape(local * 2 * CAP, 2 * tokens)
            for part in range(parts):
                core, high = part // far, part % far
                for h in range(2):
                    value = rows_ref[p, :, :, pl.ds(column(part, h), half)]
                    value = value.reshape(local * 2 * CAP, half)
                    total = lax.dot_general(
                        hot, value, (((0,), (0,)), ((), ())), preferred_element_type=F32
                    )
                    total = total.astype(BF16).reshape(2, tokens, half)
                    if h == 0:
                        target = send0_ref if core else keep0_ref
                        target[high, mx, mz : mz + 2] = total
                    else:
                        target = send1_ref if core else keep1_ref
                        target[mx, high, mz : mz + 2] = total


def experts_apply(offsets, where, info, left, right, gate_up, down):
    nx, nz = info.shape[:2]
    _, far, _, _, tokens, half = left.shape
    local, _, units, width = gate_up.shape
    gx = max(1, 8 // nz)
    pairs = gx * nz // 2
    once = pl.Buffered(1)
    shape0 = jax.ShapeDtypeStruct((far, nx, nz, tokens, half), BF16)
    shape1 = jax.ShapeDtypeStruct((nx, far, nz, tokens, half), BF16)
    spec0 = pl.BlockSpec((far, gx, nz, tokens, half), lambda g, e, w: (0, g, 0, 0, 0))
    spec1 = pl.BlockSpec((gx, far, nz, tokens, half), lambda g, e, w: (g, 0, 0, 0, 0))
    return pl.pallas_call(
        functools.partial(expert_kernel, offsets),
        out_shape=[shape0, shape1, shape0, shape1],
        grid_spec=pltpu.PrefetchScalarGridSpec(
            num_scalar_prefetch=1,
            grid=(nx // gx, local),
            in_specs=[
                pl.BlockSpec((gx, nz, 16, 256), lambda g, e, w: (g, 0, 0, 0)),
                pl.BlockSpec(
                    (2, far, gx, nz, tokens, half),
                    lambda g, e, w: (0, 0, g, 0, 0, 0),
                    pipeline_mode=once,
                ),
                pl.BlockSpec(
                    (2, gx, far, nz, tokens, half),
                    lambda g, e, w: (0, g, 0, 0, 0, 0),
                    pipeline_mode=once,
                ),
                pl.BlockSpec((None, 2, units, width), lambda g, e, w: (e, 0, 0, 0)),
                pl.BlockSpec((None, units, width), lambda g, e, w: (e, 0, 0)),
            ],
            out_specs=[spec0, spec1, spec0, spec1],
            scratch_shapes=[
                pltpu.VMEM((pairs, local, 2 * CAP, width), BF16),
                pltpu.VMEM((pairs, local, 2 * CAP, 2 * tokens), BF16),
                pltpu.VMEM((pairs, local, 2 * CAP, 128), F32),
            ],
        ),
        compiler_params=pltpu.CompilerParams(vmem_limit_bytes=60 * 1024 * 1024),
        name="experts",
    )(where, info, left, right, gate_up, down)


def matches(info_ref, blocks, first, local):
    info = jnp.concatenate([info_of(info_ref[b]) for b in blocks], axis=1)
    tokens = info_ref.shape[2] // 2
    ids, slots = info[0:2].astype(jnp.int32), info[2:4].astype(jnp.int32)
    block = lax.broadcasted_iota(jnp.int32, (1, 2 * tokens), 1) // tokens
    row = lax.broadcasted_iota(jnp.int32, (2 * CAP, 2 * tokens), 0)
    for e in range(local):
        found = []
        for k in range(2):
            live = (slots[k : k + 1] >= 0) & (ids[k : k + 1] == first + e)
            found.append(row == jnp.where(live, block * CAP + slots[k : k + 1], -1))
        share = jnp.where(found[0], info[4:5], 0.0) + jnp.where(found[1], info[5:6], 0.0)
        yield (found[0] | found[1]).astype(F32).astype(BF16), jnp.sum(share, axis=1, keepdims=True)


def column_of(me, offset, h, half):
    return pl.multiple_of((me ^ offset) * (2 * half) + h * half, 128)


def combine(me, offsets, hot, value_of, keep_ref, send_ref, xo):
    tokens, half = keep_ref.shape[-2:]
    for core in range(2):
        for yi in range(2):
            for h in range(2):
                value = value_of(column_of(me, offsets[core][yi], h, half), half)
                total = lax.dot_general(
                    hot, value, (((0,), (0,)), ((), ())), preferred_element_type=F32
                )
                target = send_ref if core else keep_ref
                place = (h, yi, xo) if h == 0 else (h, xo, yi)
                target[place] = total.astype(BF16).reshape(2, tokens, half)


def paired(both):
    count, width = both.shape
    lane = lax.broadcasted_iota(jnp.int32, (count, 128), 1)
    low = lane < 64
    even = jnp.where(low, 2 * lane, 2 * lane - 128)
    take = lambda a, i: jnp.take_along_axis(a, i, axis=1, mode="promise_in_bounds")
    hidden = []
    for c in range(0, width, 256):
        one = both[:, c : c + 128]
        two = both[:, c + 128 : c + 256] if c + 128 < width else one
        gate = jnp.where(low, take(one, even), take(two, even))
        up = jnp.where(low, take(one, even + 1), take(two, even + 1))
        unit = (gate / (1.0 + jnp.exp(-gate)) * up).astype(BF16)
        hidden.append(unit[:, : (width - c) // 2] if width - c < 256 else unit)
    return jnp.concatenate(hidden, axis=1)


def gather_kernel(offsets, *refs):
    where_ref, info_ref, gate_up_ref, down_ref = refs[:4]
    pieces = refs[4:20]
    results = refs[20:24]
    all_ref, rows_ref, hot_ref, weight_ref, wide_ref, tall_ref = refs[24:30]
    piece_sem, wide_sem, tall_sem = refs[30:]
    me, first = where_ref[0], where_ref[1]
    pairs, local, places, width = rows_ref.shape
    tokens, half = all_ref.shape[2], pieces[0].shape[-1]
    units = down_ref.shape[1]
    count = pairs * places

    def fetch(e, slot):
        return (
            pltpu.make_async_copy(gate_up_ref.at[e], wide_ref.at[slot], wide_sem.at[slot]),
            pltpu.make_async_copy(down_ref.at[e], tall_ref.at[slot], tall_sem.at[slot]),
        )

    copies = []
    for p in range(pairs):
        g, xo = p // 2, p % 2
        for core in range(2):
            for yi in range(2):
                for h in range(2):
                    if h == 0:
                        source = pieces[8 * g + 2 * core + yi].at[xo]
                    else:
                        source = pieces[8 * g + 4 + 2 * core + xo].at[yi]
                    column = column_of(me, offsets[core][yi], h, half)
                    copies.append(
                        pltpu.make_async_copy(
                            source,
                            all_ref.at[p, :, :, pl.ds(column, half)],
                            piece_sem.at[len(copies)],
                        )
                    )
    for copy in copies:
        copy.start()
    for slot in range(2):
        if slot < local:
            for copy in fetch(slot, slot):
                copy.start()
    for p in range(pairs):
        for e, (hot, weight) in enumerate(matches(info_ref, (2 * p, 2 * p + 1), first, local)):
            hot_ref[p, e] = hot
            weight_ref[p, e] = jnp.broadcast_to(weight, (places, 128))
    for p in range(pairs):
        for copy in copies[8 * p : 8 * p + 8]:
            copy.wait()
        hot = hot_ref[p].reshape(local * places, 2 * tokens)
        picked = jnp.dot(
            hot, all_ref[p].reshape(2 * tokens, width), preferred_element_type=F32
        ).astype(BF16)
        rows_ref[p] = picked.reshape(local, places, width)

    def one_expert(e, _):
        slot = lax.rem(e, 2)
        for copy in fetch(e, slot):
            copy.wait()
        rows = rows_ref[:, e].reshape(count, width)
        wide = wide_ref[slot].reshape(2 * units, width)
        both = lax.dot_general(
            rows, wide, (((1,), (1,)), ((), ())), preferred_element_type=F32
        )
        value = jnp.dot(paired(both), tall_ref[slot], preferred_element_type=F32)
        for p in range(pairs):
            scaled = value[p * places : (p + 1) * places] * weight_ref[p, e][:, :1]
            rows_ref[p, e] = scaled.astype(BF16)

        @pl.when(e + 2 < local)
        def _():
            for copy in fetch(e + 2, slot):
                copy.start()

        return 0

    lax.fori_loop(0, local, one_expert, 0)
    for p in range(pairs):
        combine(
            me,
            offsets,
            hot_ref[p].reshape(local * places, 2 * tokens),
            lambda column, half: rows_ref[p, :, :, pl.ds(column, half)].reshape(
                local * places, half
            ),
            *results[p // 2 * 2 : p // 2 * 2 + 2],
            p % 2,
        )


def experts_gather(offsets, where, info, pieces, gate_up, down):
    half = pieces[0].shape[-1]
    tokens = pieces[4].shape[-2]
    local, units, _, width = gate_up.shape
    pairs, places = 4, 2 * CAP
    result = jax.ShapeDtypeStruct((2, 2, 2, 2, tokens, half), BF16)
    smem = pl.BlockSpec(memory_space=pltpu.SMEM)
    vmem = pl.BlockSpec(memory_space=pltpu.VMEM)
    hbm = pl.BlockSpec(memory_space=pl.ANY)
    return pl.pallas_call(
        functools.partial(gather_kernel, offsets),
        out_shape=[result] * 4,
        in_specs=[smem, vmem, hbm, hbm] + [hbm] * len(pieces),
        out_specs=[vmem] * 4,
        scratch_shapes=[
            pltpu.VMEM((pairs, 2, tokens, width), BF16),
            pltpu.VMEM((pairs, local, places, width), BF16),
            pltpu.VMEM((pairs, local, places, 2 * tokens), BF16),
            pltpu.VMEM((pairs, local, places, 128), F32),
            pltpu.VMEM((2, units, 2, width), BF16),
            pltpu.VMEM((2, units, width), BF16),
            pltpu.SemaphoreType.DMA((8 * pairs,)),
            pltpu.SemaphoreType.DMA((2,)),
            pltpu.SemaphoreType.DMA((2,)),
        ],
        compiler_params=pltpu.CompilerParams(vmem_limit_bytes=44 * 1024 * 1024),
        name="experts",
    )(where, info, gate_up, down, *pieces)


def group_bits():
    far, near = bits_of(lax.axis_size(SEQ))
    (side,) = bits_of(lax.axis_size(EXP))
    high, core = bits_of(lax.axis_size(TP))
    return far, near, side, high, core


def spread_near(block, known=None):
    _, _, side, high, core = group_bits()
    half = block.shape[-1] // 2
    left, right = block[..., :half], block[..., :-16, half:]
    both = [left, swap(left, EXP, side)]
    info = jnp.stack([b[..., -16:, :256] for b in both])
    left = jnp.stack([b[..., :-16, :] for b in both])
    if known is None:
        other = swap(right, TP, high)
    else:
        other = jnp.concatenate([known[None], swap(right[1:], TP, high)])
    right = jnp.stack([right, other])
    left2 = swap(left, TP, high)
    right2 = swap(right, EXP, side)
    first = [swap(left, TP, core), swap(right, TP, core)]
    second = [swap(left2, TP, core), swap(right2, TP, core)]
    return [left, left2, first[0], second[0], right, right2, first[1], second[1]], info


def fold(kept, sent, axis, bit):
    return kept + swap(sent.astype(BF16), axis, bit).astype(F32)


HIGHEST = lax.Precision.HIGHEST


def running_sum(log_ref, rows, columns):
    i = lax.broadcasted_iota(jnp.int32, (rows, rows), 0)
    j = lax.broadcasted_iota(jnp.int32, (rows, rows), 1)
    decay = log_ref[...]
    if columns:
        ones = (j <= i).astype(F32)
        return lax.dot_general(
            ones, decay, (((1,), (1,)), ((), ())), precision=HIGHEST, preferred_element_type=F32
        )
    ones = (i <= j).astype(F32)
    return jnp.dot(decay, ones, precision=HIGHEST, preferred_element_type=F32)


def group_rows(ref, g, groups):
    count = ref.shape[0]
    row = lax.broadcasted_iota(jnp.int32, (count // groups, count), 0)
    column = lax.broadcasted_iota(jnp.int32, (count // groups, count), 1)
    pick = (column == row * groups + g).astype(F32).astype(BF16)
    return jnp.dot(pick, ref[...], preferred_element_type=F32)


def state_kernel(
    input_ref,
    inflow_ref,
    readout_ref,
    step_ref,
    log_ref,
    key_ref,
    value_ref,
    intra_ref,
    state_ref,
    sent_ref,
    kv_ref,
):
    shared = key_ref.shape[0] // input_ref.shape[0]
    for n, ref in enumerate((key_ref, value_ref)):
        for h in range(shared):
            start = (n * shared + h) * input_ref.shape[0]
            kv_ref[start : start + input_ref.shape[0]] = group_rows(ref, h, shared).astype(BF16)
    rows = input_ref.shape[0]
    heads = step_ref.shape[0]
    groups = inflow_ref.shape[0] // rows
    per_group = heads // groups
    across = running_sum(log_ref, rows, False)
    down = running_sum(log_ref, rows, True)
    step = step_ref[...]
    i = lax.broadcasted_iota(jnp.int32, (rows, rows), 0)
    j = lax.broadcasted_iota(jnp.int32, (rows, rows), 1)
    causal = j <= i
    weight = jnp.transpose(jnp.exp(across[:, rows - 1 :] - across) * step)
    for g in range(groups):
        wide = group_rows(inflow_ref, g, groups)
        both = lax.dot_general(
            group_rows(readout_ref, g, groups).astype(BF16),
            wide.astype(BF16),
            (((1,), (1,)), ((), ())),
            preferred_element_type=F32,
        )
        for pair in range(0, per_group, 2):
            first = g * per_group + pair
            columns = slice(first * HP, (first + 2) * HP)
            inputs = input_ref[:, columns]
            intra, state = [], []
            for h in (first, first + 1):
                gap = jnp.where(causal, down[:, h : h + 1] - across[h : h + 1], 0.0)
                decay = jnp.where(causal, jnp.exp(gap), 0.0)
                mixing = (decay * both * step[h : h + 1]).astype(BF16)
                intra.append(jnp.dot(mixing, inputs, preferred_element_type=F32))
                weighted = (weight[:, h : h + 1] * wide).astype(BF16)
                state.append(
                    lax.dot_general(
                        weighted, inputs, (((0,), (0,)), ((), ())), preferred_element_type=F32
                    )
                )
            left = lax.broadcasted_iota(jnp.int32, (rows, 2 * HP), 1) < HP
            intra_ref[:, columns] = jnp.where(left, intra[0], intra[1])
            left = lax.broadcasted_iota(jnp.int32, (NS, 2 * HP), 1) < HP
            block = jnp.where(left, state[0], state[1])
            state_ref[:, columns] = block
            sent_ref[:, columns] = block.astype(BF16)


def state_local(inputs, inflow, readout, step, log_decay, keys, values):
    rows, channels = inputs.shape
    assert rows == STRETCH
    return staged_call(
        state_kernel,
        (),
        (),
        (inputs, inflow, readout, step, log_decay, keys, values),
        [
            jax.ShapeDtypeStruct((rows, channels), F32),
            jax.ShapeDtypeStruct((NS, channels), F32),
            jax.ShapeDtypeStruct((NS, channels), BF16),
            jax.ShapeDtypeStruct((2 * keys.shape[0], keys.shape[1]), BF16),
        ],
    )


def lanes_of(factors, heads):
    left = lax.broadcasted_iota(jnp.int32, (1, 2 * HP), 1) < HP
    return jnp.concatenate(
        [
            jnp.where(left, factors[:, h : h + 1], factors[:, h + 1 : h + 2])
            for h in range(0, heads, 2)
        ],
        axis=1,
    )


def decay_between(place, total_ref, order, span, heads):
    row = lambda m: info_of(total_ref[order[m]])[6:7]
    upper = (place & span) != 0
    lead = own = jnp.zeros_like(row(0))
    theirs = jnp.zeros_like(own)
    for m in range(span):
        lead = lead + jnp.where((place ^ m) < place, row(m), 0.0)
        own = own + row(m)
        theirs = theirs + row(span + m)
    lead, own, theirs = jnp.exp(lead), jnp.exp(own), jnp.exp(theirs)
    return (
        lanes_of(jnp.where(upper, lead, 0.0), heads),
        lanes_of(jnp.where(upper, own, 1.0), heads),
        lanes_of(jnp.where(upper, 1.0, theirs), heads),
    )


def scan_kernel(order, span, heads, where_ref, total_ref, other_ref, state_ref, *refs):
    entering_ref = refs[0] if len(refs) == 4 else None
    new_entering_ref, new_state_ref, sent_ref = refs[-3:]
    lead, own, theirs = decay_between(where_ref[2], total_ref, order, span, heads)
    other = other_ref[...].astype(F32)
    entering = lead * other
    if entering_ref is not None:
        entering = entering + entering_ref[...]
    new_entering_ref[...] = entering
    state = own * other + theirs * state_ref[...]
    new_state_ref[...] = state
    sent_ref[...] = state.astype(BF16)


def scan_step(order, span, heads, where, totals, other, state, *entering):
    vmem = pl.BlockSpec(memory_space=pltpu.VMEM)
    smem = pl.BlockSpec(memory_space=pltpu.SMEM)
    like = jax.ShapeDtypeStruct(state.shape, F32)
    return pl.pallas_call(
        functools.partial(scan_kernel, order, span, heads),
        out_shape=[like, like, jax.ShapeDtypeStruct(state.shape, BF16)],
        in_specs=[smem] + [vmem] * (3 + len(entering)),
        out_specs=[vmem] * 3,
        compiler_params=pltpu.CompilerParams(vmem_limit_bytes=20 * 1024 * 1024),
    )(where, totals, other, state, *entering)


def span_route(span):
    nx, nz = lax.axis_size(EXP), lax.axis_size(SEQ)
    axis, bit = (EXP, span) if span < nx else (SEQ, span // nx)
    both = span * 2 < nx * nz
    pairs = [(i, i ^ bit) for i in range(lax.axis_size(axis)) if both or not i & bit]
    return axis, pairs


def finish_kernel(
    order, span, where_ref, total_ref, other_ref, entering_ref, intra_ref, readout_ref, log_ref, input_ref, gate_ref, skip_ref, gain_ref, out_ref
):
    rows, channels = input_ref.shape
    heads = log_ref.shape[0]
    groups = readout_ref.shape[0] // rows
    width = channels // groups
    grown = jnp.exp(running_sum(log_ref, rows, True))
    lead, _, _ = decay_between(where_ref[2], total_ref, order, span, heads)
    skip = lanes_of(skip_ref[...], heads)
    left = lax.broadcasted_iota(jnp.int32, (rows, 2 * HP), 1) < HP
    for g in range(groups):
        columns = slice(g * width, (g + 1) * width)
        reader = group_rows(readout_ref, g, groups).astype(BF16)
        rest = lead[:, columns] * other_ref[:, columns].astype(F32) + entering_ref[:, columns]
        inter = 0.0
        for _ in range(3):
            part = rest.astype(BF16)
            rest = rest - part.astype(F32)
            inter = inter + jnp.dot(reader, part, preferred_element_type=F32)
        first = g * (heads // groups)
        factor = jnp.concatenate(
            [
                jnp.where(left, grown[:, h : h + 1], grown[:, h + 1 : h + 2])
                for h in range(first, first + heads // groups, 2)
            ],
            axis=1,
        )
        mixed = (
            intra_ref[:, columns]
            + factor * inter
            + skip[:, columns] * input_ref[:, columns].astype(F32)
        )
        gate = gate_ref[:, columns].astype(F32)
        gated = mixed * (gate / (1.0 + jnp.exp(-gate)))
        mean_square = jnp.mean(gated * gated, axis=1, keepdims=True)
        normed = gated * lax.rsqrt(mean_square + EPSILON)
        out_ref[:, columns] = (normed * gain_ref[:, columns]).astype(BF16)


def state_finish(order, span, where, totals, other, entering, intra, *arrays):
    return staged_call(
        functools.partial(finish_kernel, order, span),
        (where,),
        (totals, other, entering, intra),
        arrays,
        [jax.ShapeDtypeStruct(arrays[2].shape, BF16)],
    )[0]


def routed_in_general(own, gate_up, down_proj):
    nz, nx, nt = lax.axis_size(SEQ), lax.axis_size(EXP), lax.axis_size(TP)
    x, t = lax.axis_index(EXP), lax.axis_index(TP)
    info, own = own[-16:, :256], own[:-16]
    rows, chunk = own.shape
    half = chunk // 2
    tp_bits = bits_of(nt)
    seq_stages = stages_of(SEQ, bits_of(nz))
    exp_stages = stages_of(EXP, bits_of(nx))
    far_stages, core_stages = stages_of(TP, tp_bits[:-1]), stages_of(TP, tp_bits[-1:])

    piece = spread(own, seq_stages)
    info_all = spread(info, seq_stages + exp_stages)
    left = spread(piece[..., :half], exp_stages + far_stages + core_stages)
    right = spread(piece[..., half:], far_stages + exp_stages + core_stages)
    left = left.reshape(2, nt // 2, nx, nz, rows, half)
    right = right.reshape(2, nx, nt // 2, nz, rows, half)
    info_all = info_all.reshape(nx, nz, 16, 256)

    where = jnp.stack([t, x * gate_up.shape[0]]).astype(jnp.int32)
    keep0, keep1, send0, send1 = experts_apply(
        offsets_of(tp_bits), where, info_all, left, right, jnp.swapaxes(gate_up, 1, 2), down_proj
    )

    def settle(kept, stages):
        for axis, bit in stages:
            count = kept.shape[0] // 2
            kept = kept[:count] + swap(kept[count:].astype(BF16), axis, bit).astype(F32)
        return kept

    def join(kept, sent):
        kept = kept.astype(F32) + swap(sent, *core_stages[0]).astype(F32)
        return kept.reshape(-1, rows, half)

    kept0 = settle(join(keep0, send0), far_stages[::-1] + exp_stages[::-1])
    kept1 = settle(join(keep1, send1), exp_stages[::-1] + far_stages[::-1])
    kept = settle(jnp.concatenate([kept0, kept1], axis=-1), seq_stages[::-1])
    routed_out = kept.reshape(rows, chunk).astype(BF16)
    order = [
        offsets_of(bits_of(nx)).index(i) * nz + offsets_of(bits_of(nz)).index(k)
        for k in range(nz)
        for i in range(nx)
    ]
    return routed_out, info_all.reshape(-1, 16, 256), order


def local(
    query_heads,
    key_heads,
    value_head_rows,
    state_input,
    state_gate,
    state_inflow,
    state_readout,
    step_size,
    log_decay,
    skip_scale,
    state_gain,
    hidden_in,
    mlp_gain,
    router_weight,
    expert_ids,
    slot_index,
    gate_up,
    down_proj,
):
    nz, nx, nt = lax.axis_size(SEQ), lax.axis_size(EXP), lax.axis_size(TP)
    z, x, t = lax.axis_index(SEQ), lax.axis_index(EXP), lax.axis_index(TP)
    _, width = hidden_in.shape
    chunk = width // nt
    seq_stages = stages_of(SEQ, bits_of(nz))
    exp_stages = stages_of(EXP, bits_of(nx))

    where = jnp.stack([t, x * gate_up.shape[0], z * nx + x]).astype(jnp.int32)
    own, known = norm_share(
        where,
        bits_of(nt)[0],
        chunk,
        hidden_in,
        mlp_gain[None],
        router_weight.T,
        expert_ids.T,
        slot_index.T,
        log_decay.T,
    )
    flat = lambda a: a.reshape(-1, a.shape[2])
    heads = step_size.shape[1]
    inflow, readout = flat(state_inflow), flat(state_readout)
    intra, state, sent, kv = state_local(
        state_input,
        inflow,
        readout,
        step_size.T,
        log_decay.T,
        flat(key_heads),
        flat(value_head_rows),
    )
    finish_args = (
        intra,
        readout,
        log_decay.T,
        state_input,
        state_gate,
        skip_scale[None],
        state_gain[None],
    )

    if (nz, nx, nt) != (4, 2, 4):
        routed_out, info_all, order = routed_in_general(own, gate_up, down_proj)
        stages = seq_stages + exp_stages
        kv_own = spread(kv, stages[:-1])
        kv_parts = [a.reshape(-1, *kv.shape) for a in (kv_own, swap(kv_own, *stages[-1]))]
        far = [o * nx for o in offsets_of(bits_of(nz))]
        window_out = attention(
            query_heads, kv_parts, [i ^ o for i in offsets_of(bits_of(nx)) for o in far], where
        )
        entering, span = (), 1
        while span * 2 < nx * nz:
            other = lax.ppermute(sent, *span_route(span))
            *entering, state, sent = scan_step(
                order, span, heads, where, info_all, other, state, *entering
            )
            span *= 2
        other = lax.ppermute(sent, *span_route(span))
        state_out = state_finish(order, span, where, info_all, other, *entering, *finish_args)
        return window_out, state_out, routed_out

    return in_groups(
        where, own, known, kv, sent, state, query_heads, finish_args, gate_up, down_proj
    )


def in_groups(where, own, known, kv, sent, state, query_heads, finish_args, gate_up, down_proj):
    nz, nx = lax.axis_size(SEQ), lax.axis_size(EXP)
    heads = finish_args[2].shape[0]
    far, near, side, high, core = group_bits()
    order = [(k >> 1 << 2) | (i << 1) | (k & 1) for k in range(nz) for i in range(nx)]
    beyond = swap(own, SEQ, far)
    beside = swap(own, SEQ, near)
    here = jnp.stack([own, beside])
    kv_own = jnp.stack([kv, swap(kv, SEQ, far)])
    kv_own = jnp.stack([kv_own, swap(kv_own, SEQ, near)])
    there = jnp.stack([beyond, swap(beyond, SEQ, near)])
    pieces_a, info_a = spread_near(here, known)
    pieces_b, info_b = spread_near(there)
    info_all = jnp.stack([info_a, info_b]).reshape(-1, 16, 256)
    other = lax.ppermute(sent, *span_route(1))
    *entering, state, sent = scan_step(order, 1, heads, where, info_all, other, state)
    other2 = lax.ppermute(sent, *span_route(2))
    kv_other = swap(kv_own, EXP, side)

    offsets = ((0, high), (core, core ^ high))
    keep_a, send_a, keep_b, send_b = experts_gather(
        offsets, where, info_all, pieces_a + pieces_b, gate_up, down_proj
    )

    kept_b = fold(keep_b.astype(F32), send_b, TP, core)
    kept_a = fold(keep_a.astype(F32), send_a, TP, core)
    *entering, state, sent = scan_step(order, 2, heads, where, info_all, other2, state, *entering)
    other4 = lax.ppermute(sent, *span_route(4))
    firsts, routed = [], []
    for name, kept in (("b", kept_b), ("a", kept_a)):
        left = fold(kept[0, 0], kept[0, 1], TP, high)
        right = fold(kept[1, 0], kept[1, 1], EXP, side)
        firsts.append((name, left, right))
    kv_own, kv_other = [a.reshape(-1, *kv.shape) for a in (kv_own, kv_other)]
    offsets = [n * nx ^ f * nx for n in (0, near) for f in (0, far)]
    carried = attention(query_heads, [kv_own], offsets, where, ends=False)
    window_out = attention(query_heads, [kv_other], [o ^ side for o in offsets], where, carried)
    state_out = state_finish(order, 4, where, info_all, other4, *entering, *finish_args)
    for name, left, right in firsts:
        left = fold(left[0], left[1], EXP, side)
        right = fold(right[0], right[1], TP, high)
        both = jnp.concatenate([left, right], axis=-1)
        routed.append(fold(both[0], both[1], SEQ, near))
    routed_out = fold(routed[1], routed[0], SEQ, far).astype(BF16)
    return window_out, state_out, routed_out


def solution(mesh):
    block = (SEQ, EXP)
    program = jax.shard_map(
        local,
        mesh=mesh,
        in_specs=(
            P(block, TP, None),
            P(block, TP, None),
            P(block, TP, None),
            P(block, TP),
            P(block, TP),
            P(block, TP, None),
            P(block, TP, None),
            P(block, TP),
            P(block, TP),
            P(TP),
            P(TP),
            P(block, None),
            P(),
            P(),
            P(block, None),
            P(block, None),
            P(EXP, (SEQ, TP), None, None),
            P(EXP, (SEQ, TP), None),
        ),
        out_specs=(P(block, TP, None), P(block, TP), P(block, TP)),
        check_vma=False,
    )
    if tuple(mesh.shape[a] for a in (SEQ, EXP, TP)) != (4, 2, 4):
        return program
    return program
```
